32 devices in a mesh: shard: 4 (over z), ctx: 2 (over core), tp: 4 (over y, x).
Axes of the slice: x: 2, y: 2, z: 4, core: 2. Of those that a mesh axis runs over, the one named last changes fastest.
Arguments:
- tokens: bfloat16 [16384, 896], P(('shard', 'ctx', 'tp')), may hold values from -6 to 6
- doc_ids: int32 [16, 1024], P(('shard', 'tp')), may hold values from -1 to 7, as said below
- w_query: bfloat16 [896, 896], P(('shard', 'ctx')), may hold values from -0.1875 to 0.1875
- b_query: bfloat16 [896], P(('shard', 'ctx')), may hold values from -3 to 3
- key_projection: bfloat16 [896, 128], P(('shard', 'ctx')), may hold values from -0.1875 to 0.1875
- key_bias_vector: bfloat16 [128], P(('shard', 'ctx')), may hold values from -3 to 3
- value_projection: bfloat16 [896, 128], P(('shard', 'ctx')), may hold values from -0.1875 to 0.1875
- value_bias_vector: bfloat16 [128], P(('shard', 'ctx')), may hold values from -3 to 3
- w_output: bfloat16 [896, 896], P(('shard', 'ctx')), may hold values from -1.5 to 1.5
- gain_attn: bfloat16 [896], P(('shard', 'ctx')), may hold values from 0.5 to 1.5
- gain_mlp: bfloat16 [896], P(('shard', 'ctx')), may hold values from 0.5 to 1.5
- w_gate: bfloat16 [896, 4864], P(('shard', 'ctx'), 'tp'), may hold values from -0.1875 to 0.1875
- w_up: bfloat16 [896, 4864], P(('shard', 'ctx'), 'tp'), may hold values from -0.1875 to 0.1875
- w_down: bfloat16 [4864, 896], P('tp', ('shard', 'ctx')), may hold values from -0.078125 to 0.078125
- cotangent: bfloat16 [16384, 896], P(('shard', 'ctx', 'tp')), may hold values from -6 to 6
Outputs:
- output: bfloat16 [16384, 896], P(('shard', 'ctx', 'tp'))
- grad_tokens: bfloat16 [16384, 896], P(('shard', 'ctx', 'tp'))
- grad_w_query: float32 [896, 896], P(('shard', 'ctx'))
- grad_b_query: float32 [896], P(('shard', 'ctx'))
- grad_w_key: float32 [896, 128], P(('shard', 'ctx'))
- grad_b_key: float32 [128], P(('shard', 'ctx'))
- grad_w_value: float32 [896, 128], P(('shard', 'ctx'))
- grad_b_value: float32 [128], P(('shard', 'ctx'))
- grad_w_output: float32 [896, 896], P(('shard', 'ctx'))
- grad_gain_attn: float32 [896], P(('shard', 'ctx'))
- grad_gain_mlp: float32 [896], P(('shard', 'ctx'))
- grad_w_gate: float32 [896, 4864], P(('shard', 'ctx'), 'tp')
- grad_w_up: float32 [896, 4864], P(('shard', 'ctx'), 'tp')
- grad_w_down: float32 [4864, 896], P('tp', ('shard', 'ctx'))
The draws below stay inside these ranges and needn't reach their ends.
Inputs may be any that keep to these rules, and one draw needn't show every extreme that they name: `doc_ids`: documents begin at multiples of 128 within a buffer, are numbered 0, 1, 2 in order in each buffer, and only the rest of a document's last block of 128 slots is padding (-1).
All inputs are finite; a program needn't handle non-finite values.
Results may differ from the reference program's by a relative error of at most 0.02.
Values may be sent and summed in bfloat16 or wider, within the bound.
No kernel may reach another device: no remote copies, remote signals or barrier semaphores. Data moves between devices by JAX's collectives and lax.ppermute only.
A program may use at most 192 MiB of HBM per device.

```python
import jax
import jax.numpy as jnp
from jax import lax

MODEL_WIDTH = 896
FF = 4864
QUERY_HEADS = 14
KEY_VALUE_HEADS = 2
HEAD_WIDTH = 64
TOK_DEV = 512
ABLK = 128
PAIR_LEN = 1024
PAIRS = 16
TOKENS = 16384
N_SHARD = 4
N_CTX = 2
N_TP = 4


def draw_doc_ids(key, part):
    block_total = PAIR_LEN // ABLK
    first_key, second_key = jax.random.split(key)
    pair_index = jnp.arange(PAIRS, dtype=jnp.int32)[:, None]
    block_index = jnp.arange(block_total, dtype=jnp.int32)[None, :]
    new_doc = jax.random.randint(first_key, (PAIRS, block_total), 0, 2, dtype=jnp.int32)
    new_doc = jnp.where(block_index == 0, 1, new_doc)
    new_doc = jnp.where(pair_index == 0, 1, new_doc)
    new_doc = jnp.where(pair_index == 1, jnp.where(block_index == 0, 1, 0), new_doc)
    block_doc = jnp.cumsum(new_doc, axis=1) - 1
    last_block = jnp.concatenate([new_doc[:, 1:], jnp.ones((PAIRS, 1), jnp.int32)], axis=1) == 1
    live_count = jax.random.randint(second_key, (PAIRS, block_total), 1, ABLK + 1, dtype=jnp.int32)
    live_count = jnp.where(pair_index == 1, ABLK, live_count)
    live_count = jnp.where((pair_index == 0) & (block_index == 0), ABLK // 2, live_count)
    live_count = jnp.where(last_block, live_count, ABLK)
    within = jnp.arange(ABLK, dtype=jnp.int32)[None, None, :]
    doc_grid = jnp.where(within < live_count[:, :, None], block_doc[:, :, None], -1)
    return doc_grid.reshape(PAIRS, PAIR_LEN).astype(jnp.int32)


def with_spikes(values, key, source, target, shards_of, factor):
    def block_of(position):
        return (jnp.arange(values.shape[position]) // (values.shape[position] // shards_of)).reshape((-1,) + (1,) * (values.ndim - 1 - position))

    one_side = jax.random.permutation(key, shards_of)[block_of(target)]
    far = (block_of(target) + shards_of // 2) % shards_of
    return jnp.where((block_of(source) == one_side) | (block_of(source) == far), factor * values, values)


def shard_levels(key, dims, cuts, low, largest):
    def one(position, parts):
        steps = jax.random.uniform(jax.random.fold_in(jax.random.fold_in(key, 6), position), (parts,), jnp.float32, low / len(cuts), largest / len(cuts))
        return jnp.repeat(jnp.exp(steps), dims[position] // parts).reshape((-1,) + (1,) * (len(dims) - position - 1))

    gain = one(*cuts[0])
    for cut in cuts[1:]:
        gain = gain * one(*cut)
    return gain


def noise(rng, shape, spread, most, shards=(), held_as=jnp.bfloat16):
    result = spread * jax.random.normal(rng, shape, jnp.float32)
    if shards:
        result = result * shard_levels(rng, shape, shards, -0.22, 0.18)
    return jnp.clip(result, -most, most).astype(held_as)


def noise_with(rng, shape, scale, most, shards, heavy, kind=jnp.bfloat16):
    entries = scale * jax.random.normal(rng, shape, jnp.float32)
    if shards:
        entries = entries * shard_levels(rng, shape, shards, -0.22, 0.18)
    return jnp.clip(with_spikes(entries, jax.random.fold_in(rng, 3), *heavy), -most, most).astype(kind)


def setup_inputs(seed: int = 0) -> dict:
    streams_of = jax.random.split(jax.random.key(seed), 16)
    return {
        "tokens": noise(streams_of[0], (TOKENS, MODEL_WIDTH), 1.0, 6.0, ((0, 32),)),
        "doc_ids": draw_doc_ids(jax.random.fold_in(streams_of[15], 71), 0),
        "w_query": noise(streams_of[2], (MODEL_WIDTH, QUERY_HEADS * HEAD_WIDTH), MODEL_WIDTH ** -0.5, 0.1875, ((0, 8),)),
        "b_query": noise(streams_of[3], (QUERY_HEADS * HEAD_WIDTH,), 0.5, 3.0, ((0, 8),)),
        "key_projection": noise(streams_of[4], (MODEL_WIDTH, KEY_VALUE_HEADS * HEAD_WIDTH), MODEL_WIDTH ** -0.5, 0.1875, ((0, 8),)),
        "key_bias_vector": noise(streams_of[5], (KEY_VALUE_HEADS * HEAD_WIDTH,), 0.5, 3.0, ((0, 8),)),
        "value_projection": noise(streams_of[6], (MODEL_WIDTH, KEY_VALUE_HEADS * HEAD_WIDTH), MODEL_WIDTH ** -0.5, 0.1875, ((0, 8),)),
        "value_bias_vector": noise(streams_of[7], (KEY_VALUE_HEADS * HEAD_WIDTH,), 0.5, 3.0, ((0, 8),)),
        "w_output": noise(streams_of[8], (QUERY_HEADS * HEAD_WIDTH, MODEL_WIDTH), (QUERY_HEADS * HEAD_WIDTH // 64) ** -0.5, 1.5, ((0, 8),)),
        "gain_attn": jnp.clip(1.0 + 0.1 * jax.random.normal(streams_of[9], (MODEL_WIDTH,), jnp.float32), 0.5, 1.5).astype(jnp.bfloat16),
        "gain_mlp": jnp.clip(1.0 + 0.1 * jax.random.normal(streams_of[10], (MODEL_WIDTH,), jnp.float32), 0.5, 1.5).astype(jnp.bfloat16),
        "w_gate": noise(streams_of[11], (MODEL_WIDTH, FF), MODEL_WIDTH ** -0.5, 0.1875, ((0, 8), (1, 4))),
        "w_up": noise(streams_of[12], (MODEL_WIDTH, FF), MODEL_WIDTH ** -0.5, 0.1875, ((0, 8), (1, 4))),
        "w_down": noise(streams_of[13], (FF, MODEL_WIDTH), FF ** -0.5, 0.078125, ((0, 4), (1, 8))),
        "cotangent": noise_with(streams_of[14], (TOKENS, MODEL_WIDTH), 1.0, 6.0, ((0, 32),), (0, 1, 32, 2.75)),
    }


EPSILON = 1e-06
THETA = 1000000.0
NEGATIVE = -1e+30
HIGH = lax.Precision.HIGHEST

@jax.custom_vjp
def low(v):
    return lax.optimization_barrier(v.astype(jnp.bfloat16)).astype(jnp.float32)

@jax.custom_vjp
def lower_gradient(v):
    return v

def low_keep(v):
    return (low(v), None)

def low_pass(kept, grad):
    return (grad,)

def back_keep(v):
    return (v, None)

def back_low(kept, grad):
    return (low(grad),)
low.defvjp(low_keep, low_pass)
lower_gradient.defvjp(back_keep, back_low)

def product_result(left_side, right_side):
    return jnp.dot(left_side, right_side, precision=HIGH, preferred_element_type=jnp.float32)

def rotation(positions, head_size):
    half_dim = head_size // 2
    frequency = THETA ** (-(jnp.arange(half_dim, dtype=jnp.float32) * 2.0) / head_size)
    angles = positions.astype(jnp.float32)[:, None] * frequency[None, :]
    return (jnp.cos(angles), jnp.sin(angles))

def apply_rotary(values, cosine_table, sine_table):
    half_dim = values.shape[-1] // 2
    first_half = values[..., :half_dim]
    second_half = values[..., half_dim:]
    cosine_table = cosine_table[:, None, :]
    sine_table = sine_table[:, None, :]
    return jnp.concatenate([first_half * cosine_table - second_half * sine_table, second_half * cosine_table + first_half * sine_table], -1)

def block_layer(tok_rows, doc_row, weights):
    w_query, b_query, key_projection, key_bias_vector, value_projection, value_bias_vector, w_output, gain_attn, gain_mlp, w_gate, w_up, w_down = weights
    length_total = tok_rows.shape[0]
    queries_per_group = QUERY_HEADS // KEY_VALUE_HEADS
    inv_one = lax.rsqrt(lax.optimization_barrier(jnp.mean(tok_rows * tok_rows, -1, keepdims=True)) + EPSILON)
    normalized_rows = low(tok_rows * inv_one * gain_attn)
    cosine_table, sine_table = rotation(jnp.arange(length_total, dtype=jnp.int32), HEAD_WIDTH)
    query_rows_gathered = apply_rotary((lower_gradient(product_result(normalized_rows, w_query)) + b_query).reshape(length_total, QUERY_HEADS, HEAD_WIDTH), cosine_table, sine_table)
    key_rows_gathered = apply_rotary((lower_gradient(product_result(normalized_rows, key_projection)) + key_bias_vector).reshape(length_total, KEY_VALUE_HEADS, HEAD_WIDTH), cosine_table, sine_table)
    value_rows_gathered = (lower_gradient(product_result(normalized_rows, value_projection)) + value_bias_vector).reshape(length_total, KEY_VALUE_HEADS, HEAD_WIDTH)
    query_rows_gathered = lower_gradient(low(query_rows_gathered))
    key_rows_gathered = lower_gradient(low(key_rows_gathered))
    value_rows_gathered = lower_gradient(low(value_rows_gathered))
    query_grouped = query_rows_gathered.reshape(length_total, KEY_VALUE_HEADS, queries_per_group, HEAD_WIDTH)
    scores = jnp.einsum('qkgd,skd->kgqs', query_grouped, key_rows_gathered, precision=HIGH) * HEAD_WIDTH ** (-0.5)
    scores = lower_gradient(scores)
    places = jnp.arange(length_total, dtype=jnp.int32)
    same_doc = (doc_row[:, None] == doc_row[None, :]) & (doc_row[:, None] >= 0) & (places[None, :] <= places[:, None])
    key_mask = same_doc | (places[:, None] == places[None, :])
    scores = jnp.where(key_mask[None, None], scores, NEGATIVE)
    row_max = lax.optimization_barrier(jnp.max(scores, -1, keepdims=True))
    exponent = jnp.exp(scores - row_max)
    attn_probs = exponent / lax.optimization_barrier(jnp.sum(exponent, -1, keepdims=True))
    mixed_heads = jnp.einsum('kgqs,skd->qkgd', low(attn_probs), value_rows_gathered, precision=HIGH).reshape(length_total, QUERY_HEADS * HEAD_WIDTH)
    mixed_heads = lower_gradient(low(mixed_heads))
    hidden = tok_rows + lower_gradient(product_result(mixed_heads, w_output))
    inv_two = lax.rsqrt(lax.optimization_barrier(jnp.mean(hidden * hidden, -1, keepdims=True)) + EPSILON)
    normed_mlp = low(hidden * inv_two * gain_mlp)
    gate_pre = lower_gradient(product_result(normed_mlp, w_gate))
    up_pre = lower_gradient(product_result(normed_mlp, w_up))
    activation = low(jax.nn.silu(gate_pre) * up_pre)
    return hidden + lower_gradient(product_result(activation, w_down))

def reference(tokens, doc_ids, w_query, b_query, key_projection, key_bias_vector, value_projection, value_bias_vector, w_output, gain_attn, gain_mlp, w_gate, w_up, w_down, cotangent):

    def to_pairs(flat_array):
        last_width = flat_array.shape[-1]
        return flat_array.reshape(N_SHARD, N_CTX, N_TP, TOK_DEV, last_width).transpose(0, 2, 1, 3, 4).reshape(PAIRS, PAIR_LEN, last_width)

    def from_pairs(flat_array):
        last_width = flat_array.shape[-1]
        return flat_array.reshape(N_SHARD, N_TP, N_CTX, TOK_DEV, last_width).transpose(0, 2, 1, 3, 4).reshape(TOKENS, last_width)
    weights = tuple((matrix.astype(jnp.float32) for matrix in (w_query, b_query, key_projection, key_bias_vector, value_projection, value_bias_vector, w_output, gain_attn, gain_mlp, w_gate, w_up, w_down)))
    paired = to_pairs(tokens.astype(jnp.float32))

    def whole(paired_rows, layer_weights):
        pair_step = jax.checkpoint(lambda pair_item: block_layer(pair_item[0], pair_item[1], layer_weights))
        return lax.map(pair_step, (paired_rows, doc_ids))
    outputs, pullback = jax.vjp(whole, paired, weights)
    grad_paired, grad_weights = pullback(to_pairs(cotangent.astype(jnp.float32)))
    return (from_pairs(outputs).astype(jnp.bfloat16), from_pairs(grad_paired).astype(jnp.bfloat16), grad_weights[0], grad_weights[1], grad_weights[2], grad_weights[3], grad_weights[4], grad_weights[5], grad_weights[6], grad_weights[7], grad_weights[8], grad_weights[9], grad_weights[10], grad_weights[11])
```

```python
import functools

import jax
import jax.numpy as jnp
from jax import lax
from jax.experimental import pallas as pl
from jax.experimental.pallas import tpu as pltpu
from jax.sharding import PartitionSpec as P

QUERY_HEADS = 14
KEY_VALUE_HEADS = 2
HEAD_WIDTH = 64
GROUP = QUERY_HEADS // KEY_VALUE_HEADS

EPSILON = 1e-06
THETA = 1000000.0
NEGATIVE = -1e30
BF = jnp.bfloat16
F32 = jnp.float32


def dot(left, right, left_dim, right_dim, out=F32):
    return lax.dot_general(
        left, right, (((left_dim,), (right_dim,)), ((), ())), preferred_element_type=out
    )


def fill_bias(bias, doc_row, doc_col, row_start, row_count, span):
    keys = lax.broadcasted_iota(jnp.int32, (span, row_count), 0)
    queries = lax.broadcasted_iota(jnp.int32, (span, row_count), 1) + row_start
    key_doc = doc_col[0:span, :]
    query_doc = doc_row[:, row_start : row_start + row_count]
    same = (key_doc == query_doc) & (query_doc >= 0) & (keys <= queries)
    bias[0:span, :] = jnp.where(same | (keys == queries), 0.0, NEGATIVE)


def load_keys(half, own, other, keys_t, keys, values_t, values):
    width = KEY_VALUE_HEADS * HEAD_WIDTH
    parts = (own,) if half == 0 else (other, own)
    for place, part in enumerate(parts):
        count = part.shape[1]
        rows = slice(place * count, (place + 1) * count)
        key_t = part[0:width, :]
        value_t = part[width : 2 * width, :]
        keys_t[:, rows] = key_t
        values_t[:, rows] = value_t
        key = key_t.astype(F32).T.astype(BF)
        for head in range(KEY_VALUE_HEADS):
            lanes = slice(head * HEAD_WIDTH, (head + 1) * HEAD_WIDTH)
            keys[head, rows, :] = key[:, lanes]
        if values is not None:
            value = value_t.astype(F32).T.astype(BF)
            for head in range(KEY_VALUE_HEADS):
                lanes = slice(head * HEAD_WIDTH, (head + 1) * HEAD_WIDTH)
                values[head, rows, :] = value[:, lanes]


def attention_forward_body(
    half_ref, doc_row, doc_col, query_t, own, other, mixed_t, lse, keys_t, keys, values_t, bias
):
    token_count = query_t.shape[1]
    step = token_count // 2
    for half in (0, 1):

        @pl.when(half_ref[0] == half)
        def _():
            load_keys(half, own, other, keys_t, keys, values_t, None)
            for block in (0, 1):
                span = half * token_count + (block + 1) * step
                start = half * token_count + block * step
                cols = slice(block * step, (block + 1) * step)
                fill_bias(bias, doc_row, doc_col, start, step, span)
                for group in range(KEY_VALUE_HEADS):
                    head_rows = slice(group * HEAD_WIDTH, (group + 1) * HEAD_WIDTH)

                    def one(index, carry):
                        head = group * GROUP + index
                        place = pl.ds(pl.multiple_of(head * HEAD_WIDTH, HEAD_WIDTH), HEAD_WIDTH)
                        score = (
                            jnp.dot(
                                keys[group, 0:span, :],
                                query_t[place, cols],
                                preferred_element_type=F32,
                            )
                            + bias[0:span, :]
                        )
                        top = jnp.max(score, axis=0, keepdims=True)
                        weight = jnp.exp(score - top)
                        total = jnp.sum(weight, axis=0, keepdims=True)
                        out = jnp.dot(
                            values_t[head_rows, 0:span],
                            weight.astype(BF),
                            preferred_element_type=F32,
                        )
                        mixed_t[place, cols] = (out / total).astype(BF)
                        lse[head, :, cols] = jnp.broadcast_to(top + jnp.log(total), (8, step))
                        return carry

                    lax.fori_loop(0, GROUP, one, 0)


def attention_forward(half, doc_row, doc_col, query_t, own, other):
    width, token_count = query_t.shape
    kv = KEY_VALUE_HEADS * HEAD_WIDTH
    vmem = pl.BlockSpec(memory_space=pltpu.VMEM)
    return pl.pallas_call(
        attention_forward_body,
        out_shape=(
            jax.ShapeDtypeStruct((width, token_count), BF),
            jax.ShapeDtypeStruct((QUERY_HEADS, 8, token_count), F32),
        ),
        in_specs=[pl.BlockSpec(memory_space=pltpu.SMEM)] + [vmem] * 5,
        out_specs=(vmem, vmem),
        scratch_shapes=[
            pltpu.VMEM((kv, 2 * token_count), BF),
            pltpu.VMEM((KEY_VALUE_HEADS, 2 * token_count, HEAD_WIDTH), BF),
            pltpu.VMEM((kv, 2 * token_count), BF),
            pltpu.VMEM((2 * token_count, token_count // 2), F32),
        ],
        cost_estimate=pl.CostEstimate(
            flops=int(15e9), bytes_accessed=4 * width * token_count, transcendentals=0
        ),
        name="attention_forward",
    )(half, doc_row, doc_col, query_t, own, other)


def attention_backward_body(
    half_ref,
    doc_row,
    doc_col,
    query_t,
    own,
    other,
    mixed_t,
    grad_t,
    lse,
    grad_query_t,
    grad_key,
    grad_value,
    keys_t,
    keys,
    values_t,
    values,
    bias,
):
    token_count = query_t.shape[1]
    step = token_count // 2
    grad_key[...] = jnp.zeros_like(grad_key)
    grad_value[...] = jnp.zeros_like(grad_value)
    for half in (0, 1):

        @pl.when(half_ref[0] == half)
        def _():
            load_keys(half, own, other, keys_t, keys, values_t, values)
            for block in (0, 1):
                span = half * token_count + (block + 1) * step
                start = half * token_count + block * step
                cols = slice(block * step, (block + 1) * step)
                fill_bias(bias, doc_row, doc_col, start, step, span)
                for group in range(KEY_VALUE_HEADS):
                    head_rows = slice(group * HEAD_WIDTH, (group + 1) * HEAD_WIDTH)

                    def one(index, carry):
                        head = group * GROUP + index
                        place = pl.ds(pl.multiple_of(head * HEAD_WIDTH, HEAD_WIDTH), HEAD_WIDTH)
                        query = query_t[place, cols]
                        grad = grad_t[place, cols]
                        delta = jnp.sum(
                            grad.astype(F32) * mixed_t[place, cols].astype(F32),
                            axis=0,
                            keepdims=True,
                        )
                        score = (
                            jnp.dot(keys[group, 0:span, :], query, preferred_element_type=F32)
                            + bias[0:span, :]
                        )
                        prob = jnp.exp(score - lse[head, 0:1, cols])
                        grad_prob = jnp.dot(
                            values[group, 0:span, :], grad, preferred_element_type=F32
                        )
                        grad_score = (prob * (grad_prob - delta)).astype(BF)
                        grad_value[group, 0:span, :] += dot(prob.astype(BF), grad, 1, 1)
                        grad_key[group, 0:span, :] += dot(grad_score, query, 1, 1)
                        grad_query_t[place, cols] = jnp.dot(
                            keys_t[head_rows, 0:span], grad_score, preferred_element_type=F32
                        ) * (HEAD_WIDTH ** (-0.5))
                        return carry

                    lax.fori_loop(0, GROUP, one, 0)


def attention_backward(half, doc_row, doc_col, query_t, own, other, mixed_t, grad_t, lse):
    width, token_count = query_t.shape
    kv = KEY_VALUE_HEADS * HEAD_WIDTH
    vmem = pl.BlockSpec(memory_space=pltpu.VMEM)
    sums = jax.ShapeDtypeStruct((KEY_VALUE_HEADS, 2 * token_count, HEAD_WIDTH), F32)
    return pl.pallas_call(
        attention_backward_body,
        out_shape=(jax.ShapeDtypeStruct((width, token_count), F32), sums, sums),
        in_specs=[pl.BlockSpec(memory_space=pltpu.SMEM)] + [vmem] * 8,
        out_specs=(vmem, vmem, vmem),
        scratch_shapes=[
            pltpu.VMEM((kv, 2 * token_count), BF),
            pltpu.VMEM((KEY_VALUE_HEADS, 2 * token_count, HEAD_WIDTH), BF),
            pltpu.VMEM((kv, 2 * token_count), BF),
            pltpu.VMEM((KEY_VALUE_HEADS, 2 * token_count, HEAD_WIDTH), BF),
            pltpu.VMEM((2 * token_count, token_count // 2), F32),
        ],
        cost_estimate=pl.CostEstimate(
            flops=int(35e9), bytes_accessed=8 * width * token_count, transcendentals=0
        ),
        name="attention_backward",
    )(half, doc_row, doc_col, query_t, own, other, mixed_t, grad_t, lse)


def rope_tables(half, token_count):
    half_dim = HEAD_WIDTH // 2
    frequency = THETA ** (-(jnp.arange(half_dim, dtype=F32) * 2.0) / HEAD_WIDTH)
    positions = half * token_count + jnp.arange(token_count, dtype=jnp.int32)
    angles = frequency[:, None] * positions.astype(F32)[None, :]
    return jnp.cos(angles), jnp.sin(angles)


def rotate(values_t, cosine, sine):
    rows, count = values_t.shape
    split = values_t.reshape(rows // HEAD_WIDTH, 2, HEAD_WIDTH // 2, count)
    first, second = split[:, 0], split[:, 1]
    return jnp.stack(
        [first * cosine - second * sine, second * cosine + first * sine], 1
    ).reshape(rows, count)


class Mesh:
    def __init__(self):
        self.shards = lax.axis_size("shard")
        self.ctxs = lax.axis_size("ctx")
        self.tps = lax.axis_size("tp")
        self.fast = (self.shards, self.ctxs, self.tps) == (4, 2, 4)
        self.z = lax.axis_index("shard")
        self.c = lax.axis_index("ctx")
        self.t = lax.axis_index("tp")

    def across(self, value):
        pairs = [(i, self.ctxs - 1 - i) for i in range(self.ctxs)]
        return lax.ppermute(value, "ctx", pairs)

    def side(self, value, which):
        return lax.ppermute(value, "tp", [(i, i ^ which) for i in range(self.tps)])

    def gather_rows(self, block):
        if not self.fast:
            return lax.all_gather(block, ("shard", "ctx"), axis=0)
        last = self.shards - 1
        plus, minus = [], []
        right = left = block
        for step in range(1, self.shards):
            right = lax.ppermute(right, "shard", [(i, i + 1) for i in range(step - 1, last)])
            left = lax.ppermute(left, "shard", [(i + 1, i) for i in range(0, last - step + 1)])
            plus.append(right)
            minus.append(left)
        line = jnp.stack(plus[::-1] + [block] + minus)
        mine = lax.dynamic_slice_in_dim(line, last - self.z, self.shards, 0)
        theirs = self.across(mine)
        low = jnp.where(self.c == 0, mine, theirs)
        high = jnp.where(self.c == 0, theirs, mine)
        full = jnp.stack([low, high], 1)
        return full.reshape((self.shards * self.ctxs,) + block.shape)

    def reduce_rows(self, value):
        blocks, rows, cols = value.shape
        if not self.fast:
            part = lax.psum_scatter(
                value, ("shard", "ctx"), scatter_dimension=0, tiled=True
            )
            return lax.psum(part[0].astype(F32), "tp")
        value = value.reshape(self.shards, self.ctxs, rows, cols)
        send = lax.dynamic_index_in_dim(value, 1 - self.c, 1, False).astype(BF)
        keep = lax.dynamic_index_in_dim(value, self.c, 1, False)
        part = keep.astype(F32) + self.across(send).astype(F32)
        part = part.reshape(self.shards, self.tps, rows // self.tps, cols)

        def quarter(which):
            return lax.dynamic_index_in_dim(part, self.t ^ which, 1, False)

        mine = quarter(0)
        for which in (1, 2, 3):
            mine = mine + self.side(quarter(which).astype(BF), which).astype(F32)
        total = lax.dynamic_index_in_dim(mine, self.z, 0, False)
        for shift in (-3, 3, -2, 2, -1, 1):
            index = jnp.clip(self.z + shift, 0, self.shards - 1)
            piece = lax.dynamic_index_in_dim(mine, index, 0, False).astype(BF)
            pairs = [
                (i, i + shift) for i in range(self.shards) if 0 <= i + shift < self.shards
            ]
            total = total + lax.ppermute(piece, "shard", pairs).astype(F32)
        low = total.astype(BF)
        one, two, three = (self.side(low, which) for which in (1, 2, 3))
        odd = (self.t & 1) == 1
        a, b = jnp.where(odd, one, low), jnp.where(odd, low, one)
        c, d = jnp.where(odd, three, two), jnp.where(odd, two, three)
        far = self.t >= 2
        return jnp.concatenate(
            [
                jnp.where(far, c, a),
                jnp.where(far, d, b),
                jnp.where(far, a, c),
                jnp.where(far, b, d),
            ],
            0,
        ).astype(F32)

    def gather_tokens(self, rows):
        if not self.fast:
            every = lax.all_gather(rows, "tp", axis=0)
            return [
                lax.dynamic_index_in_dim(every, (self.t + i) % self.tps, 0, False)
                for i in range(self.tps)
            ]
        half = rows.shape[0] // 2
        one = self.side(rows, 1)
        two = self.side(rows, 2)
        top = self.side(one[:half], 2)
        bottom = self.side(two[half:], 1)
        return [rows, one, two, jnp.concatenate([top, bottom], 0)]

    def scatter_tokens(self, parts):
        if not self.fast:
            every = jnp.stack(parts)
            ordered = jnp.stack(
                [
                    lax.dynamic_index_in_dim(every, (i - self.t) % self.tps, 0, False)
                    for i in range(self.tps)
                ]
            )
            return lax.psum_scatter(ordered, "tp", scatter_dimension=0, tiled=False)
        own, one, two, three = parts
        half = own.shape[0] // 2
        top = self.side(three[:half], 1)
        bottom = self.side(three[half:], 2)
        two = jnp.concatenate([two[:half] + top, two[half:]], 0)
        one = jnp.concatenate([one[:half], one[half:] + bottom], 0)
        return (
            own.astype(F32)
            + self.side(one, 1).astype(F32)
            + self.side(two, 2).astype(F32)
        )


def per_device(
    tokens,
    doc_ids,
    w_query,
    b_query,
    key_projection,
    key_bias_vector,
    value_projection,
    value_bias_vector,
    w_output,
    gain_attn,
    gain_mlp,
    w_gate,
    w_up,
    w_down,
    cotangent,
):
    mesh = Mesh()
    token_count, width = tokens.shape
    rows = w_query.shape[0]
    padded = (rows // 16 + 1) * 16
    query_width = QUERY_HEADS * HEAD_WIDTH
    kv_width = KEY_VALUE_HEADS * HEAD_WIDTH
    kv_rows = key_bias_vector.shape[0]
    fused_width = query_width + 2 * kv_width
    blocks = mesh.shards * mesh.ctxs

    small = jnp.concatenate(
        [b_query, key_bias_vector, value_bias_vector, gain_attn, gain_mlp]
    )
    small_ends = [rows, rows + kv_rows, rows + 2 * kv_rows, 2 * rows + 2 * kv_rows]
    small = jnp.pad(small, (0, fused_width - small.shape[0]))
    packed = jnp.concatenate(
        [
            jnp.concatenate([w_query, key_projection, value_projection], 1),
            small[None],
            jnp.zeros((padded - rows - 1, fused_width), BF),
        ],
        0,
    )
    gathered = mesh.gather_rows(packed)
    fused_weight = gathered[:, :rows].reshape(width, fused_width)
    smalls = gathered[:, rows]
    pieces = jnp.split(smalls[:, : small_ends[-1] + rows], small_ends, 1)
    bias_q, bias_k, bias_v, first_gain, second_gain = (
        piece.reshape(-1).astype(F32) for piece in pieces
    )
    fused_bias = jnp.concatenate([bias_q, bias_k, bias_v])

    output_weight = mesh.gather_rows(w_output).reshape(width, width)
    gate_weight = lax.all_gather(w_gate, ("shard", "ctx"), axis=0, tiled=True)
    up_weight = lax.all_gather(w_up, ("shard", "ctx"), axis=0, tiled=True)
    down_weight_t = lax.all_gather(w_down.T, ("shard", "ctx"), axis=0, tiled=True)
    grad_parts = mesh.gather_tokens(cotangent)

    tok_float = tokens.astype(F32)
    first_inv = lax.rsqrt(jnp.mean(tok_float * tok_float, -1, keepdims=True) + EPSILON)
    normed_attn = (tok_float * first_inv * first_gain).astype(BF)
    cosine, sine = rope_tables(mesh.c, token_count)
    fused_t = dot(fused_weight, normed_attn, 0, 1) + fused_bias[:, None]
    query_t = rotate(fused_t[:query_width], cosine, sine).astype(BF) * (HEAD_WIDTH ** (-0.5))
    key_t = rotate(fused_t[query_width : query_width + kv_width], cosine, sine).astype(BF)
    value_t = fused_t[query_width + kv_width :].astype(BF)
    own = jnp.concatenate([key_t, value_t], 0)
    other = mesh.across(own)
    half = mesh.c.astype(jnp.int32).reshape(1)
    doc_col = doc_ids.reshape(-1, 1)
    mixed_t, lse = attention_forward(half, doc_ids, doc_col, query_t, own, other)

    hidden = tok_float + dot(mixed_t, output_weight, 0, 0)
    second_inv = lax.rsqrt(jnp.mean(hidden * hidden, -1, keepdims=True) + EPSILON)
    normed_mlp = (hidden * second_inv * second_gain).astype(BF)
    normed_parts = mesh.gather_tokens(normed_mlp)

    downs, backs, acts, gates, ups = [], [], [], [], []
    for x, g in zip(normed_parts, grad_parts):
        gate = dot(x, gate_weight, 1, 0)
        up = dot(x, up_weight, 1, 0)
        sig = jax.nn.sigmoid(gate)
        silu = gate * sig
        act = (silu * up).astype(BF)
        grad_act = dot(g, down_weight_t, 1, 0)
        grad_gate = (grad_act * up * sig * (1.0 + gate * (1.0 - sig))).astype(BF)
        grad_up = (grad_act * silu).astype(BF)
        backs.append(
            (dot(grad_gate, gate_weight, 1, 1) + dot(grad_up, up_weight, 1, 1)).astype(BF)
        )
        downs.append(dot(act, down_weight_t, 1, 1).astype(BF))
        acts.append(act)
        gates.append(grad_gate)
        ups.append(grad_up)
    grad_normed_mlp = mesh.scatter_tokens(backs).astype(F32)
    down_rows = mesh.scatter_tokens(downs).astype(F32)
    result = hidden + down_rows

    normed_all = jnp.concatenate(normed_parts, 0)
    grad_all = jnp.concatenate(grad_parts, 0)

    def scatter_grad(left, right):
        full = dot(left, jnp.concatenate(right, 0), 0, 0).astype(BF)
        return lax.psum_scatter(full, ("shard", "ctx"), scatter_dimension=0, tiled=True).astype(
            F32
        )

    part_gate = scatter_grad(normed_all, gates)
    part_up = scatter_grad(normed_all, ups)
    part_down = scatter_grad(grad_all, acts).T

    grad_out = cotangent.astype(F32)
    scaled_two = grad_normed_mlp * second_gain
    grad_hidden = (
        grad_out
        + second_inv * scaled_two
        - hidden * second_inv**3 * jnp.mean(scaled_two * hidden, -1, keepdims=True)
    )
    grad_second_gain = jnp.sum(grad_normed_mlp * hidden * second_inv, 0)
    grad_branch = grad_hidden.astype(BF)
    grad_mixed_t = dot(output_weight, grad_branch, 1, 1).astype(BF)
    grad_output_weight = dot(mixed_t, grad_branch, 1, 0)
    grad_query_rot, grad_key_sum, grad_value_sum = attention_backward(
        half, doc_ids, doc_col, query_t, own, other, mixed_t, grad_mixed_t, lse
    )
    sums = jnp.concatenate([grad_key_sum * (HEAD_WIDTH ** (-0.5) * 8.0), grad_value_sum], 0)
    first_half, second_half = sums[:, :token_count], sums[:, token_count:]
    to_other = jnp.where(mesh.c == 0, second_half, first_half).astype(BF)
    own_sums = jnp.where(mesh.c == 0, first_half, second_half)
    own_sums = (own_sums + mesh.across(to_other).astype(F32)).astype(BF).astype(F32)
    own_sums_t = own_sums.transpose(0, 2, 1).reshape(2 * kv_width, token_count)
    grad_query_pre = rotate(grad_query_rot.astype(BF).astype(F32), cosine, -sine)
    grad_key_pre = rotate(own_sums_t[:kv_width], cosine, -sine)
    fused_grad_t = jnp.concatenate([grad_query_pre, grad_key_pre, own_sums_t[kv_width:]], 0)
    grad_fused_bias = jnp.sum(fused_grad_t, 1)
    fused_low = fused_grad_t.astype(BF)
    grad_normed_attn = dot(fused_low, fused_weight, 0, 1)
    grad_fused_weight = dot(normed_attn, fused_low, 0, 1)
    scaled_one = grad_normed_attn * first_gain
    grad_tokens = (
        grad_hidden
        + first_inv * scaled_one
        - tok_float * first_inv**3 * jnp.mean(scaled_one * tok_float, -1, keepdims=True)
    )
    grad_first_gain = jnp.sum(grad_normed_attn * tok_float * first_inv, 0)

    grad_smalls = jnp.concatenate(
        [
            grad_fused_bias[:query_width].reshape(blocks, rows),
            grad_fused_bias[query_width : query_width + kv_width].reshape(blocks, kv_rows),
            grad_fused_bias[query_width + kv_width :].reshape(blocks, kv_rows),
            grad_first_gain.reshape(blocks, rows),
            grad_second_gain.reshape(blocks, rows),
        ],
        1,
    )
    grad_smalls = jnp.pad(grad_smalls, ((0, 0), (0, fused_width - grad_smalls.shape[1])))
    grad_packed = jnp.concatenate(
        [
            grad_fused_weight.reshape(blocks, rows, fused_width),
            grad_smalls[:, None],
            jnp.zeros((blocks, padded - rows - 1, fused_width), F32),
        ],
        1,
    )
    grad_out_padded = jnp.pad(
        grad_output_weight.reshape(blocks, rows, width), ((0, 0), (0, padded - rows), (0, 0))
    )
    sum_output_weight = mesh.reduce_rows(grad_out_padded)[:rows]
    summed = mesh.reduce_rows(grad_packed)
    sum_small = jnp.split(summed[rows, : small_ends[-1] + rows], small_ends)
    return (
        result.astype(BF),
        grad_tokens.astype(BF),
        summed[:rows, :query_width],
        sum_small[0],
        summed[:rows, query_width : query_width + kv_width],
        sum_small[1],
        summed[:rows, query_width + kv_width :],
        sum_small[2],
        sum_output_weight,
        sum_small[3],
        sum_small[4],
        part_gate,
        part_up,
        part_down,
    )


def solution(mesh):
    both = ("shard", "ctx")
    every = ("shard", "ctx", "tp")
    in_specs = (
        P(every, None),
        P(("shard", "tp"), None),
        P(both, None),
        P(both),
        P(both, None),
        P(both),
        P(both, None),
        P(both),
        P(both, None),
        P(both),
        P(both),
        P(both, "tp"),
        P(both, "tp"),
        P("tp", both),
        P(every, None),
    )
    out_specs = (
        P(every, None),
        P(every, None),
        P(both, None),
        P(both),
        P(both, None),
        P(both),
        P(both, None),
        P(both),
        P(both, None),
        P(both),
        P(both),
        P(both, "tp"),
        P(both, "tp"),
        P("tp", both),
    )
    return jax.shard_map(
        per_device, mesh=mesh, in_specs=in_specs, out_specs=out_specs, check_vma=False
    )
```

```python
import jax
import jax.numpy as jnp
from jax import lax
from jax.experimental import pallas as pl
from jax.experimental.pallas import tpu as pltpu
from jax.sharding import PartitionSpec as P


QUERY_HEADS = 14
KEY_VALUE_HEADS = 2
HEAD_WIDTH = 64
GROUP = QUERY_HEADS // KEY_VALUE_HEADS

EPSILON = 1e-06
THETA = 1000000.0
NEGATIVE = -1e30
BF = jnp.bfloat16
F32 = jnp.float32


def dot(left, right, left_dim, right_dim, out=F32):
    return lax.dot_general(
        left, right, (((left_dim,), (right_dim,)), ((), ())), preferred_element_type=out
    )


def fill_bias(bias, doc_row, doc_col, row_start, row_count, span):
    keys = lax.broadcasted_iota(jnp.int32, (span, row_count), 0)
    queries = lax.broadcasted_iota(jnp.int32, (span, row_count), 1) + row_start
    key_doc = doc_col[0:span, :]
    query_doc = doc_row[:, row_start : row_start + row_count]
    same = (key_doc == query_doc) & (query_doc >= 0) & (keys <= queries)
    bias[0:span, :] = jnp.where(same | (keys == queries), 0.0, NEGATIVE)


def load_keys(half, own, other, keys_t, keys, values_t, values):
    width = KEY_VALUE_HEADS * HEAD_WIDTH
    parts = (own,) if half == 0 else (other, own)
    for place, part in enumerate(parts):
        count = part.shape[1]
        rows = slice(place * count, (place + 1) * count)
        key_t = part[0:width, :]
        value_t = part[width : 2 * width, :]
        keys_t[:, rows] = key_t
        values_t[:, rows] = value_t
        key = key_t.astype(F32).T.astype(BF)
        for head in range(KEY_VALUE_HEADS):
            lanes = slice(head * HEAD_WIDTH, (head + 1) * HEAD_WIDTH)
            keys[head, rows, :] = key[:, lanes]
        if values is not None:
            value = value_t.astype(F32).T.astype(BF)
            for head in range(KEY_VALUE_HEADS):
                lanes = slice(head * HEAD_WIDTH, (head + 1) * HEAD_WIDTH)
                values[head, rows, :] = value[:, lanes]


def attention_forward_body(
    half_ref, doc_row, doc_col, query_t, own, other, mixed_t, lse, keys_t, keys, values_t, bias
):
    token_count = query_t.shape[1]
    step = token_count // 2
    for half in (0, 1):

        @pl.when(half_ref[0] == half)
        def _():
            load_keys(half, own, other, keys_t, keys, values_t, None)
            for block in (0, 1):
                span = half * token_count + (block + 1) * step
                start = half * token_count + block * step
                cols = slice(block * step, (block + 1) * step)
                fill_bias(bias, doc_row, doc_col, start, step, span)
                for group in range(KEY_VALUE_HEADS):
                    head_rows = slice(group * HEAD_WIDTH, (group + 1) * HEAD_WIDTH)

                    def one(index, carry):
                        head = group * GROUP + index
                        place = pl.ds(pl.multiple_of(head * HEAD_WIDTH, HEAD_WIDTH), HEAD_WIDTH)
                        score = (
                            jnp.dot(
                                keys[group, 0:span, :],
                                query_t[place, cols],
                                preferred_element_type=F32,
                            )
                            + bias[0:span, :]
                        )
                        top = jnp.max(score, axis=0, keepdims=True)
                        weight = jnp.exp(score - top)
                        total = jnp.sum(weight, axis=0, keepdims=True)
                        out = jnp.dot(
                            values_t[head_rows, 0:span],
                            weight.astype(BF),
                            preferred_element_type=F32,
                        )
                        mixed_t[place, cols] = (out / total).astype(BF)
                        lse[head, :, cols] = jnp.broadcast_to(top + jnp.log(total), (8, step))
                        return carry

                    lax.fori_loop(0, GROUP, one, 0)


def attention_forward(half, doc_row, doc_col, query_t, own, other):
    width, token_count = query_t.shape
    kv = KEY_VALUE_HEADS * HEAD_WIDTH
    vmem = pl.BlockSpec(memory_space=pltpu.VMEM)
    return pl.pallas_call(
        attention_forward_body,
        out_shape=(
            jax.ShapeDtypeStruct((width, token_count), BF),
            jax.ShapeDtypeStruct((QUERY_HEADS, 8, token_count), F32),
        ),
        in_specs=[pl.BlockSpec(memory_space=pltpu.SMEM)] + [vmem] * 5,
        out_specs=(vmem, vmem),
        scratch_shapes=[
            pltpu.VMEM((kv, 2 * token_count), BF),
            pltpu.VMEM((KEY_VALUE_HEADS, 2 * token_count, HEAD_WIDTH), BF),
            pltpu.VMEM((kv, 2 * token_count), BF),
            pltpu.VMEM((2 * token_count, token_count // 2), F32),
        ],
        cost_estimate=pl.CostEstimate(
            flops=int(15e9), bytes_accessed=4 * width * token_count, transcendentals=0
        ),
        name="attention_forward",
    )(half, doc_row, doc_col, query_t, own, other)


def attention_backward_body(
    half_ref,
    doc_row,
    doc_col,
    query_t,
    own,
    other,
    grad_t,
    lse,
    grad_query_t,
    own_sums,
    other_sums,
    grad_key,
    grad_value,
    keys_t,
    keys,
    values_t,
    values,
    bias,
):
    token_count = query_t.shape[1]
    step = token_count // 2
    grad_key[...] = jnp.zeros_like(grad_key)
    grad_value[...] = jnp.zeros_like(grad_value)
    for half in (0, 1):

        @pl.when(half_ref[0] == half)
        def _():
            load_keys(half, own, other, keys_t, keys, values_t, values)
            for block in (0, 1):
                span = half * token_count + (block + 1) * step
                start = half * token_count + block * step
                cols = slice(block * step, (block + 1) * step)
                fill_bias(bias, doc_row, doc_col, start, step, span)
                for group in range(KEY_VALUE_HEADS):
                    head_rows = slice(group * HEAD_WIDTH, (group + 1) * HEAD_WIDTH)

                    def one(index, carry):
                        head = group * GROUP + index
                        place = pl.ds(pl.multiple_of(head * HEAD_WIDTH, HEAD_WIDTH), HEAD_WIDTH)
                        query = query_t[place, cols]
                        grad = grad_t[place, cols]
                        score = (
                            jnp.dot(keys[group, 0:span, :], query, preferred_element_type=F32)
                            + bias[0:span, :]
                        )
                        prob = jnp.exp(score - lse[head, 0:1, cols])
                        grad_prob = jnp.dot(
                            values[group, 0:span, :], grad, preferred_element_type=F32
                        )
                        delta = jnp.sum(prob * grad_prob, axis=0, keepdims=True)
                        grad_score = (prob * (grad_prob - delta)).astype(BF)
                        grad_value[group, 0:span, :] += dot(prob.astype(BF), grad, 1, 1)
                        grad_key[group, 0:span, :] += dot(grad_score, query, 1, 1)
                        grad_query_t[place, cols] = (
                            jnp.dot(
                                keys_t[head_rows, 0:span], grad_score, preferred_element_type=F32
                            )
                            * (HEAD_WIDTH ** (-0.5))
                        ).astype(BF)
                        return carry

                    lax.fori_loop(0, GROUP, one, 0)

            for head in range(2 * KEY_VALUE_HEADS):
                source = (grad_key, grad_value)[head // KEY_VALUE_HEADS]
                rows = slice(head * HEAD_WIDTH, (head + 1) * HEAD_WIDTH)
                first = source[head % KEY_VALUE_HEADS, 0:token_count, :].T
                if half == 0:
                    own_sums[rows, :] = first
                    other_sums[rows, :] = jnp.zeros_like(first)
                else:
                    own_sums[rows, :] = source[head % KEY_VALUE_HEADS, token_count:, :].T
                    other_sums[rows, :] = first


def attention_backward(half, doc_row, doc_col, query_t, own, other, grad_t, lse):
    width, token_count = query_t.shape
    kv = KEY_VALUE_HEADS * HEAD_WIDTH
    vmem = pl.BlockSpec(memory_space=pltpu.VMEM)
    sums = jax.ShapeDtypeStruct((2 * kv, token_count), F32)
    totals = pltpu.VMEM((KEY_VALUE_HEADS, 2 * token_count, HEAD_WIDTH), F32)
    return pl.pallas_call(
        attention_backward_body,
        out_shape=(jax.ShapeDtypeStruct((width, token_count), BF), sums, sums),
        in_specs=[pl.BlockSpec(memory_space=pltpu.SMEM)] + [vmem] * 7,
        out_specs=(vmem, vmem, vmem),
        scratch_shapes=[
            totals,
            totals,
            pltpu.VMEM((kv, 2 * token_count), BF),
            pltpu.VMEM((KEY_VALUE_HEADS, 2 * token_count, HEAD_WIDTH), BF),
            pltpu.VMEM((kv, 2 * token_count), BF),
            pltpu.VMEM((KEY_VALUE_HEADS, 2 * token_count, HEAD_WIDTH), BF),
            pltpu.VMEM((2 * token_count, token_count // 2), F32),
        ],
        cost_estimate=pl.CostEstimate(
            flops=int(35e9), bytes_accessed=8 * width * token_count, transcendentals=0
        ),
        name="attention_backward",
    )(half, doc_row, doc_col, query_t, own, other, grad_t, lse)


def rope_tables(half, token_count):
    half_dim = HEAD_WIDTH // 2
    frequency = THETA ** (-(jnp.arange(half_dim, dtype=F32) * 2.0) / HEAD_WIDTH)
    positions = half * token_count + jnp.arange(token_count, dtype=jnp.int32)
    angles = frequency[:, None] * positions.astype(F32)[None, :]
    return jnp.cos(angles), jnp.sin(angles)


def rotate(values_t, cosine, sine):
    rows, count = values_t.shape
    split = values_t.reshape(rows // HEAD_WIDTH, 2, HEAD_WIDTH // 2, count)
    first, second = split[:, 0], split[:, 1]
    return jnp.stack(
        [first * cosine - second * sine, second * cosine + first * sine], 1
    ).reshape(rows, count)


class Mesh:
    def __init__(self):
        self.shards = lax.axis_size("shard")
        self.ctxs = lax.axis_size("ctx")
        self.tps = lax.axis_size("tp")
        self.fast = (self.shards, self.ctxs, self.tps) == (4, 2, 4)
        self.z = lax.axis_index("shard")
        self.c = lax.axis_index("ctx")
        self.t = lax.axis_index("tp")

    def across(self, value):
        pairs = [(i, self.ctxs - 1 - i) for i in range(self.ctxs)]
        return lax.ppermute(value, "ctx", pairs)

    def side(self, value, which):
        return lax.ppermute(value, "tp", [(i, i ^ which) for i in range(self.tps)])

    def ring(self, value, which):
        return lax.ppermute(value, "shard", [(i, i ^ which) for i in range(self.shards)])

    def place(self):
        return jnp.stack([self.z, self.c, self.t]).astype(jnp.int32)

    def gather_rows(self, block):
        return lax.all_gather(block, ("shard", "ctx"), axis=0)

    def gather_spread(self, block):
        rows, _ = block.shape
        part = rows // self.tps
        quarter = lax.dynamic_slice_in_dim(block, self.t * part, part, 0)
        pieces = [block]
        pieces += [self.ring(quarter, which) for which in (1, 2, 3)]
        far = jnp.concatenate(pieces[1:], 0)
        sides = [self.side(far, which) for which in (1, 2, 3)]
        mine = [block, far] + sides
        theirs = [self.across(piece) for piece in mine]
        return far, sides, assemble_spread(self.place(), mine, theirs, rows)

    def gather_line(self, block, after, later):
        block, after = lax.optimization_barrier((block, after))
        two = self.ring(block, 2)
        one = self.ring(block, 1)
        late, relayed, later = lax.optimization_barrier((block, two, later))
        middle = lax.ppermute(late, "shard", [(1, 2), (2, 1)])
        ends = lax.ppermute(relayed, "shard", [(2, 3), (1, 0)])
        three = jnp.where((self.z == 1) | (self.z == 2), middle, ends)
        return [block, one, two, three]

    def reduce_rows(self, send, keep):
        rows, cols = keep.shape[1:]
        part = keep.astype(F32) + self.across(send).astype(F32)
        part = part.reshape(self.shards, self.tps, rows // self.tps, cols)

        def quarter(which):
            return lax.dynamic_index_in_dim(part, self.t ^ which, 1, False)

        mine = quarter(0)
        for which in (1, 2, 3):
            mine = mine + self.side(quarter(which).astype(BF), which).astype(F32)
        total = lax.dynamic_index_in_dim(mine, self.z, 0, False)
        for which in (3, 2, 1):
            piece = lax.dynamic_index_in_dim(mine, self.z ^ which, 0, False).astype(BF)
            total = total + self.ring(piece, which).astype(F32)
        low = total.astype(BF)
        one, two, three = (self.side(low, which) for which in (1, 2, 3))
        odd = (self.t & 1) == 1
        a, b = jnp.where(odd, one, low), jnp.where(odd, low, one)
        c, d = jnp.where(odd, three, two), jnp.where(odd, two, three)
        far = self.t >= 2
        return jnp.concatenate(
            [
                jnp.where(far, c, a),
                jnp.where(far, d, b),
                jnp.where(far, a, c),
                jnp.where(far, b, d),
            ],
            0,
        ).astype(F32)

    def gather_tokens(self, rows):
        if not self.fast:
            every = lax.all_gather(rows, "tp", axis=0)
            return [
                lax.dynamic_index_in_dim(every, (self.t + i) % self.tps, 0, False)
                for i in range(self.tps)
            ]
        one = self.side(rows, 1)
        two = self.side(rows, 2)
        late, one, two = lax.optimization_barrier((rows, one, two))
        return [rows, one, two, self.side(late, 3)]

    def scatter_tokens(self, parts):
        if not self.fast:
            every = jnp.stack(parts)
            ordered = jnp.stack(
                [
                    lax.dynamic_index_in_dim(every, (i - self.t) % self.tps, 0, False)
                    for i in range(self.tps)
                ]
            )
            return lax.psum_scatter(ordered, "tp", scatter_dimension=0, tiled=False)
        total = parts[0].astype(F32)
        for which in (1, 2, 3):
            total = total + self.side(parts[which], which).astype(F32)
        return total

    def scatter_line(self, send, keep):
        received = self.across(send)
        part = (keep.astype(F32) + received.astype(F32)).astype(BF)
        total = lax.dynamic_index_in_dim(part, self.z, 0, False).astype(F32)
        for which in (2, 3, 1):
            piece = lax.dynamic_index_in_dim(part, self.z ^ which, 0, False)
            total = total + self.ring(piece, which).astype(F32)
        return total


def assemble_spread_body(place, *refs):
    mine, theirs, (out, small) = refs[0:5], refs[5:10], refs[10:]
    rows = out.shape[0] // 8
    part = mine[0].shape[0] // 4
    z, c, t = place[0], place[1], place[2]
    for block in range(8):
        shard, core = block // 2, block % 2
        for side in range(4):
            first = side * part
            count = min(part, rows - first)

            def put(pieces, index, start):
                value = pieces[index][pl.ds(start, part), :]
                out[block * rows + first : block * rows + first + count, :] = value[:count]
                if count < part:
                    small[block, :, :] = value[count:]

            start = pl.multiple_of(jnp.maximum((shard ^ z) - 1, 0) * part, 16)
            for pieces, owned in ((mine, core == c), (theirs, core != c)):

                @pl.when(owned & (shard == z))
                def _():
                    put(pieces, 0, first)

                for which in range(4):

                    @pl.when(owned & (shard != z) & ((side ^ t) == which))
                    def _():
                        put(pieces, 1 + which, start)


def assemble_spread(place, mine, theirs, padded):
    cols = mine[0].shape[1]
    extra = 16
    rows = padded - extra
    vmem = pl.BlockSpec(memory_space=pltpu.VMEM)
    return pl.pallas_call(
        assemble_spread_body,
        out_shape=(
            jax.ShapeDtypeStruct((8 * rows, cols), BF),
            jax.ShapeDtypeStruct((8, extra, cols), BF),
        ),
        in_specs=[pl.BlockSpec(memory_space=pltpu.SMEM)] + [vmem] * 10,
        out_specs=(vmem, vmem),
        cost_estimate=pl.CostEstimate(
            flops=0, bytes_accessed=32 * rows * cols, transcendentals=0
        ),
        name="assemble_spread",
    )(place, *mine, *theirs)


def assemble_line_body(place, *refs):
    mine, theirs, outs = refs[0:4], refs[4:8], refs[8:]
    rows = outs[0].shape[0] // 8
    z, c = place[0], place[1]
    for here in range(4):

        @pl.when(z == here)
        def _():
            for block in range(8):
                shard, core = block // 2, block % 2
                left, right = mine[shard ^ here], theirs[shard ^ here]
                for index, out in enumerate(outs):
                    part = slice(index * rows, (index + 1) * rows)
                    out[block * rows : (block + 1) * rows, :] = jnp.where(
                        core == c, left[part, :], right[part, :]
                    )


def assemble_line(place, mine, theirs, count):
    rows, cols = mine[0].shape
    rows = rows // count
    vmem = pl.BlockSpec(memory_space=pltpu.VMEM)
    return pl.pallas_call(
        assemble_line_body,
        out_shape=[jax.ShapeDtypeStruct((8 * rows, cols), BF)] * count,
        in_specs=[pl.BlockSpec(memory_space=pltpu.SMEM)] + [vmem] * 8,
        out_specs=[vmem] * count,
        cost_estimate=pl.CostEstimate(
            flops=0, bytes_accessed=32 * rows * cols * count, transcendentals=0
        ),
        name="assemble_line",
    )(place, *mine, *theirs)


def projection_gradients_body(
    place,
    grad_query,
    own_sums,
    other_sums,
    cosine,
    sine,
    tokens,
    inverse,
    gain,
    second_gain,
    grad_hidden,
    mixed_t,
    weight,
    grad_tokens,
    send,
    keep,
    fused,
):
    half_dim = HEAD_WIDTH // 2
    query_width, kv = grad_query.shape[0], own_sums.shape[0] // 2
    rows = keep.shape[1] - 16

    def unrotate(value, start):
        first, second = value[:half_dim], value[half_dim:]
        fused[start : start + half_dim, :] = first * cosine[...] + second * sine[...]
        fused[start + half_dim : start + HEAD_WIDTH, :] = (
            second * cosine[...] - first * sine[...]
        )

    for head in range(QUERY_HEADS):
        start = head * HEAD_WIDTH
        unrotate(grad_query[start : start + HEAD_WIDTH, :].astype(F32), start)
    sums = (own_sums[...] + other_sums[...]).astype(BF).astype(F32)
    for head in range(KEY_VALUE_HEADS):
        start = head * HEAD_WIDTH
        unrotate(sums[start : start + HEAD_WIDTH], query_width + start)
    fused[query_width + kv :, :] = sums[kv:]

    exact = fused[...]
    low = exact.astype(BF)
    rest = (exact - low.astype(F32)).astype(BF)
    ones = jnp.ones((16, exact.shape[1]), BF)
    bias = dot(ones, low, 1, 1) + dot(ones, rest, 1, 1)
    low_rows = low.T
    x = tokens[...].astype(F32)
    inv = inverse[...]
    normed_t = (x * inv * gain[...]).astype(BF).T
    grad_normed = dot(low_rows, weight[...], 1, 1)
    scaled = grad_normed * gain[...]
    mean = jnp.mean(scaled * x, -1, keepdims=True)
    hidden = grad_hidden[...]
    grad_tokens[...] = (hidden + inv * scaled - x * (inv * inv * inv) * mean).astype(BF)
    grad_gain = jnp.sum(grad_normed * x * inv, 0, keepdims=True)
    left = jnp.dot(normed_t, low_rows, preferred_element_type=F32).astype(BF)
    right = jnp.dot(
        mixed_t[...], hidden.astype(BF), preferred_element_type=F32
    ).astype(BF)
    split = left.shape[1]
    first_row = jnp.concatenate(
        [bias[:8], jnp.broadcast_to(grad_gain, (8, grad_gain.shape[1]))], 1
    )
    second_row = jnp.concatenate(
        [
            jnp.broadcast_to(second_gain[...], (8, second_gain.shape[1])),
            jnp.zeros((8, split), F32),
        ],
        1,
    )
    index = lax.broadcasted_iota(jnp.int32, first_row.shape, 0)
    small = jnp.where(index == 0, first_row, jnp.where(index == 1, second_row, 0.0))
    small = jnp.concatenate([small, jnp.zeros_like(small)], 0).astype(BF)
    for block in range(8):
        shard, core = block // 2, block % 2
        part = slice(block * rows, (block + 1) * rows)
        for out, owned in ((keep, place[1] == core), (send, place[1] != core)):

            @pl.when(owned)
            def _():
                out[shard, 0:rows, 0:split] = left[part]
                out[shard, 0:rows, split:] = right[part]
                out[shard, rows:, :] = small


def projection_gradients(place, *arrays):
    tokens, weight = arrays[5], arrays[11]
    token_count, width = tokens.shape
    fused_width = weight.shape[1] - width
    vmem = pl.BlockSpec(memory_space=pltpu.VMEM)
    half = jax.ShapeDtypeStruct((4, width // 8 + 16, weight.shape[1]), BF)
    whole = [
        pl.BlockSpec(array.shape, lambda i, n=array.ndim: (0,) * n) for array in arrays[:-1]
    ]
    return pl.pallas_call(
        projection_gradients_body,
        grid=(1,),
        out_shape=(jax.ShapeDtypeStruct(tokens.shape, BF), half, half),
        in_specs=[pl.BlockSpec(memory_space=pltpu.SMEM)]
        + whole
        + [pl.BlockSpec((width, fused_width), lambda i: (0, 0))],
        out_specs=(
            pl.BlockSpec(tokens.shape, lambda i: (0, 0)),
            pl.BlockSpec(half.shape, lambda i: (0, 0, 0)),
            pl.BlockSpec(half.shape, lambda i: (0, 0, 0)),
        ),
        scratch_shapes=[pltpu.VMEM((fused_width, token_count), F32)],
        cost_estimate=pl.CostEstimate(
            flops=int(6e9), bytes_accessed=int(16e6), transcendentals=0
        ),
        name="projection_gradients",
    )(place, *arrays)


def mlp_body(x_ref, g_ref, gate_ref, up_ref, down_ref, *refs):
    back, down, units, rows_t = refs[-4:]
    x, g = x_ref[...], g_ref[...]
    gate = jnp.dot(x, gate_ref[...], preferred_element_type=F32)
    up = jnp.dot(x, up_ref[...], preferred_element_type=F32)
    sig = 1.0 / (1.0 + jnp.exp(-gate))
    silu = gate * sig
    act = (silu * up).astype(BF)
    grad_act = jnp.dot(g, down_ref[...], preferred_element_type=F32)
    grad_gate = (grad_act * up * sig * (1.0 + gate * (1.0 - sig))).astype(BF)
    grad_up = (grad_act * silu).astype(BF)
    back[...] = (
        dot(grad_gate, gate_ref[...], 1, 1) + dot(grad_up, up_ref[...], 1, 1)
    ).astype(BF)
    down[...] = dot(act, down_ref[...], 1, 1).astype(BF)
    units[0] = grad_gate
    units[1] = grad_up
    units[2] = act
    rows_t[0] = x.T
    rows_t[1] = g.T


def mlp(x, g, weights, kept, first, total):
    count, width = x.shape
    units = weights[0].shape[1]
    step = min(256, count)
    offset = first // step
    rows = pl.BlockSpec((step, width), lambda i: (i, 0))
    whole = pl.BlockSpec((width, units), lambda i: (0, 0), pipeline_mode=pl.Buffered(1))
    partial = jax.ShapeDtypeStruct((count, width), BF)
    kept = list(kept)
    outs = pl.pallas_call(
        mlp_body,
        grid=(count // step,),
        out_shape=[
            partial,
            partial,
            jax.ShapeDtypeStruct((3, total, units), BF),
            jax.ShapeDtypeStruct((2, width, total), BF),
        ],
        in_specs=[rows, rows, whole, whole, whole]
        + [pl.BlockSpec(memory_space=pl.ANY)] * len(kept),
        out_specs=[
            rows,
            rows,
            pl.BlockSpec((3, step, units), lambda i: (0, i + offset, 0)),
            pl.BlockSpec((2, width, step), lambda i: (0, 0, i + offset)),
        ],
        input_output_aliases={5 + i: 2 + i for i in range(len(kept))},
        cost_estimate=pl.CostEstimate(
            flops=12 * count * width * units,
            bytes_accessed=6 * width * units + 8 * count * (width + units),
            transcendentals=count * units,
        ),
        name="mlp",
    )(x, g, *weights, *kept)
    return outs[0], outs[1], outs[2:]


def weight_gradients_body(place, left, right, send, keep, total):
    index, last = pl.program_id(1), pl.num_programs(1) - 1
    rows = send.shape[2]
    value = jnp.dot(left[0], right[0], preferred_element_type=F32)

    @pl.when(index == 0)
    def _():
        total[...] = value

    @pl.when(index > 0)
    def _():
        total[...] += value

    @pl.when(index == last)
    def _():
        for block in range(8):
            shard, core = block // 2, block % 2
            piece = total[block * rows : (block + 1) * rows, :].astype(BF)

            @pl.when(place[1] == core)
            def _():
                keep[shard, 0] = piece

            @pl.when(place[1] != core)
            def _():
                send[shard, 0] = piece


def weight_gradients(place, units, rows_t):
    _, total, wide = units.shape
    width = rows_t.shape[1]
    step = total // 2
    half = jax.ShapeDtypeStruct((4, 3, width // 8, wide), BF)
    out = pl.BlockSpec((4, 1, width // 8, wide), lambda w, k: (0, w, 0, 0))
    return pl.pallas_call(
        weight_gradients_body,
        grid=(3, 2),
        out_shape=(half, half),
        in_specs=[
            pl.BlockSpec(memory_space=pltpu.SMEM),
            pl.BlockSpec((1, width, step), lambda w, k: (w // 2, 0, k)),
            pl.BlockSpec((1, step, wide), lambda w, k: (w, k, 0)),
        ],
        out_specs=(out, out),
        scratch_shapes=[pltpu.VMEM((width, wide), F32)],
        cost_estimate=pl.CostEstimate(
            flops=6 * total * width * wide,
            bytes_accessed=6 * total * (width + wide),
            transcendentals=0,
        ),
        name="weight_gradients",
    )(place, rows_t, units)


def per_device(
    tokens,
    doc_ids,
    w_query,
    b_query,
    key_projection,
    key_bias_vector,
    value_projection,
    value_bias_vector,
    w_output,
    gain_attn,
    gain_mlp,
    w_gate,
    w_up,
    w_down,
    cotangent,
):
    mesh = Mesh()
    token_count, width = tokens.shape
    rows = w_query.shape[0]
    padded = (rows + 5 + 15) // 16 * 16
    query_width = QUERY_HEADS * HEAD_WIDTH
    kv_width = KEY_VALUE_HEADS * HEAD_WIDTH
    kv_rows = key_bias_vector.shape[0]
    fused_width = query_width + 2 * kv_width
    blocks = mesh.shards * mesh.ctxs

    all_width = fused_width + width
    small_vectors = [b_query, key_bias_vector, value_bias_vector, gain_attn, gain_mlp]
    small_counts = [vector.shape[0] for vector in small_vectors]
    packed = jnp.concatenate(
        [jnp.concatenate([w_query, key_projection, value_projection, w_output], 1)]
        + [
            jnp.pad(vector[None], ((0, 0), (0, all_width - vector.shape[0])))
            for vector in small_vectors
        ]
        + [jnp.zeros((padded - rows - len(small_vectors), all_width), BF)],
        0,
    )
    if mesh.fast:
        far, sides, (projection, smalls) = mesh.gather_spread(packed)
        line = mesh.gather_line(jnp.concatenate([w_gate, w_up, w_down.T], 0), far, smalls)
        others = [mesh.across(part) for part in line]
        late, sides = lax.optimization_barrier((cotangent, sides))
        grad_parts = mesh.gather_tokens(late)
    else:
        gathered = lax.all_gather(packed, ("shard", "ctx"), axis=0)
        projection = gathered[:, :rows].reshape(width, all_width)
        smalls = gathered[:, rows:]
        weights = [
            lax.all_gather(part, ("shard", "ctx"), axis=0, tiled=True)
            for part in (w_gate, w_up, w_down.T)
        ]
        grad_parts = mesh.gather_tokens(cotangent)
    fused_weight = projection[:, :fused_width]
    output_weight = projection[:, fused_width:]
    bias_q, bias_k, bias_v, first_gain, second_gain = (
        smalls[:, i, :count].reshape(-1).astype(F32) for i, count in enumerate(small_counts)
    )
    fused_bias = jnp.concatenate([bias_q, bias_k, bias_v])

    tok_float = tokens.astype(F32)
    first_inv = lax.rsqrt(jnp.mean(tok_float * tok_float, -1, keepdims=True) + EPSILON)
    normed_attn = (tok_float * first_inv * first_gain).astype(BF)
    cosine, sine = rope_tables(mesh.c, token_count)
    fused_t = dot(fused_weight, normed_attn, 0, 1) + fused_bias[:, None]
    query_t = rotate(fused_t[:query_width], cosine, sine).astype(BF) * (HEAD_WIDTH ** (-0.5))
    key_t = rotate(fused_t[query_width : query_width + kv_width], cosine, sine).astype(BF)
    value_t = fused_t[query_width + kv_width :].astype(BF)
    own = jnp.concatenate([key_t, value_t], 0)
    other = mesh.across(own)
    half = mesh.c.astype(jnp.int32).reshape(1)
    doc_col = doc_ids.reshape(-1, 1)
    mixed_t, lse = attention_forward(half, doc_ids, doc_col, query_t, own, other)

    hidden = tok_float + dot(mixed_t, output_weight, 0, 0)
    second_inv = lax.rsqrt(jnp.mean(hidden * hidden, -1, keepdims=True) + EPSILON)
    normed_mlp = (hidden * second_inv * second_gain).astype(BF)
    normed_parts = mesh.gather_tokens(normed_mlp)
    if mesh.fast:
        line, others, _ = lax.optimization_barrier((line, others, normed_mlp))
        weights = assemble_line(mesh.place(), line, others, 3)

    total = token_count * mesh.tps
    backs, downs, kept = [], [], []
    for index, (x, g) in enumerate(zip(normed_parts, grad_parts)):
        back, down, kept = mlp(x, g, weights, kept, index * token_count, total)
        backs.append(back)
        downs.append(down)
    units, rows_t = kept
    grad_normed_mlp = mesh.scatter_tokens(backs).astype(F32)
    if mesh.fast:
        send, keep = weight_gradients(mesh.place(), units, rows_t)
        part_gate, part_up, part_down = mesh.scatter_line(send, keep)
        downs, grad_normed_mlp = lax.optimization_barrier((downs, grad_normed_mlp))
    else:
        part_gate, part_up, part_down = (
            lax.psum_scatter(
                dot(rows_t[i // 2], units[i], 1, 0),
                ("shard", "ctx"),
                scatter_dimension=0,
                tiled=True,
            )
            for i in range(3)
        )
    part_down = part_down.T
    grad_out = cotangent.astype(F32)
    scaled_two = grad_normed_mlp * second_gain
    grad_hidden = (
        grad_out
        + second_inv * scaled_two
        - hidden * second_inv**3 * jnp.mean(scaled_two * hidden, -1, keepdims=True)
    )
    grad_second_gain = jnp.sum(grad_normed_mlp * hidden * second_inv, 0)
    grad_branch = grad_hidden.astype(BF)
    grad_mixed_t = dot(output_weight, grad_branch, 1, 1).astype(BF)
    grad_query_rot, own_sums, to_other = attention_backward(
        half, doc_ids, doc_col, query_t, own, other, grad_mixed_t, lse
    )
    hidden_late, grad_query_rot = lax.optimization_barrier((hidden, grad_query_rot))
    result = (hidden_late + mesh.scatter_tokens(downs).astype(F32)).astype(BF)
    received = mesh.across(to_other)
    if mesh.fast:
        grad_tokens, send, keep = projection_gradients(
            mesh.place(),
            grad_query_rot,
            own_sums,
            received,
            cosine,
            sine,
            tokens,
            first_inv,
            first_gain[None],
            grad_second_gain[None],
            grad_hidden,
            mixed_t,
            projection,
        )
        summed = mesh.reduce_rows(send, keep)
        index = mesh.z * mesh.ctxs + mesh.c

        def own_part(line, start, count):
            return lax.dynamic_slice_in_dim(line, start + index * count, count, 0)

        first, second = summed[rows], summed[rows + 1]
        sum_small = [
            own_part(first, 0, rows),
            own_part(first, query_width, kv_rows),
            own_part(first, query_width + kv_width, kv_rows),
            own_part(first, fused_width, rows),
            own_part(second, 0, rows),
        ]
        return (
            result,
            grad_tokens,
            summed[:rows, :query_width],
            sum_small[0],
            summed[:rows, query_width : query_width + kv_width],
            sum_small[1],
            summed[:rows, query_width + kv_width : fused_width],
            sum_small[2],
            summed[:rows, fused_width:],
            sum_small[3],
            sum_small[4],
            part_gate,
            part_up,
            part_down,
        )
    grad_output_weight = dot(mixed_t, grad_branch, 1, 0)
    own_sums_t = (own_sums + received).astype(BF).astype(F32)
    grad_query_pre = rotate(grad_query_rot.astype(F32), cosine, -sine)
    grad_key_pre = rotate(own_sums_t[:kv_width], cosine, -sine)
    fused_grad_t = jnp.concatenate([grad_query_pre, grad_key_pre, own_sums_t[kv_width:]], 0)
    grad_fused_bias = jnp.sum(fused_grad_t, 1)
    fused_low = fused_grad_t.astype(BF)
    grad_normed_attn = dot(fused_low, fused_weight, 0, 1)
    grad_fused_weight = dot(normed_attn, fused_low, 0, 1)
    scaled_one = grad_normed_attn * first_gain
    grad_tokens = (
        grad_hidden
        + first_inv * scaled_one
        - tok_float * first_inv**3 * jnp.mean(scaled_one * tok_float, -1, keepdims=True)
    )
    grad_first_gain = jnp.sum(grad_normed_attn * tok_float * first_inv, 0)

    small_sums = [
        grad_fused_bias[:query_width],
        grad_fused_bias[query_width : query_width + kv_width],
        grad_fused_bias[query_width + kv_width :],
        grad_first_gain,
        grad_second_gain,
    ]
    grad_packed = jnp.concatenate(
        [
            jnp.concatenate([grad_fused_weight, grad_output_weight], 1).reshape(
                blocks, rows, all_width
            )
        ]
        + [
            jnp.pad(
                vector.reshape(blocks, 1, count), ((0, 0), (0, 0), (0, all_width - count))
            )
            for vector, count in zip(small_sums, small_counts)
        ]
        + [jnp.zeros((blocks, padded - rows - len(small_sums), all_width), F32)],
        1,
    )
    summed = lax.psum_scatter(grad_packed, ("shard", "ctx"), scatter_dimension=0, tiled=True)
    summed = lax.psum(summed[0], "tp")
    sum_small = [summed[rows + i, :count] for i, count in enumerate(small_counts)]
    return (
        result,
        grad_tokens.astype(BF),
        summed[:rows, :query_width],
        sum_small[0],
        summed[:rows, query_width : query_width + kv_width],
        sum_small[1],
        summed[:rows, query_width + kv_width : fused_width],
        sum_small[2],
        summed[:rows, fused_width:],
        sum_small[3],
        sum_small[4],
        part_gate,
        part_up,
        part_down,
    )


def solution(mesh):
    both = ("shard", "ctx")
    every = ("shard", "ctx", "tp")
    in_specs = (
        P(every, None),
        P(("shard", "tp"), None),
        P(both, None),
        P(both),
        P(both, None),
        P(both),
        P(both, None),
        P(both),
        P(both, None),
        P(both),
        P(both),
        P(both, "tp"),
        P(both, "tp"),
        P("tp", both),
        P(every, None),
    )
    out_specs = (
        P(every, None),
        P(every, None),
        P(both, None),
        P(both),
        P(both, None),
        P(both),
        P(both, None),
        P(both),
        P(both, None),
        P(both),
        P(both),
        P(both, "tp"),
        P(both, "tp"),
        P("tp", both),
    )

    step = jax.shard_map(
        per_device, mesh=mesh, in_specs=in_specs, out_specs=out_specs, check_vma=False
    )
    if tuple(mesh.shape[name] for name in every) != (4, 2, 4):
        return step
    return step
```

```python
import jax
import jax.numpy as jnp
from jax import lax
from jax.experimental import pallas as pl
from jax.experimental.pallas import tpu as pltpu
from jax.sharding import PartitionSpec as P


QUERY_HEADS = 14
KEY_VALUE_HEADS = 2
HEAD_WIDTH = 64
GROUP = QUERY_HEADS // KEY_VALUE_HEADS
HEADS_PER_STEP = 1

EPSILON = 1e-06
THETA = 1000000.0
NEGATIVE = -1e30
BF = jnp.bfloat16
F32 = jnp.float32


def dot(left, right, left_dim, right_dim, out=F32):
    return lax.dot_general(
        left, right, (((left_dim,), (right_dim,)), ((), ())), preferred_element_type=out
    )


def fill_bias(bias, doc_row, doc_col, row_start, row_count, span):
    keys = lax.broadcasted_iota(jnp.int32, (span, row_count), 0)
    queries = lax.broadcasted_iota(jnp.int32, (span, row_count), 1) + row_start
    key_doc = doc_col[0:span, :]
    query_doc = doc_row[:, row_start : row_start + row_count]
    same = (key_doc == query_doc) & (query_doc >= 0) & (keys <= queries)
    bias[0:span, :] = jnp.where(same | (keys == queries), 0.0, NEGATIVE)


def load_keys(half, own, other, keys_t, keys, values_t, values):
    width = KEY_VALUE_HEADS * HEAD_WIDTH
    parts = (own,) if half == 0 else (other, own)
    for place, part in enumerate(parts):
        count = part.shape[1]
        rows = slice(place * count, (place + 1) * count)
        key_t = part[0:width, :]
        value_t = part[width : 2 * width, :]
        keys_t[:, rows] = key_t
        values_t[:, rows] = value_t
        key = key_t.astype(F32).T.astype(BF)
        for head in range(KEY_VALUE_HEADS):
            lanes = slice(head * HEAD_WIDTH, (head + 1) * HEAD_WIDTH)
            keys[head, rows, :] = key[:, lanes]
        if values is not None:
            value = value_t.astype(F32).T.astype(BF)
            for head in range(KEY_VALUE_HEADS):
                lanes = slice(head * HEAD_WIDTH, (head + 1) * HEAD_WIDTH)
                values[head, rows, :] = value[:, lanes]


def attention_forward_body(
    half_ref, doc_row, doc_col, query_t, own, other, mixed_t, lse, keys_t, keys, values_t, bias
):
    token_count = query_t.shape[1]
    step = token_count // 2
    for half in (0, 1):

        @pl.when(half_ref[0] == half)
        def _():
            load_keys(half, own, other, keys_t, keys, values_t, None)
            for block in (0, 1):
                span = half * token_count + (block + 1) * step
                start = half * token_count + block * step
                cols = slice(block * step, (block + 1) * step)
                fill_bias(bias, doc_row, doc_col, start, step, span)

                def one(head):
                    group = lax.div(head, GROUP)
                    head_rows = pl.ds(pl.multiple_of(group * HEAD_WIDTH, HEAD_WIDTH), HEAD_WIDTH)
                    place = pl.ds(pl.multiple_of(head * HEAD_WIDTH, HEAD_WIDTH), HEAD_WIDTH)
                    score = (
                        jnp.dot(
                            keys[group, 0:span, :],
                            query_t[place, cols],
                            preferred_element_type=F32,
                        )
                        + bias[0:span, :]
                    )
                    top = jnp.max(score, axis=0, keepdims=True)
                    weight = jnp.exp(score - top)
                    total = jnp.sum(weight, axis=0, keepdims=True)
                    out = jnp.dot(
                        values_t[head_rows, 0:span],
                        weight.astype(BF),
                        preferred_element_type=F32,
                    )
                    mixed_t[place, cols] = (out / total).astype(BF)
                    lse[head, :, cols] = jnp.broadcast_to(top + jnp.log(total), (8, step))

                def several(index, carry):
                    for extra in range(HEADS_PER_STEP):
                        one(index * HEADS_PER_STEP + extra)
                    return carry

                lax.fori_loop(0, QUERY_HEADS // HEADS_PER_STEP, several, 0)


def attention_forward(half, doc_row, doc_col, query_t, own, other):
    width, token_count = query_t.shape
    kv = KEY_VALUE_HEADS * HEAD_WIDTH
    vmem = pl.BlockSpec(memory_space=pltpu.VMEM)
    return pl.pallas_call(
        attention_forward_body,
        out_shape=(
            jax.ShapeDtypeStruct((width, token_count), BF),
            jax.ShapeDtypeStruct((QUERY_HEADS, 8, token_count), F32),
        ),
        in_specs=[pl.BlockSpec(memory_space=pltpu.SMEM)] + [vmem] * 5,
        out_specs=(vmem, vmem),
        scratch_shapes=[
            pltpu.VMEM((kv, 2 * token_count), BF),
            pltpu.VMEM((KEY_VALUE_HEADS, 2 * token_count, HEAD_WIDTH), BF),
            pltpu.VMEM((kv, 2 * token_count), BF),
            pltpu.VMEM((2 * token_count, token_count // 2), F32),
        ],
        cost_estimate=pl.CostEstimate(
            flops=int(15e9), bytes_accessed=4 * width * token_count, transcendentals=0
        ),
        name="attention_forward",
    )(half, doc_row, doc_col, query_t, own, other)


def attention_backward_body(
    half_ref,
    doc_row,
    doc_col,
    query_t,
    own,
    other,
    grad_t,
    lse,
    grad_query_t,
    own_sums,
    other_sums,
    grad_key,
    grad_value,
    keys_t,
    keys,
    values_t,
    values,
    bias,
):
    token_count = query_t.shape[1]
    step = token_count // 2
    grad_key[...] = jnp.zeros_like(grad_key)
    grad_value[...] = jnp.zeros_like(grad_value)
    for half in (0, 1):

        @pl.when(half_ref[0] == half)
        def _():
            load_keys(half, own, other, keys_t, keys, values_t, values)
            for block in (0, 1):
                span = half * token_count + (block + 1) * step
                start = half * token_count + block * step
                cols = slice(block * step, (block + 1) * step)
                fill_bias(bias, doc_row, doc_col, start, step, span)

                def one(head):
                    group = lax.div(head, GROUP)
                    head_rows = pl.ds(pl.multiple_of(group * HEAD_WIDTH, HEAD_WIDTH), HEAD_WIDTH)
                    place = pl.ds(pl.multiple_of(head * HEAD_WIDTH, HEAD_WIDTH), HEAD_WIDTH)
                    query = query_t[place, cols]
                    grad = grad_t[place, cols]
                    score = (
                        jnp.dot(keys[group, 0:span, :], query, preferred_element_type=F32)
                        + bias[0:span, :]
                    )
                    prob = jnp.exp(score - lse[head, 0:1, cols])
                    grad_prob = jnp.dot(values[group, 0:span, :], grad, preferred_element_type=F32)
                    delta = jnp.sum(prob * grad_prob, axis=0, keepdims=True)
                    grad_score = (prob * (grad_prob - delta)).astype(BF)
                    grad_value[group, 0:span, :] += dot(prob.astype(BF), grad, 1, 1)
                    grad_key[group, 0:span, :] += dot(grad_score, query, 1, 1)
                    grad_query_t[place, cols] = (
                        jnp.dot(keys_t[head_rows, 0:span], grad_score, preferred_element_type=F32)
                        * (HEAD_WIDTH ** (-0.5))
                    ).astype(BF)

                def several(index, carry):
                    for extra in range(HEADS_PER_STEP):
                        one(index * HEADS_PER_STEP + extra)
                    return carry

                lax.fori_loop(0, QUERY_HEADS // HEADS_PER_STEP, several, 0)

            for head in range(2 * KEY_VALUE_HEADS):
                source = (grad_key, grad_value)[head // KEY_VALUE_HEADS]
                rows = slice(head * HEAD_WIDTH, (head + 1) * HEAD_WIDTH)
                first = source[head % KEY_VALUE_HEADS, 0:token_count, :].T
                if half == 0:
                    own_sums[rows, :] = first
                    other_sums[rows, :] = jnp.zeros_like(first)
                else:
                    own_sums[rows, :] = source[head % KEY_VALUE_HEADS, token_count:, :].T
                    other_sums[rows, :] = first


def attention_backward(half, doc_row, doc_col, query_t, own, other, grad_t, lse):
    width, token_count = query_t.shape
    kv = KEY_VALUE_HEADS * HEAD_WIDTH
    vmem = pl.BlockSpec(memory_space=pltpu.VMEM)
    sums = jax.ShapeDtypeStruct((2 * kv, token_count), F32)
    totals = pltpu.VMEM((KEY_VALUE_HEADS, 2 * token_count, HEAD_WIDTH), F32)
    return pl.pallas_call(
        attention_backward_body,
        out_shape=(jax.ShapeDtypeStruct((width, token_count), BF), sums, sums),
        in_specs=[pl.BlockSpec(memory_space=pltpu.SMEM)] + [vmem] * 7,
        out_specs=(vmem, vmem, vmem),
        scratch_shapes=[
            totals,
            totals,
            pltpu.VMEM((kv, 2 * token_count), BF),
            pltpu.VMEM((KEY_VALUE_HEADS, 2 * token_count, HEAD_WIDTH), BF),
            pltpu.VMEM((kv, 2 * token_count), BF),
            pltpu.VMEM((KEY_VALUE_HEADS, 2 * token_count, HEAD_WIDTH), BF),
            pltpu.VMEM((2 * token_count, token_count // 2), F32),
        ],
        cost_estimate=pl.CostEstimate(
            flops=int(35e9), bytes_accessed=8 * width * token_count, transcendentals=0
        ),
        name="attention_backward",
    )(half, doc_row, doc_col, query_t, own, other, grad_t, lse)


def rope_tables(half, token_count):
    half_dim = HEAD_WIDTH // 2
    frequency = THETA ** (-(jnp.arange(half_dim, dtype=F32) * 2.0) / HEAD_WIDTH)
    positions = half * token_count + jnp.arange(token_count, dtype=jnp.int32)
    angles = frequency[:, None] * positions.astype(F32)[None, :]
    return jnp.cos(angles), jnp.sin(angles)


def rotate(values_t, cosine, sine):
    rows, count = values_t.shape
    split = values_t.reshape(rows // HEAD_WIDTH, 2, HEAD_WIDTH // 2, count)
    first, second = split[:, 0], split[:, 1]
    return jnp.stack(
        [first * cosine - second * sine, second * cosine + first * sine], 1
    ).reshape(rows, count)


class Mesh:
    def __init__(self):
        self.shards = lax.axis_size("shard")
        self.ctxs = lax.axis_size("ctx")
        self.tps = lax.axis_size("tp")
        self.fast = (self.shards, self.ctxs, self.tps) == (4, 2, 4)
        self.z = lax.axis_index("shard")
        self.c = lax.axis_index("ctx")
        self.t = lax.axis_index("tp")

    def across(self, value):
        pairs = [(i, self.ctxs - 1 - i) for i in range(self.ctxs)]
        return lax.ppermute(value, "ctx", pairs)

    def side(self, value, which):
        return lax.ppermute(value, "tp", [(i, i ^ which) for i in range(self.tps)])

    def ring(self, value, which):
        return lax.ppermute(value, "shard", [(i, i ^ which) for i in range(self.shards)])

    def place(self):
        return jnp.stack([self.z, self.c, self.t]).astype(jnp.int32)

    def gather_rows(self, block):
        return lax.all_gather(block, ("shard", "ctx"), axis=0)

    def gather_spread(self, block):
        rows, _ = block.shape
        part = rows // self.tps
        quarter = lax.dynamic_slice_in_dim(block, self.t * part, part, 0)
        pieces = [block]
        pieces += [self.ring(quarter, which) for which in (1, 2, 3)]
        far = jnp.concatenate(pieces[1:], 0)
        sides = [self.side(far, which) for which in (1, 2, 3)]
        mine = [block, far] + sides
        theirs = [self.across(piece) for piece in mine]
        return far, sides, mine, theirs

    def gather_line(self, block, after, later):
        block, after = lax.optimization_barrier((block, after))
        two = self.ring(block, 2)
        one = self.ring(block, 1)
        late, relayed, later = lax.optimization_barrier((block, two, later))
        middle = lax.ppermute(late, "shard", [(1, 2), (2, 1)])
        ends = lax.ppermute(relayed, "shard", [(2, 3), (1, 0)])
        three = jnp.where((self.z == 1) | (self.z == 2), middle, ends)
        return [block, one, two, three]

    def reduce_rows(self, send, keep):
        mine, *quarters = fold(self.place(), keep, self.across(send))
        for which, quarter in enumerate(quarters, 1):
            mine = mine + self.side(quarter, which).astype(F32)
        total = lax.dynamic_index_in_dim(mine, self.z, 0, False)
        for which in (3, 2, 1):
            piece = lax.dynamic_index_in_dim(mine, self.z ^ which, 0, False).astype(BF)
            total = total + self.ring(piece, which).astype(F32)
        low = total.astype(BF)
        one, two, three = (self.side(low, which) for which in (1, 2, 3))
        odd = (self.t & 1) == 1
        a, b = jnp.where(odd, one, low), jnp.where(odd, low, one)
        c, d = jnp.where(odd, three, two), jnp.where(odd, two, three)
        far = self.t >= 2
        return jnp.concatenate(
            [
                jnp.where(far, c, a),
                jnp.where(far, d, b),
                jnp.where(far, a, c),
                jnp.where(far, b, d),
            ],
            0,
        ).astype(F32)

    def gather_tokens(self, rows):
        if not self.fast:
            every = lax.all_gather(rows, "tp", axis=0)
            return [
                lax.dynamic_index_in_dim(every, (self.t + i) % self.tps, 0, False)
                for i in range(self.tps)
            ]
        one = self.side(rows, 1)
        two = self.side(rows, 2)
        late, one, two = lax.optimization_barrier((rows, one, two))
        return [rows, one, two, self.side(late, 3)]

    def scatter_tokens(self, parts):
        if not self.fast:
            every = jnp.stack(parts)
            ordered = jnp.stack(
                [
                    lax.dynamic_index_in_dim(every, (i - self.t) % self.tps, 0, False)
                    for i in range(self.tps)
                ]
            )
            return lax.psum_scatter(ordered, "tp", scatter_dimension=0, tiled=False)
        return sum(piece.astype(F32) for piece in self.exchange_tokens(parts))

    def exchange_tokens(self, parts):
        return parts[:1] + [self.side(parts[which], which) for which in (1, 2, 3)]

    def scatter_line(self, send, keep):
        received = self.across(send)
        part = (keep.astype(F32) + received.astype(F32)).astype(BF)
        total = lax.dynamic_index_in_dim(part, self.z, 0, False).astype(F32)
        for which in (2, 3, 1):
            piece = lax.dynamic_index_in_dim(part, self.z ^ which, 0, False)
            total = total + self.ring(piece, which).astype(F32)
        return total


def root_inverse(x):
    return lax.rsqrt(jnp.mean(x * x, -1, keepdims=True) + EPSILON)


def project_body(place, *refs):
    mine, theirs = refs[0:5], refs[5:10]
    tokens, cosine, sine, weight, out_weight, query_t, own, gain_one, gain_two = refs[10:19]
    small, fused = refs[19:]
    width, fused_width = weight.shape
    rows = width // 8
    part = mine[0].shape[0] // 4
    z, c, t = place[0], place[1], place[2]
    for block in range(8):
        shard, core = block // 2, block % 2
        for side in range(4):
            first = side * part
            count = min(part, rows - first)

            def put(pieces, index, start):
                value = pieces[index][pl.ds(start, part), :]
                place_rows = slice(block * rows + first, block * rows + first + count)
                weight[place_rows, :] = value[:count, :fused_width]
                out_weight[place_rows, :] = value[:count, fused_width:]
                if count < part:
                    small[block, :, :] = value[count:, 0:128]

            start = pl.multiple_of(jnp.maximum((shard ^ z) - 1, 0) * part, 16)
            for pieces, owned in ((mine, core == c), (theirs, core != c)):

                @pl.when(owned & (shard == z))
                def _():
                    put(pieces, 0, first)

                for which in range(4):

                    @pl.when(owned & (shard != z) & ((side ^ t) == which))
                    def _():
                        put(pieces, 1 + which, start)

    long = jnp.zeros((16, 1024), F32)
    short = jnp.zeros((16, 128), F32)
    for block in range(8):
        piece = small[block].astype(F32)
        wide = jnp.concatenate([piece, jnp.zeros((16, 896), F32)], 1)
        long = long + (pltpu.roll(wide, rows * block, 1) if block else wide)
        short = short + (pltpu.roll(piece, 16 * block, 1) if block else piece)
    bias = jnp.concatenate([long[0:1, :width], short[1:2], short[2:3]], 1)
    gain = long[3:4, :width]
    gain_one[...] = gain
    gain_two[...] = long[4:5, :width]
    x = tokens[...].astype(F32)
    normed = (x * root_inverse(x) * gain).astype(BF)
    fused[...] = (jnp.dot(normed, weight[...], preferred_element_type=F32) + bias).T
    half_dim = HEAD_WIDTH // 2
    query_width = QUERY_HEADS * HEAD_WIDTH
    kv = KEY_VALUE_HEADS * HEAD_WIDTH
    for head in range(QUERY_HEADS + KEY_VALUE_HEADS):
        start = head * HEAD_WIDTH
        one = fused[start : start + half_dim, :]
        two = fused[start + half_dim : start + HEAD_WIDTH, :]
        low = (one * cosine[...] - two * sine[...]).astype(BF)
        high = (two * cosine[...] + one * sine[...]).astype(BF)
        if head < QUERY_HEADS:
            scale = HEAD_WIDTH ** (-0.5)
            query_t[start : start + half_dim, :] = low * BF(scale)
            query_t[start + half_dim : start + HEAD_WIDTH, :] = high * BF(scale)
        else:
            start -= query_width
            own[start : start + half_dim, :] = low
            own[start + half_dim : start + HEAD_WIDTH, :] = high
    own[kv:, :] = fused[query_width + kv :, :].astype(BF)


def project(place, mine, theirs, tokens, cosine, sine, fused_width):
    token_count, width = tokens.shape
    vmem = pl.BlockSpec(memory_space=pltpu.VMEM)
    kv = KEY_VALUE_HEADS * HEAD_WIDTH
    row = jax.ShapeDtypeStruct((1, width), F32)
    return pl.pallas_call(
        project_body,
        out_shape=(
            jax.ShapeDtypeStruct((width, fused_width), BF),
            jax.ShapeDtypeStruct((width, width), BF),
            jax.ShapeDtypeStruct((QUERY_HEADS * HEAD_WIDTH, token_count), BF),
            jax.ShapeDtypeStruct((2 * kv, token_count), BF),
            row,
            row,
        ),
        in_specs=[pl.BlockSpec(memory_space=pltpu.SMEM)] + [vmem] * 13,
        out_specs=(vmem,) * 6,
        scratch_shapes=[
            pltpu.VMEM((8, 16, 128), BF),
            pltpu.VMEM((fused_width, token_count), F32),
        ],
        cost_estimate=pl.CostEstimate(
            flops=int(3e9), bytes_accessed=int(12e6), transcendentals=0
        ),
        name="project",
    )(place, *mine, *theirs, tokens, cosine, sine)


def output_body(tokens, mixed_t, weight, gain, hidden, normed):
    value = tokens[...].astype(F32) + jnp.dot(
        mixed_t[...].T, weight[...], preferred_element_type=F32
    )
    hidden[...] = value
    normed[...] = (value * root_inverse(value) * gain[...]).astype(BF)


def output_projection(tokens, mixed_t, weight, gain):
    vmem = pl.BlockSpec(memory_space=pltpu.VMEM)
    return pl.pallas_call(
        output_body,
        out_shape=(
            jax.ShapeDtypeStruct(tokens.shape, F32),
            jax.ShapeDtypeStruct(tokens.shape, BF),
        ),
        in_specs=[vmem] * 4,
        out_specs=(vmem, vmem),
        cost_estimate=pl.CostEstimate(
            flops=int(1e9), bytes_accessed=int(6e6), transcendentals=0
        ),
        name="output_projection",
    )(tokens, mixed_t, weight, gain)


def middle_body(
    own, one, two, three, hidden, cotangent, weight, gain, grad_hidden, grad_mixed_t, grad_gain
):
    total = own[...].astype(F32) + one[...].astype(F32)
    total = total + two[...].astype(F32) + three[...].astype(F32)
    h = hidden[...]
    inv = root_inverse(h)
    scaled = total * gain[...]
    mean = jnp.mean(scaled * h, -1, keepdims=True)
    value = cotangent[...].astype(F32) + inv * scaled - h * (inv * inv * inv) * mean
    grad_hidden[...] = value
    grad_gain[...] = jnp.sum(total * h * inv, 0, keepdims=True)
    grad_mixed_t[...] = dot(weight[...], value.astype(BF), 1, 1).astype(BF)


def middle(parts, hidden, cotangent, weight, gain):
    vmem = pl.BlockSpec(memory_space=pltpu.VMEM)
    return pl.pallas_call(
        middle_body,
        out_shape=(
            jax.ShapeDtypeStruct(hidden.shape, F32),
            jax.ShapeDtypeStruct(hidden.shape[::-1], BF),
            jax.ShapeDtypeStruct(gain.shape, F32),
        ),
        in_specs=[vmem] * 8,
        out_specs=(vmem, vmem, vmem),
        cost_estimate=pl.CostEstimate(
            flops=int(1e9), bytes_accessed=int(9e6), transcendentals=0
        ),
        name="middle",
    )(*parts, hidden, cotangent, weight, gain)


def fold_body(place, keep, received, mine, *sends):
    part = mine.shape[1]
    for which, out in enumerate((mine,) + sends):
        rows = pl.ds(pl.multiple_of((place[2] ^ which) * part, 16), part)
        value = keep[0, rows, :].astype(F32) + received[0, rows, :].astype(F32)
        out[0] = value.astype(out.dtype)


def fold(place, keep, received):
    blocks, rows, cols = keep.shape
    part = rows // 4
    shape = (blocks, part, cols)
    return pl.pallas_call(
        fold_body,
        grid=(blocks,),
        out_shape=(jax.ShapeDtypeStruct(shape, F32),) + (jax.ShapeDtypeStruct(shape, BF),) * 3,
        in_specs=[pl.BlockSpec(memory_space=pltpu.SMEM)]
        + [pl.BlockSpec((1, rows, cols), lambda i: (i, 0, 0))] * 2,
        out_specs=(pl.BlockSpec((1, part, cols), lambda i: (i, 0, 0)),) * 4,
        cost_estimate=pl.CostEstimate(
            flops=0, bytes_accessed=6 * blocks * rows * cols, transcendentals=0
        ),
        name="fold",
    )(place, keep, received)


def assemble_line_body(place, *refs):
    mine, theirs, out = refs[0:4], refs[4:8], refs[8]
    rows = mine[0].shape[0]
    z, c = place[0], place[1]
    for here in range(4):

        @pl.when(z == here)
        def _():
            for block in range(8):
                shard, core = block // 2, block % 2
                left, right = mine[shard ^ here], theirs[shard ^ here]
                out[0, block * rows : (block + 1) * rows, :] = jnp.where(
                    core == c, left[...], right[...]
                )


def assemble_line(place, mine, theirs, count):
    rows, cols = mine[0].shape
    rows = rows // count
    part = pl.BlockSpec((rows, cols), lambda i: (i, 0))
    return pl.pallas_call(
        assemble_line_body,
        grid=(count,),
        out_shape=jax.ShapeDtypeStruct((count, 8 * rows, cols), BF),
        in_specs=[pl.BlockSpec(memory_space=pltpu.SMEM)] + [part] * 8,
        out_specs=pl.BlockSpec((1, 8 * rows, cols), lambda i: (i, 0, 0)),
        cost_estimate=pl.CostEstimate(
            flops=0, bytes_accessed=32 * rows * cols * count, transcendentals=0
        ),
        name="assemble_line",
    )(place, *mine, *theirs)


def projection_gradients_body(
    place,
    grad_query,
    own_sums,
    other_sums,
    cosine,
    sine,
    tokens,
    gain,
    second_gain,
    grad_hidden,
    mixed_t,
    weight,
    grad_tokens,
    send,
    keep,
    fused,
):
    half_dim = HEAD_WIDTH // 2
    query_width, kv = grad_query.shape[0], own_sums.shape[0] // 2
    rows = keep.shape[1] - 16

    def unrotate(value, start):
        first, second = value[:half_dim], value[half_dim:]
        fused[start : start + half_dim, :] = first * cosine[...] + second * sine[...]
        fused[start + half_dim : start + HEAD_WIDTH, :] = (
            second * cosine[...] - first * sine[...]
        )

    for head in range(QUERY_HEADS):
        start = head * HEAD_WIDTH
        unrotate(grad_query[start : start + HEAD_WIDTH, :].astype(F32), start)
    sums = (own_sums[...] + other_sums[...]).astype(BF).astype(F32)
    for head in range(KEY_VALUE_HEADS):
        start = head * HEAD_WIDTH
        unrotate(sums[start : start + HEAD_WIDTH], query_width + start)
    fused[query_width + kv :, :] = sums[kv:]

    exact = fused[...]
    low = exact.astype(BF)
    rest = (exact - low.astype(F32)).astype(BF)
    ones = jnp.ones((16, exact.shape[1]), BF)
    bias = dot(ones, low, 1, 1) + dot(ones, rest, 1, 1)
    low_rows = low.T
    x = tokens[...].astype(F32)
    inv = root_inverse(x)
    normed_t = (x * inv * gain[...]).astype(BF).T
    grad_normed = dot(low_rows, weight[...], 1, 1)
    scaled = grad_normed * gain[...]
    mean = jnp.mean(scaled * x, -1, keepdims=True)
    hidden = grad_hidden[...]
    grad_tokens[...] = (hidden + inv * scaled - x * (inv * inv * inv) * mean).astype(BF)
    grad_gain = jnp.sum(grad_normed * x * inv, 0, keepdims=True)
    left = jnp.dot(normed_t, low_rows, preferred_element_type=F32).astype(BF)
    right = jnp.dot(
        mixed_t[...], hidden.astype(BF), preferred_element_type=F32
    ).astype(BF)
    split = left.shape[1]
    first_row = jnp.concatenate(
        [bias[:8], jnp.broadcast_to(grad_gain, (8, grad_gain.shape[1]))], 1
    )
    second_row = jnp.concatenate(
        [
            jnp.broadcast_to(second_gain[...], (8, second_gain.shape[1])),
            jnp.zeros((8, split), F32),
        ],
        1,
    )
    index = lax.broadcasted_iota(jnp.int32, first_row.shape, 0)
    small = jnp.where(index == 0, first_row, jnp.where(index == 1, second_row, 0.0))
    small = jnp.concatenate([small, jnp.zeros_like(small)], 0).astype(BF)
    for block in range(8):
        shard, core = block // 2, block % 2
        part = slice(block * rows, (block + 1) * rows)
        for out, owned in ((keep, place[1] == core), (send, place[1] != core)):

            @pl.when(owned)
            def _():
                out[shard, 0:rows, 0:split] = left[part]
                out[shard, 0:rows, split:] = right[part]
                out[shard, rows:, :] = small


def projection_gradients(place, *arrays):
    tokens, weight = arrays[5], arrays[10]
    token_count, width = tokens.shape
    fused_width = weight.shape[1]
    half = jax.ShapeDtypeStruct((4, width // 8 + 16, fused_width + width), BF)
    whole = [
        pl.BlockSpec(array.shape, lambda i, n=array.ndim: (0,) * n) for array in arrays
    ]
    return pl.pallas_call(
        projection_gradients_body,
        grid=(1,),
        out_shape=(jax.ShapeDtypeStruct(tokens.shape, BF), half, half),
        in_specs=[pl.BlockSpec(memory_space=pltpu.SMEM)]
        + whole,
        out_specs=(
            pl.BlockSpec(tokens.shape, lambda i: (0, 0)),
            pl.BlockSpec(half.shape, lambda i: (0, 0, 0)),
            pl.BlockSpec(half.shape, lambda i: (0, 0, 0)),
        ),
        scratch_shapes=[pltpu.VMEM((fused_width, token_count), F32)],
        cost_estimate=pl.CostEstimate(
            flops=int(6e9), bytes_accessed=int(16e6), transcendentals=0
        ),
        name="projection_gradients",
    )(place, *arrays)


def mlp_body(x_ref, g_ref, gate_ref, up_ref, down_ref, *refs):
    back, down, units, rows_t = refs[-4:]
    x, g = x_ref[...], g_ref[...]
    gate = jnp.dot(x, gate_ref[...], preferred_element_type=F32)
    up = jnp.dot(x, up_ref[...], preferred_element_type=F32)
    sig = 1.0 / (1.0 + jnp.exp(-gate))
    silu = gate * sig
    act = (silu * up).astype(BF)
    grad_act = jnp.dot(g, down_ref[...], preferred_element_type=F32)
    grad_gate = (grad_act * up * sig * (1.0 + gate * (1.0 - sig))).astype(BF)
    grad_up = (grad_act * silu).astype(BF)
    back[...] = (
        dot(grad_gate, gate_ref[...], 1, 1) + dot(grad_up, up_ref[...], 1, 1)
    ).astype(BF)
    down[...] = dot(act, down_ref[...], 1, 1).astype(BF)
    units[0] = grad_gate
    units[1] = grad_up
    units[2] = act
    rows_t[0] = x.T
    rows_t[1] = g.T


def mlp(x, g, weights, kept, first, total):
    count, width = x.shape
    units = weights.shape[2]
    step = min(256, count)
    offset = first // step
    rows = pl.BlockSpec((step, width), lambda i: (i, 0))
    whole = [
        pl.BlockSpec(
            (pl.Squeezed(), width, units), lambda i, n=n: (n, 0, 0), pipeline_mode=pl.Buffered(1)
        )
        for n in range(3)
    ]
    partial = jax.ShapeDtypeStruct((count, width), BF)
    kept = list(kept)
    outs = pl.pallas_call(
        mlp_body,
        grid=(count // step,),
        out_shape=[
            partial,
            partial,
            jax.ShapeDtypeStruct((3, total, units), BF),
            jax.ShapeDtypeStruct((2, width, total), BF),
        ],
        in_specs=[rows, rows] + whole
        + [pl.BlockSpec(memory_space=pl.ANY)] * len(kept),
        out_specs=[
            rows,
            rows,
            pl.BlockSpec((3, step, units), lambda i: (0, i + offset, 0)),
            pl.BlockSpec((2, width, step), lambda i: (0, 0, i + offset)),
        ],
        input_output_aliases={5 + i: 2 + i for i in range(len(kept))},
        cost_estimate=pl.CostEstimate(
            flops=12 * count * width * units,
            bytes_accessed=6 * width * units + 8 * count * (width + units),
            transcendentals=count * units,
        ),
        name="mlp",
    )(x, g, weights, weights, weights, *kept)
    return outs[0], outs[1], outs[2:]


def weight_gradients_body(place, left, right, send, keep, total):
    index, last = pl.program_id(1), pl.num_programs(1) - 1
    rows = send.shape[2]
    value = jnp.dot(left[0], right[0], preferred_element_type=F32)

    @pl.when(index == 0)
    def _():
        total[...] = value

    @pl.when(index > 0)
    def _():
        total[...] += value

    @pl.when(index == last)
    def _():
        for block in range(8):
            shard, core = block // 2, block % 2
            piece = total[block * rows : (block + 1) * rows, :].astype(BF)

            @pl.when(place[1] == core)
            def _():
                keep[shard, 0] = piece

            @pl.when(place[1] != core)
            def _():
                send[shard, 0] = piece


def weight_gradients(place, units, rows_t):
    _, total, wide = units.shape
    width = rows_t.shape[1]
    step = total // 2
    half = jax.ShapeDtypeStruct((4, 3, width // 8, wide), BF)
    out = pl.BlockSpec((4, 1, width // 8, wide), lambda w, k: (0, w, 0, 0))
    return pl.pallas_call(
        weight_gradients_body,
        grid=(3, 2),
        out_shape=(half, half),
        in_specs=[
            pl.BlockSpec(memory_space=pltpu.SMEM),
            pl.BlockSpec((1, width, step), lambda w, k: (w // 2, 0, k)),
            pl.BlockSpec((1, step, wide), lambda w, k: (w, k, 0)),
        ],
        out_specs=(out, out),
        scratch_shapes=[pltpu.VMEM((width, wide), F32)],
        cost_estimate=pl.CostEstimate(
            flops=6 * total * width * wide,
            bytes_accessed=6 * total * (width + wide),
            transcendentals=0,
        ),
        name="weight_gradients",
    )(place, rows_t, units)


def per_device(
    tokens,
    doc_ids,
    w_query,
    b_query,
    key_projection,
    key_bias_vector,
    value_projection,
    value_bias_vector,
    w_output,
    gain_attn,
    gain_mlp,
    w_gate,
    w_up,
    w_down,
    cotangent,
):
    mesh = Mesh()
    token_count, width = tokens.shape
    rows = w_query.shape[0]
    padded = (rows + 5 + 15) // 16 * 16
    query_width = QUERY_HEADS * HEAD_WIDTH
    kv_width = KEY_VALUE_HEADS * HEAD_WIDTH
    kv_rows = key_bias_vector.shape[0]
    fused_width = query_width + 2 * kv_width
    blocks = mesh.shards * mesh.ctxs

    all_width = fused_width + width
    small_vectors = [b_query, key_bias_vector, value_bias_vector, gain_attn, gain_mlp]
    small_counts = [vector.shape[0] for vector in small_vectors]
    packed = jnp.concatenate(
        [jnp.concatenate([w_query, key_projection, value_projection, w_output], 1)]
        + [
            jnp.pad(vector[None], ((0, 0), (0, all_width - vector.shape[0])))
            for vector in small_vectors
        ]
        + [jnp.zeros((padded - rows - len(small_vectors), all_width), BF)],
        0,
    )
    if mesh.fast:
        far, sides, mine, theirs = mesh.gather_spread(packed)
        cosine, sine = rope_tables(mesh.c, token_count)
        fused_weight, output_weight, query_t, own, first_gain, second_gain = project(
            mesh.place(), mine, theirs, tokens, cosine, sine, fused_width
        )
        line = mesh.gather_line(jnp.concatenate([w_gate, w_up, w_down.T], 0), far, own)
        others = [mesh.across(part) for part in line]
        late, sides = lax.optimization_barrier((cotangent, sides))
        grad_parts = mesh.gather_tokens(late)
    else:
        gathered = lax.all_gather(packed, ("shard", "ctx"), axis=0)
        projection = gathered[:, :rows].reshape(width, all_width)
        smalls = gathered[:, rows:]
        weights = jnp.stack(
            [
                lax.all_gather(part, ("shard", "ctx"), axis=0, tiled=True)
                for part in (w_gate, w_up, w_down.T)
            ]
        )
        grad_parts = mesh.gather_tokens(cotangent)
        fused_weight = projection[:, :fused_width]
        output_weight = projection[:, fused_width:]
        bias_q, bias_k, bias_v, first_gain, second_gain = (
            smalls[:, i, :count].reshape(-1).astype(F32) for i, count in enumerate(small_counts)
        )
        fused_bias = jnp.concatenate([bias_q, bias_k, bias_v])
        tok_float = tokens.astype(F32)
        first_inv = root_inverse(tok_float)
        normed_attn = (tok_float * first_inv * first_gain).astype(BF)
        cosine, sine = rope_tables(mesh.c, token_count)
        fused_t = dot(fused_weight, normed_attn, 0, 1) + fused_bias[:, None]
        query_t = rotate(fused_t[:query_width], cosine, sine).astype(BF) * (HEAD_WIDTH ** (-0.5))
        key_t = rotate(fused_t[query_width : query_width + kv_width], cosine, sine).astype(BF)
        value_t = fused_t[query_width + kv_width :].astype(BF)
        own = jnp.concatenate([key_t, value_t], 0)
        first_gain, second_gain = first_gain[None], second_gain[None]
    other = mesh.across(own)
    half = mesh.c.astype(jnp.int32).reshape(1)
    doc_col = doc_ids.reshape(-1, 1)
    mixed_t, lse = attention_forward(half, doc_ids, doc_col, query_t, own, other)

    hidden, normed_mlp = output_projection(tokens, mixed_t, output_weight, second_gain)
    normed_parts = mesh.gather_tokens(normed_mlp)
    if mesh.fast:
        line, others, _ = lax.optimization_barrier((line, others, normed_mlp))
        weights = assemble_line(mesh.place(), line, others, 3)

    total = token_count * mesh.tps
    backs, downs, kept = [], [], []
    for index, (x, g) in enumerate(zip(normed_parts, grad_parts)):
        back, down, kept = mlp(x, g, weights, kept, index * token_count, total)
        backs.append(back)
        downs.append(down)
    units, rows_t = kept
    if mesh.fast:
        back_parts = mesh.exchange_tokens(backs)
    else:
        zero = jnp.zeros_like(tokens)
        back_parts = [mesh.scatter_tokens(backs).astype(BF), zero, zero, zero]
    if mesh.fast:
        send, keep = weight_gradients(mesh.place(), units, rows_t)
        part_gate, part_up, part_down = mesh.scatter_line(send, keep)
        downs, back_parts = lax.optimization_barrier((downs, back_parts))
    else:
        part_gate, part_up, part_down = (
            lax.psum_scatter(
                dot(rows_t[i // 2], units[i], 1, 0),
                ("shard", "ctx"),
                scatter_dimension=0,
                tiled=True,
            )
            for i in range(3)
        )
    part_down = part_down.T
    grad_hidden, grad_mixed_t, grad_second_gain = middle(
        back_parts, hidden, cotangent, output_weight, second_gain
    )
    grad_query_rot, own_sums, to_other = attention_backward(
        half, doc_ids, doc_col, query_t, own, other, grad_mixed_t, lse
    )
    hidden_late, grad_query_rot = lax.optimization_barrier((hidden, grad_query_rot))
    result = (hidden_late + mesh.scatter_tokens(downs).astype(F32)).astype(BF)
    received = mesh.across(to_other)
    if mesh.fast:
        grad_tokens, send, keep = projection_gradients(
            mesh.place(),
            grad_query_rot,
            own_sums,
            received,
            cosine,
            sine,
            tokens,
            first_gain,
            grad_second_gain,
            grad_hidden,
            mixed_t,
            fused_weight,
        )
        summed = mesh.reduce_rows(send, keep)
        index = mesh.z * mesh.ctxs + mesh.c

        def own_part(line, start, count):
            return lax.dynamic_slice_in_dim(line, start + index * count, count, 0)

        first, second = summed[rows], summed[rows + 1]
        sum_small = [
            own_part(first, 0, rows),
            own_part(first, query_width, kv_rows),
            own_part(first, query_width + kv_width, kv_rows),
            own_part(first, fused_width, rows),
            own_part(second, 0, rows),
        ]
        return (
            result,
            grad_tokens,
            summed[:rows, :query_width],
            sum_small[0],
            summed[:rows, query_width : query_width + kv_width],
            sum_small[1],
            summed[:rows, query_width + kv_width : fused_width],
            sum_small[2],
            summed[:rows, fused_width:],
            sum_small[3],
            sum_small[4],
            part_gate,
            part_up,
            part_down,
        )
    grad_output_weight = dot(mixed_t, grad_hidden.astype(BF), 1, 0)
    own_sums_t = (own_sums + received).astype(BF).astype(F32)
    grad_query_pre = rotate(grad_query_rot.astype(F32), cosine, -sine)
    grad_key_pre = rotate(own_sums_t[:kv_width], cosine, -sine)
    fused_grad_t = jnp.concatenate([grad_query_pre, grad_key_pre, own_sums_t[kv_width:]], 0)
    grad_fused_bias = jnp.sum(fused_grad_t, 1)
    fused_low = fused_grad_t.astype(BF)
    grad_normed_attn = dot(fused_low, fused_weight, 0, 1)
    grad_fused_weight = dot(normed_attn, fused_low, 0, 1)
    scaled_one = grad_normed_attn * first_gain
    grad_tokens = (
        grad_hidden
        + first_inv * scaled_one
        - tok_float * first_inv**3 * jnp.mean(scaled_one * tok_float, -1, keepdims=True)
    )
    grad_first_gain = jnp.sum(grad_normed_attn * tok_float * first_inv, 0)

    small_sums = [
        grad_fused_bias[:query_width],
        grad_fused_bias[query_width : query_width + kv_width],
        grad_fused_bias[query_width + kv_width :],
        grad_first_gain,
        grad_second_gain[0],
    ]
    grad_packed = jnp.concatenate(
        [
            jnp.concatenate([grad_fused_weight, grad_output_weight], 1).reshape(
                blocks, rows, all_width
            )
        ]
        + [
            jnp.pad(
                vector.reshape(blocks, 1, count), ((0, 0), (0, 0), (0, all_width - count))
            )
            for vector, count in zip(small_sums, small_counts)
        ]
        + [jnp.zeros((blocks, padded - rows - len(small_sums), all_width), F32)],
        1,
    )
    summed = lax.psum_scatter(grad_packed, ("shard", "ctx"), scatter_dimension=0, tiled=True)
    summed = lax.psum(summed[0], "tp")
    sum_small = [summed[rows + i, :count] for i, count in enumerate(small_counts)]
    return (
        result,
        grad_tokens.astype(BF),
        summed[:rows, :query_width],
        sum_small[0],
        summed[:rows, query_width : query_width + kv_width],
        sum_small[1],
        summed[:rows, query_width + kv_width : fused_width],
        sum_small[2],
        summed[:rows, fused_width:],
        sum_small[3],
        sum_small[4],
        part_gate,
        part_up,
        part_down,
    )


def solution(mesh):
    both = ("shard", "ctx")
    every = ("shard", "ctx", "tp")
    in_specs = (
        P(every, None),
        P(("shard", "tp"), None),
        P(both, None),
        P(both),
        P(both, None),
        P(both),
        P(both, None),
        P(both),
        P(both, None),
        P(both),
        P(both),
        P(both, "tp"),
        P(both, "tp"),
        P("tp", both),
        P(every, None),
    )
    out_specs = (
        P(every, None),
        P(every, None),
        P(both, None),
        P(both),
        P(both, None),
        P(both),
        P(both, None),
        P(both),
        P(both, None),
        P(both),
        P(both),
        P(both, "tp"),
        P(both, "tp"),
        P("tp", both),
    )

    step = jax.shard_map(
        per_device, mesh=mesh, in_specs=in_specs, out_specs=out_specs, check_vma=False
    )
    if tuple(mesh.shape[name] for name in every) != (4, 2, 4):
        return step
    return step
```

```python
import functools

import jax
import jax.numpy as jnp
from jax import lax
from jax.experimental import pallas as pl
from jax.experimental.pallas import tpu as pltpu
from jax.sharding import PartitionSpec as P


QUERY_HEADS = 14
KEY_VALUE_HEADS = 2
HEAD_WIDTH = 64
GROUP = QUERY_HEADS // KEY_VALUE_HEADS
HEADS_PER_STEP = 1

EPSILON = 1e-06
THETA = 1000000.0
NEGATIVE = -1e30
BF = jnp.bfloat16
F32 = jnp.float32


def dot(left, right, left_dim, right_dim, out=F32):
    return lax.dot_general(
        left, right, (((left_dim,), (right_dim,)), ((), ())), preferred_element_type=out
    )


def fill_bias(bias, doc_row, doc_col, row_start, row_count, span):
    keys = lax.broadcasted_iota(jnp.int32, (span, row_count), 0)
    queries = lax.broadcasted_iota(jnp.int32, (span, row_count), 1) + row_start
    key_doc = doc_col[0:span, :]
    query_doc = doc_row[:, row_start : row_start + row_count]
    same = (key_doc == query_doc) & (query_doc >= 0) & (keys <= queries)
    bias[0:span, :] = jnp.where(same | (keys == queries), 0.0, NEGATIVE)


def load_keys(half, own, other, keys_t, keys, values_t, values):
    width = KEY_VALUE_HEADS * HEAD_WIDTH
    parts = (own,) if half == 0 else (other, own)
    for place, part in enumerate(parts):
        count = part.shape[1]
        rows = slice(place * count, (place + 1) * count)
        key_t = part[0:width, :]
        value_t = part[width : 2 * width, :]
        keys_t[:, rows] = key_t
        values_t[:, rows] = value_t
        key = key_t.astype(F32).T.astype(BF)
        for head in range(KEY_VALUE_HEADS):
            lanes = slice(head * HEAD_WIDTH, (head + 1) * HEAD_WIDTH)
            keys[head, rows, :] = key[:, lanes]
        if values is not None:
            value = value_t.astype(F32).T.astype(BF)
            for head in range(KEY_VALUE_HEADS):
                lanes = slice(head * HEAD_WIDTH, (head + 1) * HEAD_WIDTH)
                values[head, rows, :] = value[:, lanes]


def attention_forward_body(
    half_ref, doc_row, doc_col, query_t, own, other, mixed_t, lse, keys_t, keys, values_t, bias
):
    token_count = query_t.shape[1]
    step = token_count // 2
    for half in (0, 1):

        @pl.when(half_ref[0] == half)
        def _():
            load_keys(half, own, other, keys_t, keys, values_t, None)
            for block in (0, 1):
                span = half * token_count + (block + 1) * step
                start = half * token_count + block * step
                cols = slice(block * step, (block + 1) * step)
                fill_bias(bias, doc_row, doc_col, start, step, span)

                def one(head):
                    group = lax.div(head, GROUP)
                    head_rows = pl.ds(pl.multiple_of(group * HEAD_WIDTH, HEAD_WIDTH), HEAD_WIDTH)
                    place = pl.ds(pl.multiple_of(head * HEAD_WIDTH, HEAD_WIDTH), HEAD_WIDTH)
                    score = (
                        jnp.dot(
                            keys[group, 0:span, :],
                            query_t[place, cols],
                            preferred_element_type=F32,
                        )
                        + bias[0:span, :]
                    )
                    top = jnp.max(score, axis=0, keepdims=True)
                    weight = jnp.exp(score - top)
                    total = jnp.sum(weight, axis=0, keepdims=True)
                    out = jnp.dot(
                        values_t[head_rows, 0:span],
                        weight.astype(BF),
                        preferred_element_type=F32,
                    )
                    mixed_t[place, cols] = (out / total).astype(BF)
                    lse[head, :, cols] = jnp.broadcast_to(top + jnp.log(total), (8, step))

                def several(index, carry):
                    for extra in range(HEADS_PER_STEP):
                        one(index * HEADS_PER_STEP + extra)
                    return carry

                lax.fori_loop(0, QUERY_HEADS // HEADS_PER_STEP, several, 0)


def attention_forward(half, doc_row, doc_col, query_t, own, other):
    width, token_count = query_t.shape
    kv = KEY_VALUE_HEADS * HEAD_WIDTH
    vmem = pl.BlockSpec(memory_space=pltpu.VMEM)
    return pl.pallas_call(
        attention_forward_body,
        out_shape=(
            jax.ShapeDtypeStruct((width, token_count), BF),
            jax.ShapeDtypeStruct((QUERY_HEADS, 8, token_count), F32),
        ),
        in_specs=[pl.BlockSpec(memory_space=pltpu.SMEM)] + [vmem] * 5,
        out_specs=(vmem, vmem),
        scratch_shapes=[
            pltpu.VMEM((kv, 2 * token_count), BF),
            pltpu.VMEM((KEY_VALUE_HEADS, 2 * token_count, HEAD_WIDTH), BF),
            pltpu.VMEM((kv, 2 * token_count), BF),
            pltpu.VMEM((2 * token_count, token_count // 2), F32),
        ],
        cost_estimate=pl.CostEstimate(
            flops=int(15e9), bytes_accessed=4 * width * token_count, transcendentals=0
        ),
        name="attention_forward",
    )(half, doc_row, doc_col, query_t, own, other)


def attention_backward_body(
    half_ref,
    doc_row,
    doc_col,
    query_t,
    own,
    other,
    grad_t,
    lse,
    grad_query_t,
    own_sums,
    other_sums,
    grad_key,
    grad_value,
    keys_t,
    keys,
    values_t,
    values,
    bias,
):
    token_count = query_t.shape[1]
    step = token_count // 2
    grad_key[...] = jnp.zeros_like(grad_key)
    grad_value[...] = jnp.zeros_like(grad_value)
    for half in (0, 1):

        @pl.when(half_ref[0] == half)
        def _():
            load_keys(half, own, other, keys_t, keys, values_t, values)
            for block in (0, 1):
                span = half * token_count + (block + 1) * step
                start = half * token_count + block * step
                cols = slice(block * step, (block + 1) * step)
                fill_bias(bias, doc_row, doc_col, start, step, span)

                def one(head):
                    group = lax.div(head, GROUP)
                    head_rows = pl.ds(pl.multiple_of(group * HEAD_WIDTH, HEAD_WIDTH), HEAD_WIDTH)
                    place = pl.ds(pl.multiple_of(head * HEAD_WIDTH, HEAD_WIDTH), HEAD_WIDTH)
                    query = query_t[place, cols]
                    grad = grad_t[place, cols]
                    score = (
                        jnp.dot(keys[group, 0:span, :], query, preferred_element_type=F32)
                        + bias[0:span, :]
                    )
                    prob = jnp.exp(score - lse[head, 0:1, cols])
                    grad_prob = jnp.dot(values[group, 0:span, :], grad, preferred_element_type=F32)
                    delta = jnp.sum(prob * grad_prob, axis=0, keepdims=True)
                    grad_score = (prob * (grad_prob - delta)).astype(BF)
                    grad_value[group, 0:span, :] += dot(prob.astype(BF), grad, 1, 1)
                    grad_key[group, 0:span, :] += dot(grad_score, query, 1, 1)
                    grad_query_t[place, cols] = (
                        jnp.dot(keys_t[head_rows, 0:span], grad_score, preferred_element_type=F32)
                        * (HEAD_WIDTH ** (-0.5))
                    ).astype(BF)

                def several(index, carry):
                    for extra in range(HEADS_PER_STEP):
                        one(index * HEADS_PER_STEP + extra)
                    return carry

                lax.fori_loop(0, QUERY_HEADS // HEADS_PER_STEP, several, 0)

            for head in range(2 * KEY_VALUE_HEADS):
                source = (grad_key, grad_value)[head // KEY_VALUE_HEADS]
                rows = slice(head * HEAD_WIDTH, (head + 1) * HEAD_WIDTH)
                first = source[head % KEY_VALUE_HEADS, 0:token_count, :].T
                if half == 0:
                    own_sums[rows, :] = first
                    other_sums[rows, :] = jnp.zeros_like(first)
                else:
                    own_sums[rows, :] = source[head % KEY_VALUE_HEADS, token_count:, :].T
                    other_sums[rows, :] = first


def attention_backward(half, doc_row, doc_col, query_t, own, other, grad_t, lse):
    width, token_count = query_t.shape
    kv = KEY_VALUE_HEADS * HEAD_WIDTH
    vmem = pl.BlockSpec(memory_space=pltpu.VMEM)
    sums = jax.ShapeDtypeStruct((2 * kv, token_count), F32)
    totals = pltpu.VMEM((KEY_VALUE_HEADS, 2 * token_count, HEAD_WIDTH), F32)
    return pl.pallas_call(
        attention_backward_body,
        out_shape=(jax.ShapeDtypeStruct((width, token_count), BF), sums, sums),
        in_specs=[pl.BlockSpec(memory_space=pltpu.SMEM)] + [vmem] * 7,
        out_specs=(vmem, vmem, vmem),
        scratch_shapes=[
            totals,
            totals,
            pltpu.VMEM((kv, 2 * token_count), BF),
            pltpu.VMEM((KEY_VALUE_HEADS, 2 * token_count, HEAD_WIDTH), BF),
            pltpu.VMEM((kv, 2 * token_count), BF),
            pltpu.VMEM((KEY_VALUE_HEADS, 2 * token_count, HEAD_WIDTH), BF),
            pltpu.VMEM((2 * token_count, token_count // 2), F32),
        ],
        cost_estimate=pl.CostEstimate(
            flops=int(35e9), bytes_accessed=8 * width * token_count, transcendentals=0
        ),
        name="attention_backward",
    )(half, doc_row, doc_col, query_t, own, other, grad_t, lse)


def rope_tables(half, token_count):
    half_dim = HEAD_WIDTH // 2
    frequency = THETA ** (-(jnp.arange(half_dim, dtype=F32) * 2.0) / HEAD_WIDTH)
    positions = half * token_count + jnp.arange(token_count, dtype=jnp.int32)
    angles = frequency[:, None] * positions.astype(F32)[None, :]
    return jnp.cos(angles), jnp.sin(angles)


def rotate(values_t, cosine, sine):
    rows, count = values_t.shape
    split = values_t.reshape(rows // HEAD_WIDTH, 2, HEAD_WIDTH // 2, count)
    first, second = split[:, 0], split[:, 1]
    return jnp.stack(
        [first * cosine - second * sine, second * cosine + first * sine], 1
    ).reshape(rows, count)


class Mesh:
    def __init__(self):
        self.shards = lax.axis_size("shard")
        self.ctxs = lax.axis_size("ctx")
        self.tps = lax.axis_size("tp")
        self.fast = (self.shards, self.ctxs, self.tps) == (4, 2, 4)
        self.z = lax.axis_index("shard")
        self.c = lax.axis_index("ctx")
        self.t = lax.axis_index("tp")

    def across(self, value):
        pairs = [(i, self.ctxs - 1 - i) for i in range(self.ctxs)]
        return lax.ppermute(value, "ctx", pairs)

    def side(self, value, which):
        return lax.ppermute(value, "tp", [(i, i ^ which) for i in range(self.tps)])

    def ring(self, value, which):
        return lax.ppermute(value, "shard", [(i, i ^ which) for i in range(self.shards)])

    def place(self):
        return jnp.stack([self.z, self.c, self.t]).astype(jnp.int32)

    def gather_rows(self, block):
        return lax.all_gather(block, ("shard", "ctx"), axis=0)

    def gather_spread(self, block):
        rows, _ = block.shape
        part = rows // self.tps
        quarter = lax.dynamic_slice_in_dim(block, self.t * part, part, 0)
        pieces = [block]
        pieces += [self.ring(quarter, which) for which in (1, 2, 3)]
        far = jnp.concatenate(pieces[1:], 0)
        sides = [self.side(far, which) for which in (1, 2, 3)]
        mine = [block, far] + sides
        theirs = [self.across(piece) for piece in mine]
        return far, sides, mine, theirs

    def gather_line(self, block, later):
        two = self.ring(block, 2)
        one = self.ring(block, 1)
        late, relayed, later = lax.optimization_barrier((block, two, later))
        middle = lax.ppermute(late, "shard", [(1, 2), (2, 1)])
        ends = lax.ppermute(relayed, "shard", [(2, 3), (1, 0)])
        three = jnp.where((self.z == 1) | (self.z == 2), middle, ends)
        return [block, one, two, three]

    def reduce_rows(self, send, keep):
        mine, *quarters = fold(self.place(), keep, self.across(send))
        for which, quarter in enumerate(quarters, 1):
            mine = mine + self.side(quarter, which).astype(F32)
        total = lax.dynamic_index_in_dim(mine, self.z, 0, False)
        for which in (3, 2, 1):
            piece = lax.dynamic_index_in_dim(mine, self.z ^ which, 0, False).astype(BF)
            total = total + self.ring(piece, which).astype(F32)
        low = total.astype(BF)
        one, two, three = (self.side(low, which) for which in (1, 2, 3))
        odd = (self.t & 1) == 1
        a, b = jnp.where(odd, one, low), jnp.where(odd, low, one)
        c, d = jnp.where(odd, three, two), jnp.where(odd, two, three)
        far = self.t >= 2
        return jnp.concatenate(
            [
                jnp.where(far, c, a),
                jnp.where(far, d, b),
                jnp.where(far, a, c),
                jnp.where(far, b, d),
            ],
            0,
        ).astype(F32)

    def gather_tokens(self, rows):
        if not self.fast:
            every = lax.all_gather(rows, "tp", axis=0)
            return [
                lax.dynamic_index_in_dim(every, (self.t + i) % self.tps, 0, False)
                for i in range(self.tps)
            ]
        one = self.side(rows, 1)
        two = self.side(rows, 2)
        late, one, two = lax.optimization_barrier((rows, one, two))
        return [rows, one, two, self.side(late, 3)]

    def scatter_tokens(self, parts):
        if not self.fast:
            every = jnp.stack(parts)
            ordered = jnp.stack(
                [
                    lax.dynamic_index_in_dim(every, (i - self.t) % self.tps, 0, False)
                    for i in range(self.tps)
                ]
            )
            return lax.psum_scatter(ordered, "tp", scatter_dimension=0, tiled=False)
        return sum(piece.astype(F32) for piece in self.exchange_tokens(parts))

    def exchange_tokens(self, parts):
        return parts[:1] + [self.side(parts[which], which) for which in (1, 2, 3)]

    def scatter_line(self, send, keep):
        pieces = fold_line(self.place(), keep, self.across(send))
        total = pieces[0]
        for which in (2, 3, 1):
            total = total + self.ring(pieces[which], which).astype(F32)
        return total


def root_inverse(x):
    return lax.rsqrt(jnp.mean(x * x, -1, keepdims=True) + EPSILON)


def project_body(place, *refs):
    mine, theirs = refs[0:5], refs[5:10]
    tokens, cosine, sine, weight, out_weight, query_t, own, gain_one, gain_two = refs[10:19]
    small, fused = refs[19:]
    width, fused_width = weight.shape
    rows = width // 8
    part = mine[0].shape[0] // 4
    z, c, t = place[0], place[1], place[2]
    for block in range(8):
        shard, core = block // 2, block % 2
        for side in range(4):
            first = side * part
            count = min(part, rows - first)

            def put(pieces, index, start):
                value = pieces[index][pl.ds(start, part), :]
                place_rows = slice(block * rows + first, block * rows + first + count)
                weight[place_rows, :] = value[:count, :fused_width]
                out_weight[place_rows, :] = value[:count, fused_width:]
                if count < part:
                    small[block, :, :] = value[count:, 0:128]

            start = pl.multiple_of(jnp.maximum((shard ^ z) - 1, 0) * part, 16)
            for pieces, owned in ((mine, core == c), (theirs, core != c)):

                @pl.when(owned & (shard == z))
                def _():
                    put(pieces, 0, first)

                for which in range(4):

                    @pl.when(owned & (shard != z) & ((side ^ t) == which))
                    def _():
                        put(pieces, 1 + which, start)

    long = jnp.zeros((16, 1024), F32)
    short = jnp.zeros((16, 128), F32)
    for block in range(8):
        piece = small[block].astype(F32)
        wide = jnp.concatenate([piece, jnp.zeros((16, 896), F32)], 1)
        long = long + (pltpu.roll(wide, rows * block, 1) if block else wide)
        short = short + (pltpu.roll(piece, 16 * block, 1) if block else piece)
    bias = jnp.concatenate([long[0:1, :width], short[1:2], short[2:3]], 1)
    gain = long[3:4, :width]
    gain_one[...] = gain
    gain_two[...] = long[4:5, :width]
    x = tokens[...].astype(F32)
    normed = (x * root_inverse(x) * gain).astype(BF)
    fused[...] = (jnp.dot(normed, weight[...], preferred_element_type=F32) + bias).T
    half_dim = HEAD_WIDTH // 2
    query_width = QUERY_HEADS * HEAD_WIDTH
    kv = KEY_VALUE_HEADS * HEAD_WIDTH
    for head in range(QUERY_HEADS + KEY_VALUE_HEADS):
        start = head * HEAD_WIDTH
        one = fused[start : start + half_dim, :]
        two = fused[start + half_dim : start + HEAD_WIDTH, :]
        low = (one * cosine[...] - two * sine[...]).astype(BF)
        high = (two * cosine[...] + one * sine[...]).astype(BF)
        if head < QUERY_HEADS:
            scale = HEAD_WIDTH ** (-0.5)
            query_t[start : start + half_dim, :] = low * BF(scale)
            query_t[start + half_dim : start + HEAD_WIDTH, :] = high * BF(scale)
        else:
            start -= query_width
            own[start : start + half_dim, :] = low
            own[start + half_dim : start + HEAD_WIDTH, :] = high
    own[kv:, :] = fused[query_width + kv :, :].astype(BF)


def project(place, mine, theirs, tokens, cosine, sine, fused_width):
    token_count, width = tokens.shape
    vmem = pl.BlockSpec(memory_space=pltpu.VMEM)
    kv = KEY_VALUE_HEADS * HEAD_WIDTH
    row = jax.ShapeDtypeStruct((1, width), F32)
    return pl.pallas_call(
        project_body,
        out_shape=(
            jax.ShapeDtypeStruct((width, fused_width), BF),
            jax.ShapeDtypeStruct((width, width), BF),
            jax.ShapeDtypeStruct((QUERY_HEADS * HEAD_WIDTH, token_count), BF),
            jax.ShapeDtypeStruct((2 * kv, token_count), BF),
            row,
            row,
        ),
        in_specs=[pl.BlockSpec(memory_space=pltpu.SMEM)] + [vmem] * 13,
        out_specs=(vmem,) * 6,
        scratch_shapes=[
            pltpu.VMEM((8, 16, 128), BF),
            pltpu.VMEM((fused_width, token_count), F32),
        ],
        cost_estimate=pl.CostEstimate(
            flops=int(3e9), bytes_accessed=int(12e6), transcendentals=0
        ),
        name="project",
    )(place, *mine, *theirs, tokens, cosine, sine)


def output_body(tokens, mixed_t, weight, gain, hidden, normed):
    value = tokens[...].astype(F32) + jnp.dot(
        mixed_t[...].T, weight[...], preferred_element_type=F32
    )
    hidden[...] = value
    normed[...] = (value * root_inverse(value) * gain[...]).astype(BF)


def output_projection(tokens, mixed_t, weight, gain):
    vmem = pl.BlockSpec(memory_space=pltpu.VMEM)
    return pl.pallas_call(
        output_body,
        out_shape=(
            jax.ShapeDtypeStruct(tokens.shape, F32),
            jax.ShapeDtypeStruct(tokens.shape, BF),
        ),
        in_specs=[vmem] * 4,
        out_specs=(vmem, vmem),
        cost_estimate=pl.CostEstimate(
            flops=int(1e9), bytes_accessed=int(6e6), transcendentals=0
        ),
        name="output_projection",
    )(tokens, mixed_t, weight, gain)


def middle_body(
    own, one, two, three, hidden, cotangent, weight, gain, grad_hidden, grad_mixed_t, grad_gain
):
    total = own[...].astype(F32) + one[...].astype(F32)
    total = total + two[...].astype(F32) + three[...].astype(F32)
    h = hidden[...]
    inv = root_inverse(h)
    scaled = total * gain[...]
    mean = jnp.mean(scaled * h, -1, keepdims=True)
    value = cotangent[...].astype(F32) + inv * scaled - h * (inv * inv * inv) * mean
    grad_hidden[...] = value
    grad_gain[...] = jnp.sum(total * h * inv, 0, keepdims=True)
    grad_mixed_t[...] = dot(weight[...], value.astype(BF), 1, 1).astype(BF)


def middle(parts, hidden, cotangent, weight, gain):
    vmem = pl.BlockSpec(memory_space=pltpu.VMEM)
    return pl.pallas_call(
        middle_body,
        out_shape=(
            jax.ShapeDtypeStruct(hidden.shape, F32),
            jax.ShapeDtypeStruct(hidden.shape[::-1], BF),
            jax.ShapeDtypeStruct(gain.shape, F32),
        ),
        in_specs=[vmem] * 8,
        out_specs=(vmem, vmem, vmem),
        cost_estimate=pl.CostEstimate(
            flops=int(1e9), bytes_accessed=int(9e6), transcendentals=0
        ),
        name="middle",
    )(*parts, hidden, cotangent, weight, gain)


def fold_body(place, keep, received, mine, *sends):
    part = mine.shape[1]
    for which, out in enumerate((mine,) + sends):
        rows = pl.ds(pl.multiple_of((place[2] ^ which) * part, 16), part)
        value = keep[0, rows, :].astype(F32) + received[0, rows, :].astype(F32)
        out[0] = value.astype(out.dtype)


def fold(place, keep, received):
    blocks, rows, cols = keep.shape
    part = rows // 4
    shape = (blocks, part, cols)
    return pl.pallas_call(
        fold_body,
        grid=(blocks,),
        out_shape=(jax.ShapeDtypeStruct(shape, F32),) + (jax.ShapeDtypeStruct(shape, BF),) * 3,
        in_specs=[pl.BlockSpec(memory_space=pltpu.SMEM)]
        + [pl.BlockSpec((1, rows, cols), lambda i: (i, 0, 0))] * 2,
        out_specs=(pl.BlockSpec((1, part, cols), lambda i: (i, 0, 0)),) * 4,
        cost_estimate=pl.CostEstimate(
            flops=0, bytes_accessed=6 * blocks * rows * cols, transcendentals=0
        ),
        name="fold",
    )(place, keep, received)


def fold_line_body(place, keep, received, *outs):
    for which, out in enumerate(outs):

        @pl.when(pl.program_id(0) == which)
        def _():
            value = keep[0].astype(F32) + received[0].astype(F32)
            out[...] = value.astype(out.dtype)


def fold_line(place, keep, received):
    shape = keep.shape[1:]
    block = pl.BlockSpec((1,) + shape, lambda i, place: (i ^ place[0], 0, 0, 0))
    out = pl.BlockSpec(shape, lambda i, place: (0, 0, 0))
    return pl.pallas_call(
        fold_line_body,
        out_shape=(jax.ShapeDtypeStruct(shape, F32),) + (jax.ShapeDtypeStruct(shape, BF),) * 3,
        grid_spec=pltpu.PrefetchScalarGridSpec(
            num_scalar_prefetch=1, grid=(4,), in_specs=[block] * 2, out_specs=(out,) * 4
        ),
        cost_estimate=pl.CostEstimate(
            flops=0, bytes_accessed=6 * keep.size, transcendentals=0
        ),
        name="fold_line",
    )(place, keep, received)


def assemble_line_body(place, *refs):
    mine, theirs, out = refs[0:4], refs[4:8], refs[8]
    rows = mine[0].shape[0]
    z, c = place[0], place[1]
    for here in range(4):

        @pl.when(z == here)
        def _():
            for block in range(8):
                shard, core = block // 2, block % 2
                left, right = mine[shard ^ here], theirs[shard ^ here]
                out[0, block * rows : (block + 1) * rows, :] = jnp.where(
                    core == c, left[...], right[...]
                )


def assemble_line(place, mine, theirs, count):
    rows, cols = mine[0].shape
    rows = rows // count
    part = pl.BlockSpec((rows, cols), lambda i: (i, 0))
    return pl.pallas_call(
        assemble_line_body,
        grid=(count,),
        out_shape=jax.ShapeDtypeStruct((count, 8 * rows, cols), BF),
        in_specs=[pl.BlockSpec(memory_space=pltpu.SMEM)] + [part] * 8,
        out_specs=pl.BlockSpec((1, 8 * rows, cols), lambda i: (i, 0, 0)),
        cost_estimate=pl.CostEstimate(
            flops=0, bytes_accessed=32 * rows * cols * count, transcendentals=0
        ),
        name="assemble_line",
    )(place, *mine, *theirs)


def projection_gradients_body(
    place,
    grad_query,
    own_sums,
    other_sums,
    cosine,
    sine,
    tokens,
    gain,
    second_gain,
    grad_hidden,
    mixed_t,
    weight,
    grad_tokens,
    send,
    keep,
    fused,
):
    half_dim = HEAD_WIDTH // 2
    query_width, kv = grad_query.shape[0], own_sums.shape[0] // 2
    rows = keep.shape[1] - 16

    def unrotate(value, start):
        first, second = value[:half_dim], value[half_dim:]
        fused[start : start + half_dim, :] = first * cosine[...] + second * sine[...]
        fused[start + half_dim : start + HEAD_WIDTH, :] = (
            second * cosine[...] - first * sine[...]
        )

    for head in range(QUERY_HEADS):
        start = head * HEAD_WIDTH
        unrotate(grad_query[start : start + HEAD_WIDTH, :].astype(F32), start)
    sums = (own_sums[...] + other_sums[...]).astype(BF).astype(F32)
    for head in range(KEY_VALUE_HEADS):
        start = head * HEAD_WIDTH
        unrotate(sums[start : start + HEAD_WIDTH], query_width + start)
    fused[query_width + kv :, :] = sums[kv:]

    exact = fused[...]
    low = exact.astype(BF)
    rest = (exact - low.astype(F32)).astype(BF)
    ones = jnp.ones((16, exact.shape[1]), BF)
    bias = dot(ones, low, 1, 1) + dot(ones, rest, 1, 1)
    low_rows = low.T
    x = tokens[...].astype(F32)
    inv = root_inverse(x)
    normed_t = (x * inv * gain[...]).astype(BF).T
    grad_normed = dot(low_rows, weight[...], 1, 1)
    scaled = grad_normed * gain[...]
    mean = jnp.mean(scaled * x, -1, keepdims=True)
    hidden = grad_hidden[...]
    grad_tokens[...] = (hidden + inv * scaled - x * (inv * inv * inv) * mean).astype(BF)
    grad_gain = jnp.sum(grad_normed * x * inv, 0, keepdims=True)
    left = jnp.dot(normed_t, low_rows, preferred_element_type=F32).astype(BF)
    right = jnp.dot(
        mixed_t[...], hidden.astype(BF), preferred_element_type=F32
    ).astype(BF)
    split = left.shape[1]
    first_row = jnp.concatenate(
        [bias[:8], jnp.broadcast_to(grad_gain, (8, grad_gain.shape[1]))], 1
    )
    second_row = jnp.concatenate(
        [
            jnp.broadcast_to(second_gain[...], (8, second_gain.shape[1])),
            jnp.zeros((8, split), F32),
        ],
        1,
    )
    index = lax.broadcasted_iota(jnp.int32, first_row.shape, 0)
    small = jnp.where(index == 0, first_row, jnp.where(index == 1, second_row, 0.0))
    small = jnp.concatenate([small, jnp.zeros_like(small)], 0).astype(BF)
    for block in range(8):
        shard, core = block // 2, block % 2
        part = slice(block * rows, (block + 1) * rows)
        for out, owned in ((keep, place[1] == core), (send, place[1] != core)):

            @pl.when(owned)
            def _():
                out[shard, 0:rows, 0:split] = left[part]
                out[shard, 0:rows, split:] = right[part]
                out[shard, rows:, :] = small


def projection_gradients(place, *arrays):
    tokens, weight = arrays[5], arrays[10]
    token_count, width = tokens.shape
    fused_width = weight.shape[1]
    half = jax.ShapeDtypeStruct((4, width // 8 + 16, fused_width + width), BF)
    whole = [
        pl.BlockSpec(array.shape, lambda i, n=array.ndim: (0,) * n) for array in arrays
    ]
    return pl.pallas_call(
        projection_gradients_body,
        grid=(1,),
        out_shape=(jax.ShapeDtypeStruct(tokens.shape, BF), half, half),
        in_specs=[pl.BlockSpec(memory_space=pltpu.SMEM)]
        + whole,
        out_specs=(
            pl.BlockSpec(tokens.shape, lambda i: (0, 0)),
            pl.BlockSpec(half.shape, lambda i: (0, 0, 0)),
            pl.BlockSpec(half.shape, lambda i: (0, 0, 0)),
        ),
        scratch_shapes=[pltpu.VMEM((fused_width, token_count), F32)],
        cost_estimate=pl.CostEstimate(
            flops=int(6e9), bytes_accessed=int(16e6), transcendentals=0
        ),
        name="projection_gradients",
    )(place, *arrays)


def mlp_body(chunks, *refs):
    xs, gs = refs[:chunks], refs[chunks : 2 * chunks]
    gate_ref, up_ref, down_ref = refs[2 * chunks : 2 * chunks + 3]
    backs, downs = refs[-2 - 2 * chunks : -2 - chunks], refs[-2 - chunks : -2]
    units, rows_t = refs[-2:]
    x, g = xs[0][...], gs[0][...]
    first = True
    if chunks == 2:
        first = pl.program_id(0) < pl.num_programs(0) // 2
        x, g = jnp.where(first, x, xs[1][...]), jnp.where(first, g, gs[1][...])
    gate = jnp.dot(x, gate_ref[...], preferred_element_type=F32)
    up = jnp.dot(x, up_ref[...], preferred_element_type=F32)
    sig = 1.0 / (1.0 + jnp.exp(-gate))
    silu = gate * sig
    act = (silu * up).astype(BF)
    grad_act = jnp.dot(g, down_ref[...], preferred_element_type=F32)
    grad_gate = (grad_act * up * sig * (1.0 + gate * (1.0 - sig))).astype(BF)
    grad_up = (grad_act * silu).astype(BF)
    back = (dot(grad_gate, gate_ref[...], 1, 1) + dot(grad_up, up_ref[...], 1, 1)).astype(BF)
    down = dot(act, down_ref[...], 1, 1).astype(BF)
    if chunks == 1:
        backs[0][...] = back
        downs[0][...] = down
    else:
        for index, chosen in enumerate((first, jnp.logical_not(first))):

            @pl.when(chosen)
            def _():
                backs[index][...] = back
                downs[index][...] = down

    units[0] = grad_gate
    units[1] = grad_up
    units[2] = act
    rows_t[0] = x.T
    rows_t[1] = g.T


def mlp(xs, gs, weights, kept, first, total):
    chunks = len(xs)
    count, width = xs[0].shape
    units = weights.shape[2]
    step = min(256, count)
    steps = count // step
    offset = first // step
    rows = [
        pl.BlockSpec((step, width), lambda i, n=n: (jnp.clip(i - n * steps, 0, steps - 1), 0))
        for n in range(chunks)
    ]
    whole = [
        pl.BlockSpec(
            (pl.Squeezed(), width, units), lambda i, n=n: (n, 0, 0), pipeline_mode=pl.Buffered(1)
        )
        for n in range(3)
    ]
    partial = jax.ShapeDtypeStruct((count, width), BF)
    kept = list(kept)
    outs = pl.pallas_call(
        functools.partial(mlp_body, chunks),
        grid=(chunks * steps,),
        out_shape=[partial] * (2 * chunks)
        + [
            jax.ShapeDtypeStruct((3, total, units), BF),
            jax.ShapeDtypeStruct((2, width, total), BF),
        ],
        in_specs=rows + rows + whole + [pl.BlockSpec(memory_space=pl.ANY)] * len(kept),
        out_specs=rows
        + rows
        + [
            pl.BlockSpec((3, step, units), lambda i: (0, i + offset, 0)),
            pl.BlockSpec((2, width, step), lambda i: (0, 0, i + offset)),
        ],
        input_output_aliases={2 * chunks + 3 + i: 2 * chunks + i for i in range(len(kept))},
        cost_estimate=pl.CostEstimate(
            flops=12 * chunks * count * width * units,
            bytes_accessed=6 * width * units + 8 * chunks * count * (width + units),
            transcendentals=chunks * count * units,
        ),
        name="mlp",
    )(*xs, *gs, weights, weights, weights, *kept)
    return list(outs[:chunks]), list(outs[chunks : 2 * chunks]), outs[2 * chunks :]


def weight_gradients_body(place, left, right, send, keep, total):
    index, last = pl.program_id(1), pl.num_programs(1) - 1
    rows = send.shape[2]
    value = jnp.dot(left[0], right[0], preferred_element_type=F32)

    @pl.when(index == 0)
    def _():
        total[...] = value

    @pl.when(index > 0)
    def _():
        total[...] += value

    @pl.when(index == last)
    def _():
        for block in range(8):
            shard, core = block // 2, block % 2
            piece = total[block * rows : (block + 1) * rows, :].astype(BF)

            @pl.when(place[1] == core)
            def _():
                keep[shard, 0] = piece

            @pl.when(place[1] != core)
            def _():
                send[shard, 0] = piece


def weight_gradients(place, units, rows_t):
    _, total, wide = units.shape
    width = rows_t.shape[1]
    step = total // 2
    half = jax.ShapeDtypeStruct((4, 3, width // 8, wide), BF)
    out = pl.BlockSpec((4, 1, width // 8, wide), lambda w, k: (0, w, 0, 0))
    return pl.pallas_call(
        weight_gradients_body,
        grid=(3, 2),
        out_shape=(half, half),
        in_specs=[
            pl.BlockSpec(memory_space=pltpu.SMEM),
            pl.BlockSpec((1, width, step), lambda w, k: (w // 2, 0, k)),
            pl.BlockSpec((1, step, wide), lambda w, k: (w, k, 0)),
        ],
        out_specs=(out, out),
        scratch_shapes=[pltpu.VMEM((width, wide), F32)],
        cost_estimate=pl.CostEstimate(
            flops=6 * total * width * wide,
            bytes_accessed=6 * total * (width + wide),
            transcendentals=0,
        ),
        name="weight_gradients",
    )(place, rows_t, units)


def per_device(
    tokens,
    doc_ids,
    w_query,
    b_query,
    key_projection,
    key_bias_vector,
    value_projection,
    value_bias_vector,
    w_output,
    gain_attn,
    gain_mlp,
    w_gate,
    w_up,
    w_down,
    cotangent,
):
    mesh = Mesh()
    token_count, width = tokens.shape
    rows = w_query.shape[0]
    padded = (rows + 5 + 15) // 16 * 16
    query_width = QUERY_HEADS * HEAD_WIDTH
    kv_width = KEY_VALUE_HEADS * HEAD_WIDTH
    kv_rows = key_bias_vector.shape[0]
    fused_width = query_width + 2 * kv_width
    blocks = mesh.shards * mesh.ctxs

    all_width = fused_width + width
    small_vectors = [b_query, key_bias_vector, value_bias_vector, gain_attn, gain_mlp]
    small_counts = [vector.shape[0] for vector in small_vectors]
    packed = jnp.concatenate(
        [jnp.concatenate([w_query, key_projection, value_projection, w_output], 1)]
        + [
            jnp.pad(vector[None], ((0, 0), (0, all_width - vector.shape[0])))
            for vector in small_vectors
        ]
        + [jnp.zeros((padded - rows - len(small_vectors), all_width), BF)],
        0,
    )
    if mesh.fast:
        _, sides, mine, theirs = mesh.gather_spread(packed)
        cosine, sine = rope_tables(mesh.c, token_count)
        fused_weight, output_weight, query_t, own, first_gain, second_gain = project(
            mesh.place(), mine, theirs, tokens, cosine, sine, fused_width
        )
        line = mesh.gather_line(jnp.concatenate([w_gate, w_up, w_down.T], 0), own)
        others = [mesh.across(part) for part in line]
        late, sides = lax.optimization_barrier((cotangent, sides))
        grad_parts = mesh.gather_tokens(late)
    else:
        gathered = lax.all_gather(packed, ("shard", "ctx"), axis=0)
        projection = gathered[:, :rows].reshape(width, all_width)
        smalls = gathered[:, rows:]
        weights = jnp.stack(
            [
                lax.all_gather(part, ("shard", "ctx"), axis=0, tiled=True)
                for part in (w_gate, w_up, w_down.T)
            ]
        )
        grad_parts = mesh.gather_tokens(cotangent)
        fused_weight = projection[:, :fused_width]
        output_weight = projection[:, fused_width:]
        bias_q, bias_k, bias_v, first_gain, second_gain = (
            smalls[:, i, :count].reshape(-1).astype(F32) for i, count in enumerate(small_counts)
        )
        fused_bias = jnp.concatenate([bias_q, bias_k, bias_v])
        tok_float = tokens.astype(F32)
        first_inv = root_inverse(tok_float)
        normed_attn = (tok_float * first_inv * first_gain).astype(BF)
        cosine, sine = rope_tables(mesh.c, token_count)
        fused_t = dot(fused_weight, normed_attn, 0, 1) + fused_bias[:, None]
        query_t = rotate(fused_t[:query_width], cosine, sine).astype(BF) * (HEAD_WIDTH ** (-0.5))
        key_t = rotate(fused_t[query_width : query_width + kv_width], cosine, sine).astype(BF)
        value_t = fused_t[query_width + kv_width :].astype(BF)
        own = jnp.concatenate([key_t, value_t], 0)
        first_gain, second_gain = first_gain[None], second_gain[None]
    other = mesh.across(own)
    half = mesh.c.astype(jnp.int32).reshape(1)
    doc_col = doc_ids.reshape(-1, 1)
    mixed_t, lse = attention_forward(half, doc_ids, doc_col, query_t, own, other)

    hidden, normed_mlp = output_projection(tokens, mixed_t, output_weight, second_gain)
    normed_parts = mesh.gather_tokens(normed_mlp)
    if mesh.fast:
        line, others, _ = lax.optimization_barrier((line, others, normed_mlp))
        weights = assemble_line(mesh.place(), line, others, 3)

    total = token_count * mesh.tps
    backs, downs, kept = [], [], []
    groups = ((0, 1), (1, 3), (3, 4)) if mesh.tps == 4 else ((i, i + 1) for i in range(mesh.tps))
    for index, (low, high) in enumerate(groups):
        some_backs, some_downs, kept = mlp(
            normed_parts[low:high],
            grad_parts[low:high],
            weights,
            kept,
            low * token_count,
            total,
        )
        backs += some_backs
        downs += some_downs
    units, rows_t = kept
    if mesh.fast:
        back_parts = mesh.exchange_tokens(backs)
    else:
        zero = jnp.zeros_like(tokens)
        back_parts = [mesh.scatter_tokens(backs).astype(BF), zero, zero, zero]
    if mesh.fast:
        send, keep = weight_gradients(mesh.place(), units, rows_t)
        part_gate, part_up, part_down = mesh.scatter_line(send, keep)
        downs, back_parts = lax.optimization_barrier((downs, back_parts))
    else:
        part_gate, part_up, part_down = (
            lax.psum_scatter(
                dot(rows_t[i // 2], units[i], 1, 0),
                ("shard", "ctx"),
                scatter_dimension=0,
                tiled=True,
            )
            for i in range(3)
        )
    part_down = part_down.T
    grad_hidden, grad_mixed_t, grad_second_gain = middle(
        back_parts, hidden, cotangent, output_weight, second_gain
    )
    grad_query_rot, own_sums, to_other = attention_backward(
        half, doc_ids, doc_col, query_t, own, other, grad_mixed_t, lse
    )
    hidden_late, grad_query_rot = lax.optimization_barrier((hidden, grad_query_rot))
    result = (hidden_late + mesh.scatter_tokens(downs).astype(F32)).astype(BF)
    received = mesh.across(to_other)
    if mesh.fast:
        grad_tokens, send, keep = projection_gradients(
            mesh.place(),
            grad_query_rot,
            own_sums,
            received,
            cosine,
            sine,
            tokens,
            first_gain,
            grad_second_gain,
            grad_hidden,
            mixed_t,
            fused_weight,
        )
        summed = mesh.reduce_rows(send, keep)
        index = mesh.z * mesh.ctxs + mesh.c

        def own_part(line, start, count):
            return lax.dynamic_slice_in_dim(line, start + index * count, count, 0)

        first, second = summed[rows], summed[rows + 1]
        sum_small = [
            own_part(first, 0, rows),
            own_part(first, query_width, kv_rows),
            own_part(first, query_width + kv_width, kv_rows),
            own_part(first, fused_width, rows),
            own_part(second, 0, rows),
        ]
        return (
            result,
            grad_tokens,
            summed[:rows, :query_width],
            sum_small[0],
            summed[:rows, query_width : query_width + kv_width],
            sum_small[1],
            summed[:rows, query_width + kv_width : fused_width],
            sum_small[2],
            summed[:rows, fused_width:],
            sum_small[3],
            sum_small[4],
            part_gate,
            part_up,
            part_down,
        )
    grad_output_weight = dot(mixed_t, grad_hidden.astype(BF), 1, 0)
    own_sums_t = (own_sums + received).astype(BF).astype(F32)
    grad_query_pre = rotate(grad_query_rot.astype(F32), cosine, -sine)
    grad_key_pre = rotate(own_sums_t[:kv_width], cosine, -sine)
    fused_grad_t = jnp.concatenate([grad_query_pre, grad_key_pre, own_sums_t[kv_width:]], 0)
    grad_fused_bias = jnp.sum(fused_grad_t, 1)
    fused_low = fused_grad_t.astype(BF)
    grad_normed_attn = dot(fused_low, fused_weight, 0, 1)
    grad_fused_weight = dot(normed_attn, fused_low, 0, 1)
    scaled_one = grad_normed_attn * first_gain
    grad_tokens = (
        grad_hidden
        + first_inv * scaled_one
        - tok_float * first_inv**3 * jnp.mean(scaled_one * tok_float, -1, keepdims=True)
    )
    grad_first_gain = jnp.sum(grad_normed_attn * tok_float * first_inv, 0)

    small_sums = [
        grad_fused_bias[:query_width],
        grad_fused_bias[query_width : query_width + kv_width],
        grad_fused_bias[query_width + kv_width :],
        grad_first_gain,
        grad_second_gain[0],
    ]
    grad_packed = jnp.concatenate(
        [
            jnp.concatenate([grad_fused_weight, grad_output_weight], 1).reshape(
                blocks, rows, all_width
            )
        ]
        + [
            jnp.pad(
                vector.reshape(blocks, 1, count), ((0, 0), (0, 0), (0, all_width - count))
            )
            for vector, count in zip(small_sums, small_counts)
        ]
        + [jnp.zeros((blocks, padded - rows - len(small_sums), all_width), F32)],
        1,
    )
    summed = lax.psum_scatter(grad_packed, ("shard", "ctx"), scatter_dimension=0, tiled=True)
    summed = lax.psum(summed[0], "tp")
    sum_small = [summed[rows + i, :count] for i, count in enumerate(small_counts)]
    return (
        result,
        grad_tokens.astype(BF),
        summed[:rows, :query_width],
        sum_small[0],
        summed[:rows, query_width : query_width + kv_width],
        sum_small[1],
        summed[:rows, query_width + kv_width : fused_width],
        sum_small[2],
        summed[:rows, fused_width:],
        sum_small[3],
        sum_small[4],
        part_gate,
        part_up,
        part_down,
    )


def solution(mesh):
    both = ("shard", "ctx")
    every = ("shard", "ctx", "tp")
    in_specs = (
        P(every, None),
        P(("shard", "tp"), None),
        P(both, None),
        P(both),
        P(both, None),
        P(both),
        P(both, None),
        P(both),
        P(both, None),
        P(both),
        P(both),
        P(both, "tp"),
        P(both, "tp"),
        P("tp", both),
        P(every, None),
    )
    out_specs = (
        P(every, None),
        P(every, None),
        P(both, None),
        P(both),
        P(both, None),
        P(both),
        P(both, None),
        P(both),
        P(both, None),
        P(both),
        P(both),
        P(both, "tp"),
        P(both, "tp"),
        P("tp", both),
    )

    step = jax.shard_map(
        per_device, mesh=mesh, in_specs=in_specs, out_specs=out_specs, check_vma=False
    )
    if tuple(mesh.shape[name] for name in every) != (4, 2, 4):
        return step
    return step
```

```python
import functools

import jax
import jax.numpy as jnp
from jax import lax
from jax.experimental import pallas as pl
from jax.experimental.pallas import tpu as pltpu
from jax.sharding import PartitionSpec as P


QUERY_HEADS = 14
KEY_VALUE_HEADS = 2
HEAD_WIDTH = 64
GROUP = QUERY_HEADS // KEY_VALUE_HEADS
HEADS_PER_STEP = 1

EPSILON = 1e-06
THETA = 1000000.0
NEGATIVE = -1e30
BF = jnp.bfloat16
F32 = jnp.float32


def dot(left, right, left_dim, right_dim, out=F32):
    return lax.dot_general(
        left, right, (((left_dim,), (right_dim,)), ((), ())), preferred_element_type=out
    )


def fill_bias(bias, doc_row, row_start, row_count, span):
    keys = lax.broadcasted_iota(jnp.int32, (span, row_count), 0)
    queries = lax.broadcasted_iota(jnp.int32, (span, row_count), 1) + row_start
    key_doc = jnp.broadcast_to(doc_row[:, 0:span], (8, span)).T[:, 0:1]
    query_doc = doc_row[:, row_start : row_start + row_count]
    same = (key_doc == query_doc) & (query_doc >= 0) & (keys <= queries)
    bias[0:span, :] = jnp.where(same | (keys == queries), 0.0, NEGATIVE)


def load_keys(half, own, other, keys_t, keys, values_t, values):
    width = KEY_VALUE_HEADS * HEAD_WIDTH
    parts = (own,) if half == 0 else (other, own)
    for place, part in enumerate(parts):
        count = part.shape[1]
        rows = slice(place * count, (place + 1) * count)
        key_t = part[0:width, :]
        value_t = part[width : 2 * width, :]
        keys_t[:, rows] = key_t
        values_t[:, rows] = value_t
        key = key_t.astype(F32).T.astype(BF)
        for head in range(KEY_VALUE_HEADS):
            lanes = slice(head * HEAD_WIDTH, (head + 1) * HEAD_WIDTH)
            keys[head, rows, :] = key[:, lanes]
        if values is not None:
            value = value_t.astype(F32).T.astype(BF)
            for head in range(KEY_VALUE_HEADS):
                lanes = slice(head * HEAD_WIDTH, (head + 1) * HEAD_WIDTH)
                values[head, rows, :] = value[:, lanes]


def attention_forward_body(
    half_ref,
    doc_row,
    query_t,
    own,
    other,
    mixed_t,
    exact_t,
    lse,
    keys_t,
    keys,
    values_t,
    bias,
):
    token_count = query_t.shape[1]
    step = token_count // 2
    for half in (0, 1):

        @pl.when(half_ref[0] == half)
        def _():
            load_keys(half, own, other, keys_t, keys, values_t, None)
            for block in (0, 1):
                span = half * token_count + (block + 1) * step
                start = half * token_count + block * step
                cols = slice(block * step, (block + 1) * step)
                fill_bias(bias, doc_row, start, step, span)

                def one(head):
                    group = lax.div(head, GROUP)
                    head_rows = pl.ds(pl.multiple_of(group * HEAD_WIDTH, HEAD_WIDTH), HEAD_WIDTH)
                    place = pl.ds(pl.multiple_of(head * HEAD_WIDTH, HEAD_WIDTH), HEAD_WIDTH)
                    score = (
                        jnp.dot(
                            keys[group, 0:span, :],
                            query_t[place, cols],
                            preferred_element_type=F32,
                        )
                        + bias[0:span, :]
                    )
                    top = jnp.max(score, axis=0, keepdims=True)
                    weight = jnp.exp(score - top)
                    total = jnp.sum(weight, axis=0, keepdims=True)
                    out = jnp.dot(
                        values_t[head_rows, 0:span],
                        weight.astype(BF),
                        preferred_element_type=F32,
                    )
                    out = out / total
                    exact_t[place, cols] = out
                    mixed_t[place, cols] = out.astype(BF)
                    lse[head, :, cols] = jnp.broadcast_to(top + jnp.log(total), (8, step))

                def several(index, carry):
                    for extra in range(HEADS_PER_STEP):
                        one(index * HEADS_PER_STEP + extra)
                    return carry

                lax.fori_loop(0, QUERY_HEADS // HEADS_PER_STEP, several, 0)


def attention_forward(half, doc_row, query_t, own, other):
    width, token_count = query_t.shape
    kv = KEY_VALUE_HEADS * HEAD_WIDTH
    vmem = pl.BlockSpec(memory_space=pltpu.VMEM)
    return pl.pallas_call(
        attention_forward_body,
        out_shape=(
            jax.ShapeDtypeStruct((width, token_count), BF),
            jax.ShapeDtypeStruct((width, token_count), F32),
            jax.ShapeDtypeStruct((QUERY_HEADS, 8, token_count), F32),
        ),
        in_specs=[pl.BlockSpec(memory_space=pltpu.SMEM)] + [vmem] * 4,
        out_specs=(vmem, vmem, vmem),
        scratch_shapes=[
            pltpu.VMEM((kv, 2 * token_count), BF),
            pltpu.VMEM((KEY_VALUE_HEADS, 2 * token_count, HEAD_WIDTH), BF),
            pltpu.VMEM((kv, 2 * token_count), BF),
            pltpu.VMEM((2 * token_count, token_count // 2), F32),
        ],
        cost_estimate=pl.CostEstimate(
            flops=int(15e9), bytes_accessed=4 * width * token_count, transcendentals=0
        ),
        name="attention_forward",
    )(half, doc_row, query_t, own, other)


def attention_backward_body(
    half_ref,
    doc_row,
    query_t,
    own,
    other,
    grad_t,
    exact_t,
    lse,
    grad_query_t,
    own_sums,
    other_sums,
    grad_key,
    grad_value,
    keys_t,
    keys,
    values_t,
    values,
    bias,
):
    token_count = query_t.shape[1]
    step = token_count // 2
    grad_key[...] = jnp.zeros_like(grad_key)
    grad_value[...] = jnp.zeros_like(grad_value)
    for half in (0, 1):

        @pl.when(half_ref[0] == half)
        def _():
            load_keys(half, own, other, keys_t, keys, values_t, values)
            for block in (0, 1):
                span = half * token_count + (block + 1) * step
                start = half * token_count + block * step
                cols = slice(block * step, (block + 1) * step)
                fill_bias(bias, doc_row, start, step, span)

                def one(head):
                    group = lax.div(head, GROUP)
                    head_rows = pl.ds(pl.multiple_of(group * HEAD_WIDTH, HEAD_WIDTH), HEAD_WIDTH)
                    place = pl.ds(pl.multiple_of(head * HEAD_WIDTH, HEAD_WIDTH), HEAD_WIDTH)
                    query = query_t[place, cols]
                    grad = grad_t[place, cols]
                    score = (
                        jnp.dot(keys[group, 0:span, :], query, preferred_element_type=F32)
                        + bias[0:span, :]
                    )
                    prob = jnp.exp(score - lse[head, 0:1, cols])
                    grad_prob = jnp.dot(values[group, 0:span, :], grad, preferred_element_type=F32)
                    delta = jnp.sum(grad.astype(F32) * exact_t[place, cols], axis=0, keepdims=True)
                    grad_score = (prob * (grad_prob - delta)).astype(BF)
                    grad_value[group, 0:span, :] += dot(prob.astype(BF), grad, 1, 1)
                    grad_key[group, 0:span, :] += dot(grad_score, query, 1, 1)
                    grad_query_t[place, cols] = (
                        jnp.dot(keys_t[head_rows, 0:span], grad_score, preferred_element_type=F32)
                        * (HEAD_WIDTH ** (-0.5))
                    ).astype(BF)

                def several(index, carry):
                    for extra in range(HEADS_PER_STEP):
                        one(index * HEADS_PER_STEP + extra)
                    return carry

                lax.fori_loop(0, QUERY_HEADS // HEADS_PER_STEP, several, 0)

            for head in range(2 * KEY_VALUE_HEADS):
                source = (grad_key, grad_value)[head // KEY_VALUE_HEADS]
                rows = slice(head * HEAD_WIDTH, (head + 1) * HEAD_WIDTH)
                first = source[head % KEY_VALUE_HEADS, 0:token_count, :].T
                if half == 0:
                    own_sums[rows, :] = first
                    other_sums[rows, :] = jnp.zeros_like(first)
                else:
                    own_sums[rows, :] = source[head % KEY_VALUE_HEADS, token_count:, :].T
                    other_sums[rows, :] = first


def attention_backward(half, doc_row, query_t, own, other, grad_t, exact_t, lse):
    width, token_count = query_t.shape
    kv = KEY_VALUE_HEADS * HEAD_WIDTH
    vmem = pl.BlockSpec(memory_space=pltpu.VMEM)
    sums = jax.ShapeDtypeStruct((2 * kv, token_count), F32)
    totals = pltpu.VMEM((KEY_VALUE_HEADS, 2 * token_count, HEAD_WIDTH), F32)
    return pl.pallas_call(
        attention_backward_body,
        out_shape=(jax.ShapeDtypeStruct((width, token_count), BF), sums, sums),
        in_specs=[pl.BlockSpec(memory_space=pltpu.SMEM)] + [vmem] * 7,
        out_specs=(vmem, vmem, vmem),
        scratch_shapes=[
            totals,
            totals,
            pltpu.VMEM((kv, 2 * token_count), BF),
            pltpu.VMEM((KEY_VALUE_HEADS, 2 * token_count, HEAD_WIDTH), BF),
            pltpu.VMEM((kv, 2 * token_count), BF),
            pltpu.VMEM((KEY_VALUE_HEADS, 2 * token_count, HEAD_WIDTH), BF),
            pltpu.VMEM((2 * token_count, token_count // 2), F32),
        ],
        cost_estimate=pl.CostEstimate(
            flops=int(35e9), bytes_accessed=8 * width * token_count, transcendentals=0
        ),
        name="attention_backward",
    )(half, doc_row, query_t, own, other, grad_t, exact_t, lse)


def rope_tables(half, token_count):
    half_dim = HEAD_WIDTH // 2
    frequency = THETA ** (-(jnp.arange(half_dim, dtype=F32) * 2.0) / HEAD_WIDTH)
    positions = half * token_count + jnp.arange(token_count, dtype=jnp.int32)
    angles = frequency[:, None] * positions.astype(F32)[None, :]
    return jnp.cos(angles), jnp.sin(angles)


def rotate(values_t, cosine, sine):
    rows, count = values_t.shape
    split = values_t.reshape(rows // HEAD_WIDTH, 2, HEAD_WIDTH // 2, count)
    first, second = split[:, 0], split[:, 1]
    return jnp.stack(
        [first * cosine - second * sine, second * cosine + first * sine], 1
    ).reshape(rows, count)


class Mesh:
    def __init__(self):
        self.shards = lax.axis_size("shard")
        self.ctxs = lax.axis_size("ctx")
        self.tps = lax.axis_size("tp")
        self.fast = (self.shards, self.ctxs, self.tps) == (4, 2, 4)
        self.z = lax.axis_index("shard")
        self.c = lax.axis_index("ctx")
        self.t = lax.axis_index("tp")

    def across(self, value):
        pairs = [(i, self.ctxs - 1 - i) for i in range(self.ctxs)]
        return lax.ppermute(value, "ctx", pairs)

    def side(self, value, which):
        return lax.ppermute(value, "tp", [(i, i ^ which) for i in range(self.tps)])

    def ring(self, value, which):
        return lax.ppermute(value, "shard", [(i, i ^ which) for i in range(self.shards)])

    def place(self):
        return jnp.stack([self.z, self.c, self.t]).astype(jnp.int32)

    def gather_rows(self, block):
        return lax.all_gather(block, ("shard", "ctx"), axis=0)

    def gather_spread(self, block):
        rows, _ = block.shape
        part = rows // self.tps
        quarter = lax.dynamic_slice_in_dim(block, self.t * part, part, 0)
        pieces = [block]
        pieces += [self.ring(quarter, which) for which in (1, 2, 3)]
        far = jnp.concatenate(pieces[1:], 0)
        sides = [self.side(far, which) for which in (1, 2, 3)]
        mine = [block, far] + sides
        theirs = [self.across(piece) for piece in mine]
        return far, sides, mine, theirs

    def gather_line(self, block, after, later):
        block, after = lax.optimization_barrier((block, after))
        two = self.ring(block, 2)
        one = self.ring(block, 1)
        late, relayed, later = lax.optimization_barrier((block, two, later))
        middle = lax.ppermute(late, "shard", [(1, 2), (2, 1)])
        ends = lax.ppermute(relayed, "shard", [(2, 3), (1, 0)])
        three = jnp.where((self.z == 1) | (self.z == 2), middle, ends)
        return [block, one, two, three]

    def reduce_rows(self, send, keep):
        mine, *quarters = fold(self.place(), keep, self.across(send))
        for which, quarter in enumerate(quarters, 1):
            mine = mine + self.side(quarter, which).astype(F32)
        total = lax.dynamic_index_in_dim(mine, self.z, 0, False)
        for which in (3, 2, 1):
            piece = lax.dynamic_index_in_dim(mine, self.z ^ which, 0, False).astype(BF)
            total = total + self.ring(piece, which).astype(F32)
        low = total.astype(BF)
        one, two, three = (self.side(low, which) for which in (1, 2, 3))
        odd = (self.t & 1) == 1
        a, b = jnp.where(odd, one, low), jnp.where(odd, low, one)
        c, d = jnp.where(odd, three, two), jnp.where(odd, two, three)
        far = self.t >= 2
        return jnp.concatenate(
            [
                jnp.where(far, c, a),
                jnp.where(far, d, b),
                jnp.where(far, a, c),
                jnp.where(far, b, d),
            ],
            0,
        ).astype(F32)

    def gather_tokens(self, rows):
        if not self.fast:
            every = lax.all_gather(rows, "tp", axis=0)
            return [
                lax.dynamic_index_in_dim(every, (self.t + i) % self.tps, 0, False)
                for i in range(self.tps)
            ]
        one = self.side(rows, 1)
        two = self.side(rows, 2)
        late, one, two = lax.optimization_barrier((rows, one, two))
        return [rows, one, two, self.side(late, 3)]

    def scatter_tokens(self, parts):
        if not self.fast:
            every = jnp.stack(parts)
            ordered = jnp.stack(
                [
                    lax.dynamic_index_in_dim(every, (i - self.t) % self.tps, 0, False)
                    for i in range(self.tps)
                ]
            )
            return lax.psum_scatter(ordered, "tp", scatter_dimension=0, tiled=False)
        return sum(piece.astype(F32) for piece in self.exchange_tokens(parts))

    def exchange_tokens(self, parts):
        return parts[:1] + [self.side(parts[which], which) for which in (1, 2, 3)]

    def scatter_line(self, send, keep):
        received = self.across(send)
        part = (keep.astype(F32) + received.astype(F32)).astype(BF)
        total = lax.dynamic_index_in_dim(part, self.z, 0, False).astype(F32)
        for which in (2, 3, 1):
            piece = lax.dynamic_index_in_dim(part, self.z ^ which, 0, False)
            total = total + self.ring(piece, which).astype(F32)
        return total


def root_inverse(x):
    return lax.rsqrt(jnp.mean(x * x, -1, keepdims=True) + EPSILON)


def project_body(place, *refs):
    mine, theirs = refs[0:5], refs[5:10]
    tokens, cosine, sine, weight, out_weight, query_t, own, gain_one, gain_two = refs[10:19]
    small, fused = refs[19:]
    width, fused_width = weight.shape
    rows = width // 8
    part = mine[0].shape[0] // 4
    z, c, t = place[0], place[1], place[2]
    for block in range(8):
        shard, core = block // 2, block % 2
        for side in range(4):
            first = side * part
            count = min(part, rows - first)

            def put(pieces, index, start):
                value = pieces[index][pl.ds(start, part), :]
                place_rows = slice(block * rows + first, block * rows + first + count)
                weight[place_rows, :] = value[:count, :fused_width]
                out_weight[place_rows, :] = value[:count, fused_width:]
                if count < part:
                    small[block, :, :] = value[count:, 0:128]

            start = pl.multiple_of(jnp.maximum((shard ^ z) - 1, 0) * part, 16)
            for pieces, owned in ((mine, core == c), (theirs, core != c)):

                @pl.when(owned & (shard == z))
                def _():
                    put(pieces, 0, first)

                for which in range(4):

                    @pl.when(owned & (shard != z) & ((side ^ t) == which))
                    def _():
                        put(pieces, 1 + which, start)

    long = jnp.zeros((16, 1024), F32)
    short = jnp.zeros((16, 128), F32)
    for block in range(8):
        piece = small[block].astype(F32)
        wide = jnp.concatenate([piece, jnp.zeros((16, 896), F32)], 1)
        long = long + (pltpu.roll(wide, rows * block, 1) if block else wide)
        short = short + (pltpu.roll(piece, 16 * block, 1) if block else piece)
    bias = jnp.concatenate([long[0:1, :width], short[1:2], short[2:3]], 1)
    gain = long[3:4, :width]
    gain_one[...] = gain
    gain_two[...] = long[4:5, :width]
    x = tokens[...].astype(F32)
    normed = (x * root_inverse(x) * gain).astype(BF)
    fused[...] = (jnp.dot(normed, weight[...], preferred_element_type=F32) + bias).T
    half_dim = HEAD_WIDTH // 2
    query_width = QUERY_HEADS * HEAD_WIDTH
    kv = KEY_VALUE_HEADS * HEAD_WIDTH
    for head in range(QUERY_HEADS + KEY_VALUE_HEADS):
        start = head * HEAD_WIDTH
        one = fused[start : start + half_dim, :]
        two = fused[start + half_dim : start + HEAD_WIDTH, :]
        low = (one * cosine[...] - two * sine[...]).astype(BF)
        high = (two * cosine[...] + one * sine[...]).astype(BF)
        if head < QUERY_HEADS:
            scale = HEAD_WIDTH ** (-0.5)
            query_t[start : start + half_dim, :] = low * BF(scale)
            query_t[start + half_dim : start + HEAD_WIDTH, :] = high * BF(scale)
        else:
            start -= query_width
            own[start : start + half_dim, :] = low
            own[start + half_dim : start + HEAD_WIDTH, :] = high
    own[kv:, :] = fused[query_width + kv :, :].astype(BF)


def project(place, mine, theirs, tokens, cosine, sine, fused_width):
    token_count, width = tokens.shape
    vmem = pl.BlockSpec(memory_space=pltpu.VMEM)
    kv = KEY_VALUE_HEADS * HEAD_WIDTH
    row = jax.ShapeDtypeStruct((1, width), F32)
    return pl.pallas_call(
        project_body,
        out_shape=(
            jax.ShapeDtypeStruct((width, fused_width), BF),
            jax.ShapeDtypeStruct((width, width), BF),
            jax.ShapeDtypeStruct((QUERY_HEADS * HEAD_WIDTH, token_count), BF),
            jax.ShapeDtypeStruct((2 * kv, token_count), BF),
            row,
            row,
        ),
        in_specs=[pl.BlockSpec(memory_space=pltpu.SMEM)] + [vmem] * 13,
        out_specs=(vmem,) * 6,
        scratch_shapes=[
            pltpu.VMEM((8, 16, 128), BF),
            pltpu.VMEM((fused_width, token_count), F32),
        ],
        cost_estimate=pl.CostEstimate(
            flops=int(3e9), bytes_accessed=int(12e6), transcendentals=0
        ),
        name="project",
    )(place, *mine, *theirs, tokens, cosine, sine)


def output_body(tokens, mixed_t, weight, gain, hidden, normed):
    value = tokens[...].astype(F32) + jnp.dot(
        mixed_t[...].T, weight[...], preferred_element_type=F32
    )
    hidden[...] = value
    normed[...] = (value * root_inverse(value) * gain[...]).astype(BF)


def output_projection(tokens, mixed_t, weight, gain):
    vmem = pl.BlockSpec(memory_space=pltpu.VMEM)
    return pl.pallas_call(
        output_body,
        out_shape=(
            jax.ShapeDtypeStruct(tokens.shape, F32),
            jax.ShapeDtypeStruct(tokens.shape, BF),
        ),
        in_specs=[vmem] * 4,
        out_specs=(vmem, vmem),
        cost_estimate=pl.CostEstimate(
            flops=int(1e9), bytes_accessed=int(6e6), transcendentals=0
        ),
        name="output_projection",
    )(tokens, mixed_t, weight, gain)


def middle_body(
    own, one, two, three, hidden, cotangent, weight, gain, grad_hidden, grad_mixed_t, grad_gain
):
    total = own[...].astype(F32) + one[...].astype(F32)
    total = total + two[...].astype(F32) + three[...].astype(F32)
    h = hidden[...]
    inv = root_inverse(h)
    scaled = total * gain[...]
    mean = jnp.mean(scaled * h, -1, keepdims=True)
    value = cotangent[...].astype(F32) + inv * scaled - h * (inv * inv * inv) * mean
    grad_hidden[...] = value
    grad_gain[...] = jnp.sum(total * h * inv, 0, keepdims=True)
    grad_mixed_t[...] = dot(weight[...], value.astype(BF), 1, 1).astype(BF)


def middle(parts, hidden, cotangent, weight, gain):
    vmem = pl.BlockSpec(memory_space=pltpu.VMEM)
    return pl.pallas_call(
        middle_body,
        out_shape=(
            jax.ShapeDtypeStruct(hidden.shape, F32),
            jax.ShapeDtypeStruct(hidden.shape[::-1], BF),
            jax.ShapeDtypeStruct(gain.shape, F32),
        ),
        in_specs=[vmem] * 8,
        out_specs=(vmem, vmem, vmem),
        cost_estimate=pl.CostEstimate(
            flops=int(1e9), bytes_accessed=int(9e6), transcendentals=0
        ),
        name="middle",
    )(*parts, hidden, cotangent, weight, gain)


def fold_body(place, keep, received, mine, *sends):
    part = mine.shape[1]
    for which, out in enumerate((mine,) + sends):
        rows = pl.ds(pl.multiple_of((place[2] ^ which) * part, 16), part)
        value = keep[0, rows, :].astype(F32) + received[0, rows, :].astype(F32)
        out[0] = value.astype(out.dtype)


def fold(place, keep, received):
    blocks, rows, cols = keep.shape
    part = rows // 4
    shape = (blocks, part, cols)
    return pl.pallas_call(
        fold_body,
        grid=(blocks,),
        out_shape=(jax.ShapeDtypeStruct(shape, F32),) + (jax.ShapeDtypeStruct(shape, BF),) * 3,
        in_specs=[pl.BlockSpec(memory_space=pltpu.SMEM)]
        + [pl.BlockSpec((1, rows, cols), lambda i: (i, 0, 0))] * 2,
        out_specs=(pl.BlockSpec((1, part, cols), lambda i: (i, 0, 0)),) * 4,
        cost_estimate=pl.CostEstimate(
            flops=0, bytes_accessed=6 * blocks * rows * cols, transcendentals=0
        ),
        name="fold",
    )(place, keep, received)


def assemble_line_body(place, *refs):
    mine, theirs, out = refs[0:4], refs[4:8], refs[8]
    rows = mine[0].shape[0]
    z, c = place[0], place[1]
    for here in range(4):

        @pl.when(z == here)
        def _():
            for block in range(8):
                shard, core = block // 2, block % 2
                left, right = mine[shard ^ here], theirs[shard ^ here]
                out[0, block * rows : (block + 1) * rows, :] = jnp.where(
                    core == c, left[...], right[...]
                )


def assemble_line(place, mine, theirs, count):
    rows, cols = mine[0].shape
    rows = rows // count
    part = pl.BlockSpec((rows, cols), lambda i: (i, 0))
    return pl.pallas_call(
        assemble_line_body,
        grid=(count,),
        out_shape=jax.ShapeDtypeStruct((count, 8 * rows, cols), BF),
        in_specs=[pl.BlockSpec(memory_space=pltpu.SMEM)] + [part] * 8,
        out_specs=pl.BlockSpec((1, 8 * rows, cols), lambda i: (i, 0, 0)),
        cost_estimate=pl.CostEstimate(
            flops=0, bytes_accessed=32 * rows * cols * count, transcendentals=0
        ),
        name="assemble_line",
    )(place, *mine, *theirs)


def projection_gradients_body(
    place,
    grad_query,
    own_sums,
    other_sums,
    cosine,
    sine,
    tokens,
    gain,
    second_gain,
    grad_hidden,
    mixed_t,
    weight,
    grad_tokens,
    send,
    keep,
    fused,
):
    half_dim = HEAD_WIDTH // 2
    query_width, kv = grad_query.shape[0], own_sums.shape[0] // 2
    rows = keep.shape[1] - 16

    def unrotate(value, start):
        first, second = value[:half_dim], value[half_dim:]
        fused[start : start + half_dim, :] = first * cosine[...] + second * sine[...]
        fused[start + half_dim : start + HEAD_WIDTH, :] = (
            second * cosine[...] - first * sine[...]
        )

    for head in range(QUERY_HEADS):
        start = head * HEAD_WIDTH
        unrotate(grad_query[start : start + HEAD_WIDTH, :].astype(F32), start)
    sums = (own_sums[...] + other_sums[...]).astype(BF).astype(F32)
    for head in range(KEY_VALUE_HEADS):
        start = head * HEAD_WIDTH
        unrotate(sums[start : start + HEAD_WIDTH], query_width + start)
    fused[query_width + kv :, :] = sums[kv:]

    exact = fused[...]
    low = exact.astype(BF)
    rest = (exact - low.astype(F32)).astype(BF)
    ones = jnp.ones((16, exact.shape[1]), BF)
    bias = dot(ones, low, 1, 1) + dot(ones, rest, 1, 1)
    low_rows = low.T
    x = tokens[...].astype(F32)
    inv = root_inverse(x)
    normed_t = (x * inv * gain[...]).astype(BF).T
    grad_normed = dot(low_rows, weight[...], 1, 1)
    scaled = grad_normed * gain[...]
    mean = jnp.mean(scaled * x, -1, keepdims=True)
    hidden = grad_hidden[...]
    grad_tokens[...] = (hidden + inv * scaled - x * (inv * inv * inv) * mean).astype(BF)
    grad_gain = jnp.sum(grad_normed * x * inv, 0, keepdims=True)
    left = jnp.dot(normed_t, low_rows, preferred_element_type=F32).astype(BF)
    right = jnp.dot(
        mixed_t[...], hidden.astype(BF), preferred_element_type=F32
    ).astype(BF)
    split = left.shape[1]
    first_row = jnp.concatenate(
        [bias[:8], jnp.broadcast_to(grad_gain, (8, grad_gain.shape[1]))], 1
    )
    second_row = jnp.concatenate(
        [
            jnp.broadcast_to(second_gain[...], (8, second_gain.shape[1])),
            jnp.zeros((8, split), F32),
        ],
        1,
    )
    index = lax.broadcasted_iota(jnp.int32, first_row.shape, 0)
    small = jnp.where(index == 0, first_row, jnp.where(index == 1, second_row, 0.0))
    small = jnp.concatenate([small, jnp.zeros_like(small)], 0).astype(BF)
    for block in range(8):
        shard, core = block // 2, block % 2
        part = slice(block * rows, (block + 1) * rows)
        for out, owned in ((keep, place[1] == core), (send, place[1] != core)):

            @pl.when(owned)
            def _():
                out[shard, 0:rows, 0:split] = left[part]
                out[shard, 0:rows, split:] = right[part]
                out[shard, rows:, :] = small


def projection_gradients(place, *arrays):
    tokens, weight = arrays[5], arrays[10]
    token_count, width = tokens.shape
    fused_width = weight.shape[1]
    half = jax.ShapeDtypeStruct((4, width // 8 + 16, fused_width + width), BF)
    whole = [
        pl.BlockSpec(array.shape, lambda i, n=array.ndim: (0,) * n) for array in arrays
    ]
    return pl.pallas_call(
        projection_gradients_body,
        grid=(1,),
        out_shape=(jax.ShapeDtypeStruct(tokens.shape, BF), half, half),
        in_specs=[pl.BlockSpec(memory_space=pltpu.SMEM)]
        + whole,
        out_specs=(
            pl.BlockSpec(tokens.shape, lambda i: (0, 0)),
            pl.BlockSpec(half.shape, lambda i: (0, 0, 0)),
            pl.BlockSpec(half.shape, lambda i: (0, 0, 0)),
        ),
        scratch_shapes=[pltpu.VMEM((fused_width, token_count), F32)],
        cost_estimate=pl.CostEstimate(
            flops=int(6e9), bytes_accessed=int(16e6), transcendentals=0
        ),
        name="projection_gradients",
    )(place, *arrays)


def mlp_body(chunks, *refs):
    xs, gs = refs[:chunks], refs[chunks : 2 * chunks]
    gate_ref, up_ref, down_ref = refs[2 * chunks : 2 * chunks + 3]
    backs, downs = refs[-2 - 2 * chunks : -2 - chunks], refs[-2 - chunks : -2]
    units, rows_t = refs[-2:]
    x, g = xs[0][...], gs[0][...]
    first = True
    if chunks == 2:
        first = pl.program_id(0) < pl.num_programs(0) // 2
        x, g = jnp.where(first, x, xs[1][...]), jnp.where(first, g, gs[1][...])
    gate = jnp.dot(x, gate_ref[...], preferred_element_type=F32)
    up = jnp.dot(x, up_ref[...], preferred_element_type=F32)
    sig = 1.0 / (1.0 + jnp.exp(-gate))
    silu = gate * sig
    act = (silu * up).astype(BF)
    grad_act = jnp.dot(g, down_ref[...], preferred_element_type=F32)
    grad_gate = (grad_act * up * sig * (1.0 + gate * (1.0 - sig))).astype(BF)
    grad_up = (grad_act * silu).astype(BF)
    back = (dot(grad_gate, gate_ref[...], 1, 1) + dot(grad_up, up_ref[...], 1, 1)).astype(BF)
    down = dot(act, down_ref[...], 1, 1).astype(BF)
    if chunks == 1:
        backs[0][...] = back
        downs[0][...] = down
    else:
        for index, chosen in enumerate((first, jnp.logical_not(first))):

            @pl.when(chosen)
            def _():
                backs[index][...] = back
                downs[index][...] = down

    units[0] = grad_gate
    units[1] = grad_up
    units[2] = act
    rows_t[0] = x.T
    rows_t[1] = g.T


def mlp(xs, gs, weights, kept, first, total):
    chunks = len(xs)
    count, width = xs[0].shape
    units = weights.shape[2]
    step = min(256, count)
    steps = count // step
    offset = first // step
    rows = [
        pl.BlockSpec((step, width), lambda i, n=n: (jnp.clip(i - n * steps, 0, steps - 1), 0))
        for n in range(chunks)
    ]
    whole = [
        pl.BlockSpec(
            (pl.Squeezed(), width, units), lambda i, n=n: (n, 0, 0), pipeline_mode=pl.Buffered(1)
        )
        for n in range(3)
    ]
    partial = jax.ShapeDtypeStruct((count, width), BF)
    kept = list(kept)
    outs = pl.pallas_call(
        functools.partial(mlp_body, chunks),
        grid=(chunks * steps,),
        out_shape=[partial] * (2 * chunks)
        + [
            jax.ShapeDtypeStruct((3, total, units), BF),
            jax.ShapeDtypeStruct((2, width, total), BF),
        ],
        in_specs=rows + rows + whole + [pl.BlockSpec(memory_space=pl.ANY)] * len(kept),
        out_specs=rows
        + rows
        + [
            pl.BlockSpec((3, step, units), lambda i: (0, i + offset, 0)),
            pl.BlockSpec((2, width, step), lambda i: (0, 0, i + offset)),
        ],
        input_output_aliases={2 * chunks + 3 + i: 2 * chunks + i for i in range(len(kept))},
        cost_estimate=pl.CostEstimate(
            flops=12 * chunks * count * width * units,
            bytes_accessed=6 * width * units + 8 * chunks * count * (width + units),
            transcendentals=chunks * count * units,
        ),
        name="mlp",
    )(*xs, *gs, weights, weights, weights, *kept)
    return list(outs[:chunks]), list(outs[chunks : 2 * chunks]), outs[2 * chunks :]


def weight_gradients_body(place, left, right, send, keep, total):
    index, last = pl.program_id(1), pl.num_programs(1) - 1
    rows = send.shape[2]
    value = jnp.dot(left[0], right[0], preferred_element_type=F32)

    @pl.when(index == 0)
    def _():
        total[...] = value

    @pl.when(index > 0)
    def _():
        total[...] += value

    @pl.when(index == last)
    def _():
        for block in range(8):
            shard, core = block // 2, block % 2
            piece = total[block * rows : (block + 1) * rows, :].astype(BF)

            @pl.when(place[1] == core)
            def _():
                keep[shard, 0] = piece

            @pl.when(place[1] != core)
            def _():
                send[shard, 0] = piece


def weight_gradients(place, units, rows_t):
    _, total, wide = units.shape
    width = rows_t.shape[1]
    step = total // 2
    half = jax.ShapeDtypeStruct((4, 3, width // 8, wide), BF)
    out = pl.BlockSpec((4, 1, width // 8, wide), lambda w, k: (0, w, 0, 0))
    return pl.pallas_call(
        weight_gradients_body,
        grid=(3, 2),
        out_shape=(half, half),
        in_specs=[
            pl.BlockSpec(memory_space=pltpu.SMEM),
            pl.BlockSpec((1, width, step), lambda w, k: (w // 2, 0, k)),
            pl.BlockSpec((1, step, wide), lambda w, k: (w, k, 0)),
        ],
        out_specs=(out, out),
        scratch_shapes=[pltpu.VMEM((width, wide), F32)],
        cost_estimate=pl.CostEstimate(
            flops=6 * total * width * wide,
            bytes_accessed=6 * total * (width + wide),
            transcendentals=0,
        ),
        name="weight_gradients",
    )(place, rows_t, units)


def per_device(
    tokens,
    doc_ids,
    w_query,
    b_query,
    key_projection,
    key_bias_vector,
    value_projection,
    value_bias_vector,
    w_output,
    gain_attn,
    gain_mlp,
    w_gate,
    w_up,
    w_down,
    cotangent,
):
    mesh = Mesh()
    token_count, width = tokens.shape
    rows = w_query.shape[0]
    padded = (rows + 5 + 15) // 16 * 16
    query_width = QUERY_HEADS * HEAD_WIDTH
    kv_width = KEY_VALUE_HEADS * HEAD_WIDTH
    kv_rows = key_bias_vector.shape[0]
    fused_width = query_width + 2 * kv_width
    blocks = mesh.shards * mesh.ctxs

    all_width = fused_width + width
    small_vectors = [b_query, key_bias_vector, value_bias_vector, gain_attn, gain_mlp]
    small_counts = [vector.shape[0] for vector in small_vectors]
    packed = jnp.concatenate(
        [jnp.concatenate([w_query, key_projection, value_projection, w_output], 1)]
        + [
            jnp.pad(vector[None], ((0, 0), (0, all_width - vector.shape[0])))
            for vector in small_vectors
        ]
        + [jnp.zeros((padded - rows - len(small_vectors), all_width), BF)],
        0,
    )
    if mesh.fast:
        far, sides, mine, theirs = mesh.gather_spread(packed)
        cosine, sine = rope_tables(mesh.c, token_count)
        fused_weight, output_weight, query_t, own, first_gain, second_gain = project(
            mesh.place(), mine, theirs, tokens, cosine, sine, fused_width
        )
        line = mesh.gather_line(jnp.concatenate([w_gate, w_up, w_down.T], 0), far, own)
        others = [mesh.across(part) for part in line]
        late, sides = lax.optimization_barrier((cotangent, sides))
        grad_parts = mesh.gather_tokens(late)
    else:
        gathered = lax.all_gather(packed, ("shard", "ctx"), axis=0)
        projection = gathered[:, :rows].reshape(width, all_width)
        smalls = gathered[:, rows:]
        weights = jnp.stack(
            [
                lax.all_gather(part, ("shard", "ctx"), axis=0, tiled=True)
                for part in (w_gate, w_up, w_down.T)
            ]
        )
        grad_parts = mesh.gather_tokens(cotangent)
        fused_weight = projection[:, :fused_width]
        output_weight = projection[:, fused_width:]
        bias_q, bias_k, bias_v, first_gain, second_gain = (
            smalls[:, i, :count].reshape(-1).astype(F32) for i, count in enumerate(small_counts)
        )
        fused_bias = jnp.concatenate([bias_q, bias_k, bias_v])
        tok_float = tokens.astype(F32)
        first_inv = root_inverse(tok_float)
        normed_attn = (tok_float * first_inv * first_gain).astype(BF)
        cosine, sine = rope_tables(mesh.c, token_count)
        fused_t = dot(fused_weight, normed_attn, 0, 1) + fused_bias[:, None]
        query_t = rotate(fused_t[:query_width], cosine, sine).astype(BF) * (HEAD_WIDTH ** (-0.5))
        key_t = rotate(fused_t[query_width : query_width + kv_width], cosine, sine).astype(BF)
        value_t = fused_t[query_width + kv_width :].astype(BF)
        own = jnp.concatenate([key_t, value_t], 0)
        first_gain, second_gain = first_gain[None], second_gain[None]
    other = mesh.across(own)
    half = mesh.c.astype(jnp.int32).reshape(1)
    mixed_t, exact_t, lse = attention_forward(half, doc_ids, query_t, own, other)

    hidden, normed_mlp = output_projection(tokens, mixed_t, output_weight, second_gain)
    normed_parts = mesh.gather_tokens(normed_mlp)
    if mesh.fast:
        line, others, _ = lax.optimization_barrier((line, others, normed_mlp))
        weights = assemble_line(mesh.place(), line, others, 3)

    total = token_count * mesh.tps
    backs, downs, kept = [], [], []
    groups = ((0, 1), (1, 3), (3, 4)) if mesh.tps == 4 else ((i, i + 1) for i in range(mesh.tps))
    for index, (low, high) in enumerate(groups):
        some_backs, some_downs, kept = mlp(
            normed_parts[low:high],
            grad_parts[low:high],
            weights,
            kept,
            low * token_count,
            total,
        )
        backs += some_backs
        downs += some_downs
    units, rows_t = kept
    if mesh.fast:
        back_parts = mesh.exchange_tokens(backs)
    else:
        zero = jnp.zeros_like(tokens)
        back_parts = [mesh.scatter_tokens(backs).astype(BF), zero, zero, zero]
    if mesh.fast:
        send, keep = weight_gradients(mesh.place(), units, rows_t)
        part_gate, part_up, part_down = mesh.scatter_line(send, keep)
        downs, back_parts = lax.optimization_barrier((downs, back_parts))
    else:
        part_gate, part_up, part_down = (
            lax.psum_scatter(
                dot(rows_t[i // 2], units[i], 1, 0),
                ("shard", "ctx"),
                scatter_dimension=0,
                tiled=True,
            )
            for i in range(3)
        )
    part_down = part_down.T
    grad_hidden, grad_mixed_t, grad_second_gain = middle(
        back_parts, hidden, cotangent, output_weight, second_gain
    )
    grad_query_rot, own_sums, to_other = attention_backward(
        half, doc_ids, query_t, own, other, grad_mixed_t, exact_t, lse
    )
    hidden_late, grad_query_rot = lax.optimization_barrier((hidden, grad_query_rot))
    result = (hidden_late + mesh.scatter_tokens(downs).astype(F32)).astype(BF)
    received = mesh.across(to_other)
    if mesh.fast:
        grad_tokens, send, keep = projection_gradients(
            mesh.place(),
            grad_query_rot,
            own_sums,
            received,
            cosine,
            sine,
            tokens,
            first_gain,
            grad_second_gain,
            grad_hidden,
            mixed_t,
            fused_weight,
        )
        summed = mesh.reduce_rows(send, keep)
        index = mesh.z * mesh.ctxs + mesh.c

        def own_part(line, start, count):
            return lax.dynamic_slice_in_dim(line, start + index * count, count, 0)

        first, second = summed[rows], summed[rows + 1]
        sum_small = [
            own_part(first, 0, rows),
            own_part(first, query_width, kv_rows),
            own_part(first, query_width + kv_width, kv_rows),
            own_part(first, fused_width, rows),
            own_part(second, 0, rows),
        ]
        return (
            result,
            grad_tokens,
            summed[:rows, :query_width],
            sum_small[0],
            summed[:rows, query_width : query_width + kv_width],
            sum_small[1],
            summed[:rows, query_width + kv_width : fused_width],
            sum_small[2],
            summed[:rows, fused_width:],
            sum_small[3],
            sum_small[4],
            part_gate,
            part_up,
            part_down,
        )
    grad_output_weight = dot(mixed_t, grad_hidden.astype(BF), 1, 0)
    own_sums_t = (own_sums + received).astype(BF).astype(F32)
    grad_query_pre = rotate(grad_query_rot.astype(F32), cosine, -sine)
    grad_key_pre = rotate(own_sums_t[:kv_width], cosine, -sine)
    fused_grad_t = jnp.concatenate([grad_query_pre, grad_key_pre, own_sums_t[kv_width:]], 0)
    grad_fused_bias = jnp.sum(fused_grad_t, 1)
    fused_low = fused_grad_t.astype(BF)
    grad_normed_attn = dot(fused_low, fused_weight, 0, 1)
    grad_fused_weight = dot(normed_attn, fused_low, 0, 1)
    scaled_one = grad_normed_attn * first_gain
    grad_tokens = (
        grad_hidden
        + first_inv * scaled_one
        - tok_float * first_inv**3 * jnp.mean(scaled_one * tok_float, -1, keepdims=True)
    )
    grad_first_gain = jnp.sum(grad_normed_attn * tok_float * first_inv, 0)

    small_sums = [
        grad_fused_bias[:query_width],
        grad_fused_bias[query_width : query_width + kv_width],
        grad_fused_bias[query_width + kv_width :],
        grad_first_gain,
        grad_second_gain[0],
    ]
    grad_packed = jnp.concatenate(
        [
            jnp.concatenate([grad_fused_weight, grad_output_weight], 1).reshape(
                blocks, rows, all_width
            )
        ]
        + [
            jnp.pad(
                vector.reshape(blocks, 1, count), ((0, 0), (0, 0), (0, all_width - count))
            )
            for vector, count in zip(small_sums, small_counts)
        ]
        + [jnp.zeros((blocks, padded - rows - len(small_sums), all_width), F32)],
        1,
    )
    summed = lax.psum_scatter(grad_packed, ("shard", "ctx"), scatter_dimension=0, tiled=True)
    summed = lax.psum(summed[0], "tp")
    sum_small = [summed[rows + i, :count] for i, count in enumerate(small_counts)]
    return (
        result,
        grad_tokens.astype(BF),
        summed[:rows, :query_width],
        sum_small[0],
        summed[:rows, query_width : query_width + kv_width],
        sum_small[1],
        summed[:rows, query_width + kv_width : fused_width],
        sum_small[2],
        summed[:rows, fused_width:],
        sum_small[3],
        sum_small[4],
        part_gate,
        part_up,
        part_down,
    )


def solution(mesh):
    both = ("shard", "ctx")
    every = ("shard", "ctx", "tp")
    in_specs = (
        P(every, None),
        P(("shard", "tp"), None),
        P(both, None),
        P(both),
        P(both, None),
        P(both),
        P(both, None),
        P(both),
        P(both, None),
        P(both),
        P(both),
        P(both, "tp"),
        P(both, "tp"),
        P("tp", both),
        P(every, None),
    )
    out_specs = (
        P(every, None),
        P(every, None),
        P(both, None),
        P(both),
        P(both, None),
        P(both),
        P(both, None),
        P(both),
        P(both, None),
        P(both),
        P(both),
        P(both, "tp"),
        P(both, "tp"),
        P("tp", both),
    )

    step = jax.shard_map(
        per_device, mesh=mesh, in_specs=in_specs, out_specs=out_specs, check_vma=False
    )
    if tuple(mesh.shape[name] for name in every) != (4, 2, 4):
        return step
    return step
```
